32 devices in a mesh: dp: 4 (over y, core), ctx: 2 (over x), exp: 4 (over z).
Axes of the slice: x: 2, y: 2, z: 4, core: 2. Of those that a mesh axis runs over, the one named last changes fastest.
Arguments:
- tokens: bfloat16 [16, 256, 2048], P(('dp', 'exp'), 'ctx'), may hold values from -6 to 6
- teacher: float32 [16, 256, 2048], P(('dp', 'exp'), 'ctx'), may hold values from -6 to 6
- lengths: int32 [16], replicated, may hold values from 64 to 256, as said below
- routes: int32 [16, 256, 4], P(('dp', 'exp'), 'ctx'), may hold values from 0 to 7, all different within a row; in each aligned block of 128 rows (0 to 127, 128 to 255, ..., all dimensions but the last counted through in order) at most 89 rows name the same one
- attn_gain: bfloat16 [2048], P(('dp', 'ctx', 'exp')), may hold values from 0.5 to 1.5
- ffn_gain: bfloat16 [2048], P(('dp', 'ctx', 'exp')), may hold values from 0.5 to 1.5
- router_weight: bfloat16 [2048, 8], P(('dp', 'ctx', 'exp')), may hold values from -0.0625 to 0.0625
- shared_gate: bfloat16 [2048], P(('dp', 'ctx', 'exp')), may hold values from -0.125 to 0.125
- qkv_weight: bfloat16 [2048, 3, 2048], P(('dp', 'ctx'), None, 'exp'), may hold values from -0.125 to 0.125
- qkv_bias: bfloat16 [3, 2048], P(None, 'exp'), may hold values from -1.1953125 to 1.1953125
- out_weight: bfloat16 [2048, 2048], P(('dp', 'ctx'), 'exp'), may hold values from -1 to 1
- shared_up: bfloat16 [2048, 2, 5632], P(('dp', 'ctx'), None, 'exp'), may hold values from -0.125 to 0.125
- shared_down: bfloat16 [2048, 5632], P(('dp', 'ctx'), 'exp'), may hold values from -0.21875 to 0.21875
- expert_up: bfloat16 [2048, 8, 2816], P(('dp', 'ctx'), 'exp'), may hold values from -0.125 to 0.125
- expert_down: bfloat16 [2048, 8, 1408], P(('dp', 'ctx'), 'exp'), may hold values from -0.875 to 0.875
Outputs:
- layer_out: bfloat16 [16, 256, 2048], P(('dp', 'exp'), 'ctx')
- grad_tokens: float32 [16, 256, 2048], P(('dp', 'exp'), 'ctx')
- grad_attn_gain: float32 [2048], P(('dp', 'ctx', 'exp'))
- grad_ffn_gain: float32 [2048], P(('dp', 'ctx', 'exp'))
- grad_router: float32 [2048, 8], P(('dp', 'ctx', 'exp'))
- grad_shared_gate: float32 [2048], P(('dp', 'ctx', 'exp'))
- grad_qkv: float32 [2048, 3, 2048], P(('dp', 'ctx'), None, 'exp')
- grad_qkv_bias: float32 [2, 2048], P(None, ('dp', 'ctx', 'exp'))
- grad_key_bias: float32 [2048], P(('dp', 'ctx', 'exp'))
- grad_out: float32 [2048, 2048], P(('dp', 'ctx'), 'exp')
- grad_shared_up: float32 [2048, 2, 5632], P(('dp', 'ctx'), None, 'exp')
- grad_shared_down: float32 [2048, 5632], P(('dp', 'ctx'), 'exp')
- grad_expert_up: float32 [2048, 8, 2816], P(('dp', 'ctx'), 'exp')
- grad_expert_down: float32 [2048, 8, 1408], P(('dp', 'ctx'), 'exp')
The draws below stay inside these ranges and needn't reach their ends.
Inputs may be any that keep to these rules, and one draw needn't show every extreme that they name: A sequence's valid positions are its first lengths[s]; one sequence is full and another has a quarter of 256. `routes`: the 4 experts of a token differ. In the rows of one device (aligned blocks of 128 positions of one sequence) no expert is named more than 89 times, a bound that some block reaches.
All inputs are finite; a program needn't handle non-finite values.
Results may differ from the reference program's by a relative error of at most 0.015.
Values may be sent and summed in bfloat16 or wider, within the bound.
No kernel may reach another device: no remote copies, remote signals or barrier semaphores. Data moves between devices by JAX's collectives and lax.ppermute only.
A program may use at most 320 MiB of HBM per device.

```python
import math
import jax
import jax.numpy as jnp
import numpy as np
from jax import lax

D = 2048
HEADS = 16
HD = 128
FE = 1408
FS = 5632
TOPK = 4
TOK_DEV = 128
EXPERTS = 8
SEQ_LEN = 256
SEQS = 16
TOKENS = 4096
CAP = 89


def draw_lengths(key, part):
    drawn = jax.random.randint(key, (SEQS,), SEQ_LEN // 4, SEQ_LEN + 1, dtype=jnp.int32)
    chosen = jax.random.randint(jax.random.fold_in(key, 7), (), 0, SEQS, dtype=jnp.int32)
    places = jnp.arange(SEQS, dtype=jnp.int32)
    drawn = jnp.where(places == chosen, SEQ_LEN, drawn)
    return jnp.where(places == (chosen + 1) % SEQS, SEQ_LEN // 4, drawn)


def block_levels(key, shape, pieces, low, largest):
    def one(dim, blocks):
        draws = jax.random.uniform(jax.random.fold_in(jax.random.fold_in(key, 6), dim), (blocks,), jnp.float32, low / len(pieces), largest / len(pieces))
        return jnp.repeat(jnp.exp(draws), shape[dim] // blocks).reshape((-1,) + (1,) * (len(shape) - dim - 1))

    loudness = one(*pieces[0])
    for cut in pieces[1:]:
        loudness = loudness * one(*cut)
    return loudness


def assign_block(rng, own, number, rows, count, top, bound, lean):
    order = jax.random.permutation(rng, count)
    packed, usual = shares(count, rows * top, bound, lean, True), shares(count, rows * top, bound, lean, False)
    places = jnp.arange(count)

    def named(sizes, offset_by):
        used = int((sizes > 0).sum())
        fixed = max(1, used // 4)
        shifted = fixed + (places - fixed + offset_by * (used - fixed)) % max(1, count - fixed)
        return jnp.zeros((count,), jnp.int32).at[order[jnp.where(places < fixed, places, shifted)]].set(jnp.asarray(sizes, jnp.int32))

    sizes = jnp.where(number % 4 == 0, named(packed, number // 4), named(usual, number - number // 4 - 1))
    mixed = jax.random.permutation(jax.random.fold_in(own, 3), count)
    source_of, taker = mixed[0:count // 2 * 2:2], mixed[1:count // 2 * 2:2]
    slack = jnp.minimum(sizes[source_of] - 1, bound - sizes[taker]) // 2
    slack = jnp.where((source_of == order[0]) | (taker == order[0]) | (sizes[taker] == 0), 0, jnp.maximum(slack, 0))
    shifted = jax.random.randint(jax.random.fold_in(own, 4), (count // 2,), 0, 1 << 20) % (slack + 1)
    sizes = sizes.at[source_of].add(-shifted).at[taker].add(shifted)
    labels = jnp.searchsorted(jnp.cumsum(sizes), jnp.arange(rows * top), side="right").astype(jnp.int32)
    grid = labels.reshape(top, rows).T
    grid = grid[jax.random.permutation(jax.random.fold_in(own, 1), rows)]
    offset_by = jax.random.randint(jax.random.fold_in(own, 2), (rows, 1), 0, top)
    return jnp.take_along_axis(grid, (jnp.arange(top)[None, :] + offset_by) % top, axis=1)


def shares(number_of, total, most, slope, full):
    portions = [(1 << 20) // math.isqrt(standing ** slope) + 1 for standing in range(1, number_of + 1)]
    largest = most if full else min(most, max(-(-total // number_of), total * portions[0] // sum(portions)))
    least = 1 if total - largest >= number_of - 1 else 0
    counts, spare = [largest] + [least] * (number_of - 1), total - largest - least * (number_of - 1)
    while spare > 0:
        candidates = [i for i in range(1, number_of) if counts[i] < largest] or [i for i in range(1, number_of) if counts[i] < most]
        mass, budget = sum([portions[i] for i in candidates]), spare
        for i in candidates:
            extra = min(most - counts[i], max(1, budget * portions[i] // mass), spare)
            counts[i] = counts[i] + extra
            spare = spare - extra
    return np.array(counts)


def centred(rng, shape, deviation, most, split=(), kind=jnp.bfloat16):
    array = deviation * jax.random.normal(rng, shape, jnp.float32)
    if split:
        array = array * block_levels(rng, shape, split, -0.22, 0.18)
    return jnp.clip(array, -most, most).astype(kind)


def setup_inputs(seed: int = 0) -> dict:
    seeds = jax.random.split(jax.random.key(seed), 16)
    tokens = centred(seeds[0], (SEQS, SEQ_LEN, D), 1.0, 6.0, ((0, 16), (1, 2)))
    teacher = centred(seeds[1], (SEQS, SEQ_LEN, D), 1.0, 6.0, ((0, 16), (1, 2)), jnp.float32)
    lengths = draw_lengths(jax.random.fold_in(seeds[15], 71), 0)
    routes_keys = jax.random.split(jax.random.fold_in(seeds[3], 1), SEQS * SEQ_LEN // TOK_DEV)
    routes_turns = jax.random.permutation(jax.random.fold_in(seeds[3], 3), SEQS * SEQ_LEN // TOK_DEV)
    routes = jax.vmap(lambda own, number: assign_block(jax.random.fold_in(seeds[3], 2), own, number, TOK_DEV, EXPERTS, TOPK, CAP, 1))(routes_keys, routes_turns).reshape((SEQS, SEQ_LEN, TOPK))
    attn_gain = jnp.clip(1.0 + 0.1 * jax.random.normal(seeds[4], (D,), jnp.float32), 0.5, 1.5).astype(jnp.bfloat16)
    ffn_gain = jnp.clip(1.0 + 0.1 * jax.random.normal(seeds[5], (D,), jnp.float32), 0.5, 1.5).astype(jnp.bfloat16)
    router_weight = centred(seeds[6], (D, EXPERTS), (4 * D) ** -0.5, 0.0625, ((0, 32),))
    shared_gate = centred(seeds[7], (D,), D ** -0.5, 0.125, ((0, 32),))
    qkv_weight = centred(seeds[8], (D, 3, HEADS * HD), D ** -0.5, 0.125, ((0, 8), (2, 4)))
    qkv_bias = centred(seeds[9], (3, HEADS * HD), 0.2, 1.1953125, ((1, 4),))
    out_weight = centred(seeds[10], (D, HEADS * HD), (HEADS * HD // 64) ** -0.5, 1.0, ((0, 8), (1, 4)))
    shared_up = centred(seeds[11], (D, 2, FS), D ** -0.5, 0.125, ((0, 8), (2, 4)))
    shared_down = centred(seeds[12], (D, FS), (FS // 8) ** -0.5, 0.21875, ((0, 8), (1, 4)))
    expert_up = centred(seeds[13], (D, EXPERTS, 2 * FE), D ** -0.5, 0.125, ((0, 8), (1, 4)))
    expert_down = centred(seeds[14], (D, EXPERTS, FE), (max(4, FE * TOPK // (EXPERTS * 16))) ** -0.5, 0.875, ((0, 8), (1, 4)))
    return {"tokens": tokens, "teacher": teacher, "lengths": lengths, "routes": routes, "attn_gain": attn_gain, "ffn_gain": ffn_gain, "router_weight": router_weight, "shared_gate": shared_gate, "qkv_weight": qkv_weight, "qkv_bias": qkv_bias, "out_weight": out_weight, "shared_up": shared_up, "shared_down": shared_down, "expert_up": expert_up, "expert_down": expert_down}


EPSILON = 1e-06
ROPE_BASE = 1000000.0
NEGATIVE = -1e+30
HIGHEST = lax.Precision.HIGHEST

@jax.custom_vjp
def low(v):
    return lax.optimization_barrier(v.astype(jnp.bfloat16)).astype(jnp.float32)

@jax.custom_vjp
def low_back(v):
    return v

def low_keep(v):
    return (low(v), None)

def low_pass(kept, grad):
    return (grad,)

def back_keep(v):
    return (v, None)

def back_low(kept, grad):
    return (low(grad),)
low.defvjp(low_keep, low_pass)
low_back.defvjp(back_keep, back_low)

def rope_tables(positions, head_width):
    frequency = ROPE_BASE ** (-jnp.arange(0, head_width, 2, dtype=jnp.float32) / head_width)
    angles = positions[:, None] * frequency[None, :]
    cosine_table = jnp.concatenate([jnp.cos(angles), jnp.cos(angles)], axis=1)
    sine_table = jnp.concatenate([jnp.sin(angles), jnp.sin(angles)], axis=1)
    return (cosine_table, sine_table)

def rotate(values, cosine_table, sine_table):
    halfway = values.shape[-1] // 2
    turned = jnp.concatenate([-values[..., halfway:], values[..., :halfway]], axis=-1)
    return values * cosine_table[:, None, :] + turned * sine_table[:, None, :]

def forward(params, inputs, target, length, chosen, factor):
    attn_gain, ffn_gain, router_weight, shared_gate, qkv_weight, qkv_bias, out_weight, shared_up, shared_down, expert_up, expert_down = params
    places = jnp.arange(SEQ_LEN, dtype=jnp.int32)
    attn_scale = lax.rsqrt(lax.optimization_barrier(jnp.mean(inputs * inputs, axis=1, keepdims=True)) + EPSILON)
    normed_attn = low(inputs * attn_scale * attn_gain)
    projected = low_back(jnp.einsum('ld,dbc->blc', normed_attn, qkv_weight, precision=HIGHEST) + qkv_bias[:, None, :])
    cosine_table, sine_table = rope_tables(places.astype(jnp.float32), HD)
    queries = low(rotate(projected[0].reshape(SEQ_LEN, HEADS, HD), cosine_table, sine_table))
    keys = low(rotate(projected[1].reshape(SEQ_LEN, HEADS, HD), cosine_table, sine_table))
    values = low(projected[2].reshape(SEQ_LEN, HEADS, HD))
    scores = low_back(jnp.einsum('ihd,jhd->hij', queries, keys, precision=HIGHEST) * HD ** (-0.5))
    allowed = (places[None, :] <= places[:, None]) & (places[None, :] < length)
    weights = jax.nn.softmax(jnp.where(allowed[None], scores, NEGATIVE), axis=-1)
    attention = jnp.einsum('hij,jhd->ihd', weights, values, precision=HIGHEST).reshape(SEQ_LEN, HEADS * HD)
    attn_low = low(low_back(attention))
    hidden = inputs + low_back(jnp.einsum('lc,dc->ld', attn_low, out_weight, precision=HIGHEST))
    ffn_scale = lax.rsqrt(lax.optimization_barrier(jnp.mean(hidden * hidden, axis=1, keepdims=True)) + EPSILON)
    normed_ffn = low(hidden * ffn_scale * ffn_gain)
    logits = jnp.einsum('ld,de->le', normed_ffn, router_weight, precision=HIGHEST)
    router_probs = jax.nn.softmax(logits, axis=-1)
    route_pick = (chosen[:, :, None] == jnp.arange(EXPERTS, dtype=jnp.int32)[None, None, :]).astype(jnp.float32)
    gate_values = jnp.einsum('le,lke->lk', router_probs, route_pick, precision=HIGHEST)
    mixing = jnp.einsum('lk,lke->le', gate_values, route_pick, precision=HIGHEST)
    shared_pre = low_back(jnp.einsum('ld,dbc->blc', normed_ffn, shared_up, precision=HIGHEST))
    shared_act = low(jax.nn.silu(shared_pre[0]) * shared_pre[1])
    shared_out = low_back(jnp.einsum('lc,dc->ld', shared_act, shared_down, precision=HIGHEST))
    shared_sig = jax.nn.sigmoid(jnp.einsum('ld,d->l', normed_ffn, shared_gate, precision=HIGHEST))
    expert_in = low_back(jnp.broadcast_to(normed_ffn[None], (EXPERTS, SEQ_LEN, D)))
    expert_pre = low_back(jnp.einsum('eld,dec->elc', expert_in, expert_up, precision=HIGHEST))
    expert_act = low(jax.nn.silu(expert_pre[..., :FE]) * expert_pre[..., FE:])
    expert_out = low(low_back(jnp.einsum('elc,dec->eld', expert_act, expert_down, precision=HIGHEST)))
    routed = jnp.einsum('le,eld->ld', mixing, expert_out, precision=HIGHEST)
    result = hidden + shared_sig[:, None] * shared_out + routed
    valid_rows = (places < length).astype(jnp.float32)
    loss_value = factor * 0.5 * jnp.sum(valid_rows[:, None] * (result - target) ** 2)
    return (result, loss_value)

def reference(tokens, teacher, lengths, routes, attn_gain, ffn_gain, router_weight, shared_gate, qkv_weight, qkv_bias, out_weight, shared_up, shared_down, expert_up, expert_down):
    params = tuple((member.astype(jnp.float32) for member in (attn_gain, ffn_gain, router_weight, shared_gate, qkv_weight, qkv_bias, out_weight, shared_up, shared_down, expert_up, expert_down)))
    count_valid = jnp.sum(lengths).astype(jnp.float32)
    factor = TOKENS / count_valid

    def one_sequence(totals, member):
        inputs, target, length, chosen = member

        def closure(weights, sequence):
            return forward(weights, sequence, target, length, chosen, factor)
        (result, loss_value), pullback = jax.vjp(closure, params, inputs.astype(jnp.float32))
        gradients, grad_inputs = pullback((jnp.zeros_like(result), jnp.ones_like(loss_value)))
        totals = jax.tree.map(jnp.add, totals, gradients)
        return (totals, (result.astype(jnp.bfloat16), grad_inputs))
    starting = tuple((jnp.zeros_like(member) for member in params))
    totals, (layer_out, grad_tokens) = lax.scan(one_sequence, starting, (tokens, teacher, lengths, routes))
    bias_grads = totals[5]
    grad_qkv_bias = jnp.stack([bias_grads[0], bias_grads[2]])
    grad_key_bias = bias_grads[1]
    return (layer_out, grad_tokens, totals[0], totals[1], totals[2], totals[3], totals[4], grad_qkv_bias, grad_key_bias, totals[6], totals[7], totals[8], totals[9], totals[10])
```

```python
import functools

import jax
import jax.numpy as jnp
from jax import lax
from jax.experimental import pallas as pl
from jax.experimental.pallas import tpu as pltpu
from jax.sharding import PartitionSpec as P

HD = 128
EPSILON = 1e-06
ROPE_BASE = 1000000.0
NEGATIVE = -1e30
HIGHEST = lax.Precision.HIGHEST
BF = jnp.bfloat16
F32 = jnp.float32


def core_swap(v):
    n = lax.axis_size("dp")
    return lax.ppermute(v, "dp", [(i, i ^ 1) for i in range(n)])


def y_swap(v):
    n = lax.axis_size("dp")
    return lax.ppermute(v, "dp", [(i, i ^ 2) for i in range(n)])


def shift(v, axis, s):
    n = lax.axis_size(axis)
    return lax.ppermute(v, axis, [(i, (i + s) % n) for i in range(n)])


def after(values, anchors):
    return lax.optimization_barrier((tuple(values), tuple(anchors)))[0]


def gather_shards(v):
    nz = lax.axis_size("exp")
    mine = [v] + [shift(v, "exp", s) for s in range(1, nz)]
    return mine + [core_swap(m) for m in mine]


def gather_rows(v):
    return jnp.concatenate(gather_shards(v), axis=0)


def home_sum(keep, away):
    nz = lax.axis_size("exp")
    rows = keep.shape[0] // nz
    both = (keep.astype(F32) + core_swap(away).astype(F32)).astype(keep.dtype)
    parts = [both[s * rows : (s + 1) * rows] for s in range(nz)]
    total = parts[0].astype(F32)
    for s in range(1, nz):
        total = total + shift(parts[s], "exp", -s).astype(F32)
    return total


def sum_everywhere(v):
    v = v + core_swap(v)
    v = v + y_swap(v)
    for axis in ("ctx", "exp"):
        v = functools.reduce(
            jnp.add, [v] + [shift(v, axis, s) for s in range(1, lax.axis_size(axis))]
        )
    return v


def gather_weight(mine, other, anchors):
    n = lax.axis_size("ctx")
    x, c, y = lax.axis_index("ctx"), lax.axis_index("dp") % 2, lax.axis_index("dp") // 2
    a, b = mine, core_swap(other)
    if anchors:
        a, b = after((a, b), anchors)
    ax = [a] + [shift(a, "ctx", s) for s in range(1, n)]
    by = y_swap(b)
    ay = [y_swap(v) for v in ax]
    bx = [b] + [shift(b, "ctx", s) for s in range(1, n)]
    bxy = [by] + [shift(by, "ctx", s) for s in range(1, n)]
    rows, cols = mine.shape
    out = jnp.zeros((2, 2, n, rows, cols), mine.dtype)
    zero = jnp.int32(0)

    def put(buffer, block, yy, cc, xx):
        return lax.dynamic_update_slice(buffer, block[None, None, None], (yy, cc, xx, zero, zero))

    for s in range(n):
        xs = lax.rem(x + n - s, n)
        out = put(out, ax[s], y, c, xs)
        out = put(out, bx[s], y, 1 - c, xs)
    for s in range(n):
        xs = lax.rem(x + n - s, n)
        out = put(out, ay[s], 1 - y, c, xs)
        out = put(out, bxy[s], 1 - y, 1 - c, xs)
    return out.reshape(4 * n * rows, cols), (ax[-1], by)


def scatter_grad(grad):
    n = lax.axis_size("ctx")
    x, c, y = lax.axis_index("ctx"), lax.axis_index("dp") % 2, lax.axis_index("dp") // 2
    rows = grad.shape[0] // (4 * n)
    blocks = grad.reshape(2, 2, n, rows, grad.shape[1])

    def block(yy, cc, xx):
        return lax.dynamic_slice(
            blocks, (yy, cc, xx, 0, 0), (1, 1, 1, rows, grad.shape[1])
        ).reshape(rows, grad.shape[1])

    def line(yy, cc):
        return lax.dynamic_slice(
            blocks, (yy, cc, 0, 0, 0), (1, 1, n, rows, grad.shape[1])
        ).reshape(n, rows, grad.shape[1])

    def add(*terms):
        return functools.reduce(jnp.add, [t.astype(F32) for t in terms])

    got = y_swap(line(1 - y, c))
    mine = None
    for s in range(n):
        xs = lax.rem(x + n - s, n)
        both = add(
            block(y, c, xs), lax.dynamic_index_in_dim(got, xs, 0, keepdims=False)
        )
        mine = both if s == 0 else mine + shift(both.astype(BF), "ctx", -s).astype(F32)
    away = stay = None
    for s in range(n):
        xs = lax.rem(x + n - s, n)
        far, near = block(1 - y, 1 - c, xs), block(y, 1 - c, xs)
        if s:
            far, near = shift(far, "ctx", -s), shift(near, "ctx", -s)
        away = far.astype(F32) if s == 0 else away + far.astype(F32)
        stay = near.astype(F32) if s == 0 else stay + near.astype(F32)
    theirs = stay + y_swap(away.astype(BF)).astype(F32)
    return mine, core_swap(theirs.astype(BF)).astype(F32)


def turn(v):
    lane = lax.broadcasted_iota(jnp.int32, v.shape, 1)
    rolled = pltpu.roll(v, HD // 2, 1)
    return jnp.where(lane < HD // 2, -rolled, rolled)


def qkv_kernel(rows_ref, weight_ref, bias_ref, cos_ref, sin_ref, q_ref, kv_ref):
    width = q_ref.shape[1]
    cos, sin = cos_ref[...], sin_ref[...]
    tokens = cos.shape[0]
    projected = (
        jnp.dot(rows_ref[...], weight_ref[...], preferred_element_type=F32) + bias_ref[...]
    )
    for t in range(projected.shape[0] // tokens):
        for h in range(2 * width // HD):
            piece = projected[t * tokens : (t + 1) * tokens, h * HD : (h + 1) * HD]
            out = (piece * cos + turn(piece) * sin).astype(BF)
            at = h * HD
            if at < width:
                q_ref[t * tokens : (t + 1) * tokens, at : at + HD] = out
            else:
                kv_ref[t * tokens : (t + 1) * tokens, at - width : at - width + HD] = out
    kv_ref[:, width:] = projected[:, 2 * width :].astype(BF)


def qkv_call(rows, weight, bias, cos, sin, width):
    total, depth = rows.shape
    tile = min(total, 4 * cos.shape[0])
    return pl.pallas_call(
        qkv_kernel,
        grid=(total // tile,),
        in_specs=[
            pl.BlockSpec((tile, depth), lambda i: (i, 0)),
            pl.BlockSpec((depth, 3 * width), lambda i: (0, 0)),
            pl.BlockSpec((1, 3 * width), lambda i: (0, 0)),
            pl.BlockSpec(cos.shape, lambda i: (0, 0)),
            pl.BlockSpec(sin.shape, lambda i: (0, 0)),
        ],
        out_specs=[
            pl.BlockSpec((tile, width), lambda i: (i, 0)),
            pl.BlockSpec((tile, 2 * width), lambda i: (i, 0)),
        ],
        out_shape=[
            jax.ShapeDtypeStruct((total, width), BF),
            jax.ShapeDtypeStruct((total, 2 * width), BF),
        ],
        cost_estimate=pl.CostEstimate(
            flops=2 * total * depth * 3 * width,
            transcendentals=0,
            bytes_accessed=2 * (total * depth + depth * 3 * width + total * 3 * width),
        ),
        name="qkv_rope",
    )(rows, weight, bias, cos, sin)


def probabilities(query, keys, length, x, scale):
    tokens, count = query.shape[0], keys.shape[0]
    scores = (
        lax.dot_general(query, keys, (((1,), (1,)), ((), ())), preferred_element_type=F32) * scale
    )
    row = lax.broadcasted_iota(jnp.int32, (tokens, count), 0) + x * tokens
    col = lax.broadcasted_iota(jnp.int32, (tokens, count), 1)
    place = jnp.zeros((tokens, count), jnp.int32)
    for s in range(count // tokens):
        inside = (col >= s * tokens) & (col < (s + 1) * tokens)
        place = jnp.where(inside, col - s * tokens + (x - s) * tokens, place)
    allowed = (place >= 0) & (place <= row) & (place < length)
    masked = jnp.where(allowed, scores, NEGATIVE)
    top = jnp.max(masked, axis=1, keepdims=True)
    weights = jnp.where(allowed, jnp.exp(masked - top), 0.0)
    return weights / jnp.sum(weights, axis=1, keepdims=True)


def attend_kernel(scale, info_ref, q_ref, *refs):
    kv_refs, out_ref = refs[:-1], refs[-1]
    group = pl.program_id(0)
    width = q_ref.shape[1]
    for h in range(width // HD):
        at = h * HD
        keys = jnp.concatenate([r[:, at : at + HD] for r in kv_refs], axis=0)
        values = jnp.concatenate([r[:, width + at : width + at + HD] for r in kv_refs], axis=0)
        prob = probabilities(
            q_ref[:, at : at + HD], keys, info_ref[group], info_ref[pl.num_programs(0)], scale
        )
        out_ref[:, at : at + HD] = jnp.dot(
            prob.astype(BF), values, preferred_element_type=F32
        ).astype(BF)


def attend_call(info, query, kvs, tokens, scale):
    total, width = query.shape
    groups = total // tokens
    return pl.pallas_call(
        functools.partial(attend_kernel, scale),
        grid_spec=pltpu.PrefetchScalarGridSpec(
            num_scalar_prefetch=1,
            grid=(groups,),
            in_specs=[pl.BlockSpec((tokens, width), lambda i, info: (i, 0))]
            + [pl.BlockSpec((tokens, 2 * width), lambda i, info: (i, 0)) for _ in kvs],
            out_specs=pl.BlockSpec((tokens, width), lambda i, info: (i, 0)),
        ),
        out_shape=jax.ShapeDtypeStruct((total, width), BF),
        cost_estimate=pl.CostEstimate(
            flops=4 * total * width * tokens * len(kvs),
            transcendentals=total * tokens * len(kvs) * width // HD,
            bytes_accessed=2 * total * width * (2 + 2 * len(kvs)),
        ),
        name="attend",
    )(info, query, *kvs)


def unrope(grad, cos, sin):
    return grad * cos - turn(grad * sin)


def attend_back_kernel(scale, count, info_ref, q_ref, da_ref, *refs):
    kv_refs = refs[:count]
    cos_ref, sin_ref = refs[count : count + 2]
    dq_ref = refs[count + 2]
    dkv_refs = refs[count + 3 :]
    group = pl.program_id(0)
    tokens, width = q_ref.shape
    for h in range(width // HD):
        at = h * HD
        keys = jnp.concatenate([r[:, at : at + HD] for r in kv_refs], axis=0)
        values = jnp.concatenate([r[:, width + at : width + at + HD] for r in kv_refs], axis=0)
        query, grad = q_ref[:, at : at + HD], da_ref[:, at : at + HD]
        prob = probabilities(
            query, keys, info_ref[group], info_ref[pl.num_programs(0)], scale
        )
        dprob = lax.dot_general(
            grad, values, (((1,), (1,)), ((), ())), preferred_element_type=F32
        )
        row_dot = jnp.sum(prob * dprob, axis=1, keepdims=True)
        dscore = (prob * (dprob - row_dot)).astype(BF)
        dq = jnp.dot(dscore, keys, preferred_element_type=F32) * scale
        dq_ref[:, at : at + HD] = unrope(dq, cos_ref[:tokens], sin_ref[:tokens]).astype(BF)
        dk = (
            lax.dot_general(dscore, query, (((0,), (0,)), ((), ())), preferred_element_type=F32)
            * scale
        )
        dv = lax.dot_general(
            prob.astype(BF), grad, (((0,), (0,)), ((), ())), preferred_element_type=F32
        )
        for s in range(count):
            part = slice(s * tokens, (s + 1) * tokens)
            dkv_refs[s][:, at : at + HD] = unrope(dk[part], cos_ref[part], sin_ref[part]).astype(
                dkv_refs[s].dtype
            )
            dkv_refs[s][:, width + at : width + at + HD] = dv[part].astype(dkv_refs[s].dtype)


def attend_back_call(info, query, grad, kvs, cos, sin, tokens, scale):
    total, width = query.shape
    groups, count = total // tokens, len(kvs)
    one = pl.BlockSpec((tokens, width), lambda i, info: (i, 0))
    two = pl.BlockSpec((tokens, 2 * width), lambda i, info: (i, 0))
    table = pl.BlockSpec(cos.shape, lambda i, info: (0, 0))
    return pl.pallas_call(
        functools.partial(attend_back_kernel, scale, count),
        grid_spec=pltpu.PrefetchScalarGridSpec(
            num_scalar_prefetch=1,
            grid=(groups,),
            in_specs=[one, one] + [two] * count + [table, table],
            out_specs=[one] + [two] * count,
        ),
        out_shape=[jax.ShapeDtypeStruct((total, width), BF)]
        + [jax.ShapeDtypeStruct((total, 2 * width), F32 if s == 0 else BF) for s in range(count)],
        cost_estimate=pl.CostEstimate(
            flops=10 * total * width * tokens * count,
            transcendentals=total * tokens * count * width // HD,
            bytes_accessed=2 * total * width * (3 + 5 * count),
        ),
        name="attend_back",
    )(info, query, grad, *kvs, cos, sin)


def rope_tables(positions):
    frequency = ROPE_BASE ** (-jnp.arange(0, HD, 2, dtype=F32) / HD)
    angles = positions[:, None] * frequency[None, :]
    return (
        jnp.concatenate([jnp.cos(angles), jnp.cos(angles)], axis=1),
        jnp.concatenate([jnp.sin(angles), jnp.sin(angles)], axis=1),
    )


def dot_t(a, b):
    return lax.dot_general(a, b, (((1,), (1,)), ((), ())), preferred_element_type=F32)


def dot_rows(a, b):
    return lax.dot_general(a, b, (((0,), (0,)), ((), ())), preferred_element_type=F32)


def norm_scale(values):
    return lax.rsqrt(jnp.mean(values * values, axis=1, keepdims=True) + EPSILON)


def norm_back(values, scale, gain, grads):
    weighted = grads * gain
    grad_values = scale * weighted - values * scale**3 * jnp.mean(
        weighted * values, axis=1, keepdims=True
    )
    return grad_values, jnp.sum(grads * values * scale, axis=0)


def body(
    tokens,
    teacher,
    lengths,
    routes,
    attn_gain,
    ffn_gain,
    router_weight,
    shared_gate,
    qkv_weight,
    qkv_bias,
    out_weight,
    shared_up,
    shared_down,
    expert_up,
    expert_down,
):
    tok_rows, model_width = tokens.shape[1:]
    nz, n = lax.axis_size("exp"), lax.axis_size("ctx")
    z, x, dp = lax.axis_index("exp"), lax.axis_index("ctx"), lax.axis_index("dp")
    c = dp % 2
    devices = lax.axis_size(("dp", "ctx", "exp"))
    me = lax.axis_index(("dp", "ctx", "exp"))
    seq_len = tok_rows * n
    experts = router_weight.shape[1]
    own_expert = 2 * z + c
    rows_w = qkv_weight.shape[0]
    width = qkv_weight.shape[2] // 2
    units, shared = expert_down.shape[2], shared_down.shape[1] // 2
    score_scale = HD ** (-0.5)
    first = c == 0

    def halves(v, axis):
        size = v.shape[axis] // 2
        low = lax.slice_in_dim(v, 0, size, axis=axis)
        high = lax.slice_in_dim(v, size, 2 * size, axis=axis)
        return jnp.where(first, low, high), jnp.where(first, high, low)

    token_shards = gather_shards(tokens[0])

    piece = jnp.concatenate(
        [
            router_weight.T,
            attn_gain[None],
            ffn_gain[None],
            shared_gate[None],
        ],
        axis=0,
    )
    span = model_width // devices
    lane = lax.broadcasted_iota(jnp.int32, (experts + 3, model_width), 1)
    vectors = sum_everywhere(
        jnp.where(lane // span == me, jnp.tile(piece, (1, devices)), jnp.zeros((), BF))
    )
    router_t = vectors[:experts]
    attn_factor = vectors[experts].astype(F32)[None]
    ffn_factor = vectors[experts + 1].astype(F32)[None]
    gate_full = vectors[experts + 2]

    chosen = (
        routes[0][:, None, :] == jnp.arange(experts, dtype=jnp.int32)[None, :, None]
    ).any(axis=2)
    chosen_t = chosen.astype(BF).T
    chosen_mine = jnp.concatenate(
        [chosen_t[None]] + [shift(chosen_t, "exp", s)[None] for s in range(1, nz)], axis=0
    )
    chosen_all = jnp.concatenate([chosen_mine, core_swap(chosen_mine)], axis=0)
    routed_own = (
        lax.dynamic_index_in_dim(chosen_all, own_expert, 1, keepdims=False)
        .astype(F32)
        .reshape(-1, 1)
    )

    qkv_halves = halves(qkv_weight, 2)
    out_halves = halves(out_weight, 1)
    shared_halves = halves(shared_up, 2)
    down_halves = halves(shared_down, 1)
    expert_halves = [v[:, 0] for v in halves(expert_up, 1)]
    expert_down_halves = [v[:, 0] for v in halves(expert_down, 1)]
    attn_pair = [
        jnp.concatenate([q[:, 0], q[:, 1], q[:, 2], o], axis=1)
        for q, o in zip(qkv_halves, out_halves)
    ]
    gate_pair = [
        jnp.concatenate([e[:, :units], s[:, 0]], axis=1)
        for e, s in zip(expert_halves, shared_halves)
    ]
    up_pair = [
        jnp.concatenate([e[:, units:], s[:, 1]], axis=1)
        for e, s in zip(expert_halves, shared_halves)
    ]
    down_pair = [
        jnp.concatenate([e, s], axis=1) for e, s in zip(expert_down_halves, down_halves)
    ]
    attn_weight, marks = gather_weight(*attn_pair, ())
    gate_weight, marks = gather_weight(*gate_pair, marks)
    up_weight, marks = gather_weight(*up_pair, marks)
    down_weight, marks = gather_weight(*down_pair, marks)
    out_full = attn_weight[:, 3 * width :]

    count_valid = jnp.sum(lengths).astype(F32)
    factor = lengths.shape[0] * seq_len / count_valid
    positions = x * tok_rows + jnp.arange(tok_rows, dtype=jnp.int32)
    own_length = lengths[dp * nz + z]
    valid_rows = (positions < own_length).astype(F32)[:, None]
    shard_dp = jnp.repeat(jnp.stack([dp, dp ^ 1]), nz)
    shard_z = jnp.tile(lax.rem(z + nz - jnp.arange(nz, dtype=jnp.int32), nz), 2)
    info = jnp.concatenate([lengths[shard_dp * nz + shard_z], x[None].astype(jnp.int32)])
    key_places = jnp.concatenate([positions - s * tok_rows for s in range(n)])
    cos_all, sin_all = rope_tables(key_places.astype(F32))
    cos, sin = cos_all[:tok_rows], sin_all[:tok_rows]

    inputs = tokens[0].astype(F32)
    attn_scale = norm_scale(inputs)
    wide = jnp.concatenate(token_shards, axis=0).astype(F32)
    attn_rows = (wide * norm_scale(wide) * attn_factor).astype(BF)
    bias = jnp.where(first, qkv_bias[:, :width], qkv_bias[:, width:])
    query, kv = qkv_call(
        attn_rows, attn_weight, bias.astype(F32).reshape(1, 3 * width), cos, sin, width
    )
    kvs = [kv] + [
        lax.ppermute(kv, "ctx", [(i, i + s) for i in range(n - s)]) for s in range(1, n)
    ]
    attended = attend_call(info, query, kvs, tok_rows, score_scale)
    half = nz * tok_rows

    def project_home(parts, weights):
        away = sum(dot_t(p[half:], w) for p, w in zip(parts, weights)).astype(BF)
        keep = sum(dot_t(p[:half], w) for p, w in zip(parts, weights)).astype(BF)
        return home_sum(keep, away)

    hidden = inputs + project_home([attended], [out_full])

    ffn_scale = norm_scale(hidden)
    normed_ffn = (hidden * ffn_scale * ffn_factor).astype(BF)
    ffn_rows = gather_rows(normed_ffn)
    small = jnp.concatenate([router_t, gate_full[None]], axis=0)
    logits = dot_t(ffn_rows, small)
    probs_all = jax.nn.softmax(logits[:, :experts], axis=1)
    sig_all = jax.nn.sigmoid(logits[:, experts:])
    own_col = (jnp.arange(experts, dtype=jnp.int32) == own_expert).astype(F32)[None]
    gate_all = jnp.sum(probs_all * own_col, axis=1, keepdims=True) * routed_own
    is_expert = lax.broadcasted_iota(jnp.int32, (1, units + shared), 1) < units
    row_scale = jnp.where(is_expert, gate_all, sig_all)

    gate_pre = jnp.dot(ffn_rows, gate_weight, preferred_element_type=F32)
    up_pre = jnp.dot(ffn_rows, up_weight, preferred_element_type=F32)
    act = jax.nn.silu(gate_pre) * up_pre
    act_scaled = (act * row_scale).astype(BF)
    result = hidden + project_home([act_scaled], [down_weight])
    grad_result = factor * valid_rows * (result - teacher[0])

    back_rows = gather_rows(grad_result.astype(BF))
    grad_act = jnp.dot(back_rows, down_weight, preferred_element_type=F32)
    touched = act * grad_act
    grad_gate_all = jnp.sum(touched[:, :units], axis=1) * routed_own[:, 0]
    grad_sig_all = jnp.sum(touched[:, units:], axis=1)
    scaled = grad_act * row_scale
    sigmoid_gate = jax.nn.sigmoid(gate_pre)
    grad_gate_pre = (
        scaled * up_pre * sigmoid_gate * (1.0 + gate_pre * (1.0 - sigmoid_gate))
    ).astype(BF)
    grad_up_pre = (scaled * gate_pre * sigmoid_gate).astype(BF)
    scalar_rows = jnp.concatenate(
        [own_col.T * grad_gate_all[None], grad_sig_all[None]], axis=0
    ).reshape(experts + 1, 2, nz, tok_rows)
    scalar_both = scalar_rows[:, 0] + core_swap(scalar_rows[:, 1])
    scalar_own = scalar_both[:, 0]
    for s in range(1, nz):
        scalar_own = scalar_own + shift(scalar_both[:, s], "exp", -s)

    grad_normed = project_home([grad_gate_pre, grad_up_pre], [gate_weight, up_weight])
    grad_down = scatter_grad(dot_rows(back_rows, act_scaled).astype(BF))
    grad_gate = scatter_grad(dot_rows(ffn_rows, grad_gate_pre).astype(BF))
    grad_up = scatter_grad(dot_rows(ffn_rows, grad_up_pre).astype(BF))

    own_logits = dot_t(normed_ffn, small)
    probs = jax.nn.softmax(own_logits[:, :experts], axis=1)
    sig = jax.nn.sigmoid(own_logits[:, experts])
    grad_probs = scalar_own[:experts].T
    grad_logits = probs * (grad_probs - jnp.sum(probs * grad_probs, axis=1, keepdims=True))
    grad_sig = scalar_own[experts] * sig * (1.0 - sig)
    grad_small = jnp.concatenate([grad_logits, grad_sig[:, None]], axis=1)
    normed_wide = normed_ffn.astype(F32)
    grad_small_full = lax.dot_general(
        grad_small, normed_wide, (((0,), (0,)), ((), ())), precision=HIGHEST
    )
    grad_normed = grad_normed + jnp.dot(grad_small, small.astype(F32), precision=HIGHEST)
    grad_hidden_norm, grad_ffn_full = norm_back(hidden, ffn_scale, ffn_factor, grad_normed)
    grad_hidden = grad_result + grad_hidden_norm
    ffn_vectors = sum_everywhere(jnp.concatenate([grad_small_full, grad_ffn_full[None]], axis=0))

    attn_back = gather_rows(grad_hidden.astype(BF))
    grad_attended = jnp.dot(attn_back, out_full, preferred_element_type=F32).astype(BF)
    grad_query, grad_kv, *sent = attend_back_call(
        info, query, grad_attended, kvs, cos_all, sin_all, tok_rows, score_scale
    )
    for s, other in enumerate(sent, start=1):
        grad_kv = grad_kv + lax.ppermute(
            other, "ctx", [(i + s, i) for i in range(n - s)]
        ).astype(F32)
    grad_projected = jnp.concatenate([grad_query, grad_kv.astype(BF)], axis=1)
    grad_normed_attn = project_home([grad_projected], [attn_weight[:, : 3 * width]])
    grad_attn = scatter_grad(
        jnp.concatenate(
            [dot_rows(attn_rows, grad_projected), dot_rows(attn_back, attended)], axis=1
        ).astype(BF)
    )
    bias_own = jnp.sum(grad_projected.astype(F32), axis=0).reshape(3, width)
    blocks = model_width // width
    column = lax.broadcasted_iota(jnp.int32, (3, model_width), 1)
    bias_wide = jnp.where(column // width == own_expert, jnp.tile(bias_own, (1, blocks)), 0.0)
    grad_inputs_norm, grad_attn_full = norm_back(inputs, attn_scale, attn_factor, grad_normed_attn)
    grad_tokens = (grad_hidden + grad_inputs_norm)[None]
    attn_vectors = sum_everywhere(jnp.concatenate([bias_wide, grad_attn_full[None]], axis=0))

    def join(pair, axis):
        mine, theirs = pair
        return jnp.concatenate(
            [jnp.where(first, mine, theirs), jnp.where(first, theirs, mine)], axis=axis
        )

    def own_span(v):
        return lax.dynamic_slice_in_dim(v, me * span, span, 1)

    grad_qkv = join([g[:, : 3 * width].reshape(rows_w, 3, width) for g in grad_attn], 2)
    grad_out = join([g[:, 3 * width :] for g in grad_attn], 1)
    grad_expert_up = join(
        [
            jnp.concatenate([g[:, :units], u[:, :units]], axis=1)[:, None]
            for g, u in zip(grad_gate, grad_up)
        ],
        1,
    )
    grad_shared_up = join(
        [
            jnp.concatenate([g[:, None, units:], u[:, None, units:]], axis=1)
            for g, u in zip(grad_gate, grad_up)
        ],
        2,
    )
    grad_expert_down = join([g[:, None, :units] for g in grad_down], 1)
    grad_shared_down = join([g[:, units:] for g in grad_down], 1)
    ffn_own, attn_own = own_span(ffn_vectors), own_span(attn_vectors)
    return (
        result.astype(BF)[None],
        grad_tokens,
        attn_own[3],
        ffn_own[experts + 1],
        ffn_own[:experts].T,
        ffn_own[experts],
        grad_qkv,
        jnp.stack([attn_own[0], attn_own[2]]),
        attn_own[1],
        grad_out,
        grad_shared_up,
        grad_shared_down,
        grad_expert_up,
        grad_expert_down,
    )


def solution(mesh):
    every = ("dp", "ctx", "exp")
    return jax.shard_map(
        body,
        mesh=mesh,
        in_specs=(
            P(("dp", "exp"), "ctx", None),
            P(("dp", "exp"), "ctx", None),
            P(),
            P(("dp", "exp"), "ctx", None),
            P(every),
            P(every),
            P(every, None),
            P(every),
            P(("dp", "ctx"), None, "exp"),
            P(None, "exp"),
            P(("dp", "ctx"), "exp"),
            P(("dp", "ctx"), None, "exp"),
            P(("dp", "ctx"), "exp"),
            P(("dp", "ctx"), "exp", None),
            P(("dp", "ctx"), "exp", None),
        ),
        out_specs=(
            P(("dp", "exp"), "ctx", None),
            P(("dp", "exp"), "ctx", None),
            P(every),
            P(every),
            P(every, None),
            P(every),
            P(("dp", "ctx"), None, "exp"),
            P(None, every),
            P(every),
            P(("dp", "ctx"), "exp"),
            P(("dp", "ctx"), None, "exp"),
            P(("dp", "ctx"), "exp"),
            P(("dp", "ctx"), "exp", None),
            P(("dp", "ctx"), "exp", None),
        ),
        check_vma=False,
    )
```

```python
import functools

import jax
import jax.numpy as jnp
from jax import lax
from jax.experimental import pallas as pl
from jax.experimental.pallas import tpu as pltpu
from jax.sharding import PartitionSpec as P

HD = 128
EPSILON = 1e-06
ROPE_BASE = 1000000.0
NEGATIVE = -1e30
HIGHEST = lax.Precision.HIGHEST
BF = jnp.bfloat16
F32 = jnp.float32
TILE_M = 512
TILE_N = 256
PACE = 8


def core_swap(v):
    n = lax.axis_size("dp")
    return lax.ppermute(v, "dp", [(i, i ^ 1) for i in range(n)])


def y_swap(v):
    n = lax.axis_size("dp")
    return lax.ppermute(v, "dp", [(i, i ^ 2) for i in range(n)])


def shift(v, axis, s):
    n = lax.axis_size(axis)
    return lax.ppermute(v, axis, [(i, (i + s) % n) for i in range(n)])


def after(values, anchors):
    return lax.optimization_barrier((tuple(values), tuple(anchors)))[0]


def meet(*trees):
    return lax.optimization_barrier(trees)


def exchange(v):
    return lax.all_to_all(v, "exp", split_axis=0, concat_axis=0, tiled=True)


def gather_exp(v):
    nz = lax.axis_size("exp")
    wide = jnp.broadcast_to(v[None], (nz, *v.shape)).reshape(nz * v.shape[0], *v.shape[1:])
    return exchange(wide)


def gather_rows(v):
    return both_cores(gather_exp(v))


def both_cores(mine):
    return [mine, core_swap(mine)]


def home_start(keep, got):
    nz = lax.axis_size("exp")
    both = (keep.astype(F32) + got.astype(F32)).astype(keep.dtype)
    return both, list(exchange(both).reshape(nz, keep.shape[0] // nz, *keep.shape[1:]))


def total(parts):
    return functools.reduce(jnp.add, [p.astype(F32) for p in parts])


def sum_shifts(v, axis):
    return functools.reduce(
        jnp.add, [v] + [shift(v, axis, s) for s in range(1, lax.axis_size(axis))]
    )


def spread(v, size, index):
    place = lax.broadcasted_iota(jnp.int32, (size, *(1,) * v.ndim), 0)
    return jnp.where(place == index, v[None], jnp.zeros((), v.dtype))


def gather_group(v):
    v = sum_shifts(spread(v, lax.axis_size("exp"), lax.axis_index("exp")), "exp")
    v = spread(v, 2, lax.axis_index("dp") % 2)
    return v + core_swap(v)


def gather_plane(v):
    v = spread(v, 2, lax.axis_index("dp") // 2)
    v = v + y_swap(v)
    return sum_shifts(spread(v, lax.axis_size("ctx"), lax.axis_index("ctx")), "ctx")


def own_of(v, axis, size, index):
    return total(
        [
            shift(lax.dynamic_index_in_dim(v, lax.rem(index + s, size), 0, False), axis, s)
            if s
            else lax.dynamic_index_in_dim(v, index, 0, False)
            for s in range(size)
        ]
    )


def scatter_everywhere(v):
    y, c = lax.axis_index("dp") // 2, lax.axis_index("dp") % 2
    v = own_of(v, "ctx", lax.axis_size("ctx"), lax.axis_index("ctx"))
    pick = lax.dynamic_index_in_dim
    v = pick(v, y, 0, False) + y_swap(pick(v, 1 - y, 0, False))
    v = pick(v, c, 0, False) + core_swap(pick(v, 1 - c, 0, False))
    return own_of(v, "exp", lax.axis_size("exp"), lax.axis_index("exp"))


def weight_ctx(pair):
    return [shift(pair, "ctx", s) for s in range(1, lax.axis_size("ctx"))]


def weight_first(pair):
    return weight_ctx(pair), y_swap(pair)


def weight_second(px, py):
    n = lax.axis_size("ctx")
    return [y_swap(v[0])[None] for v in px], [shift(py[1], "ctx", s)[None] for s in range(1, n)]


def weight_blocks(pair, px, py, axy, bxy):
    near = [pair, *px]
    return (
        [(v, 0) for v in near]
        + [(v, 1) for v in near]
        + [(py, 0)]
        + [(v, 0) for v in axy]
        + [(py, 1)]
        + [(v, 0) for v in bxy]
    )


def block_spec(block, cols, at):
    array, index = block
    return pl.BlockSpec((None, array.shape[1], cols), lambda i, p: (index, 0, at(i)))


def arrays(blocks):
    return [array for array, _ in blocks]


def grad_first_y(groups):
    return y_swap(groups[1])


def grad_first_ctx(groups, anchors=()):
    lines = list(groups[3:])
    if anchors:
        lines = after(lines, anchors)
    return [shift(v, "ctx", -s) for s, v in enumerate(lines, start=1)]


def grad_first(groups):
    return grad_first_y(groups), grad_first_ctx(groups)


def grad_second(groups, far, sent):
    near, _, line, *_ = groups
    lines = [line, *sent]
    mine_sent = [
        shift(total([near[s], far[s]]).astype(BF), "ctx", -s) for s in range(1, near.shape[0])
    ]
    theirs_sent = y_swap(total([v[1] for v in lines]).astype(BF))
    return ([near[0], far[0]], [v[0] for v in lines]), (mine_sent, [theirs_sent])


def grad_last(kept, sent):
    mine, theirs = total(kept[0] + sent[0]), total(kept[1] + sent[1])
    return mine, core_swap(theirs.astype(BF)).astype(F32)


def cost(flops, transcendentals, bytes_accessed):
    return pl.CostEstimate(
        flops=flops // PACE,
        transcendentals=transcendentals // PACE,
        bytes_accessed=bytes_accessed // PACE,
    )


def whole(v):
    return pl.BlockSpec(v.shape, lambda *_: (0,) * v.ndim)


def window(places_ref, j, size):
    return pl.ds(pl.multiple_of(places_ref[j] * size, size), size)


def reorder(places_ref, row_refs, scratch, blocks):
    start = 0
    size = scratch.shape[1] // blocks
    for ref in row_refs:
        rows = ref.shape[0]
        for j in range(blocks):
            scratch[start : start + rows, j * size : (j + 1) * size] = ref[
                :, window(places_ref, j, size)
            ]
        start += rows


def turn(v):
    lane = lax.broadcasted_iota(jnp.int32, v.shape, 1)
    rolled = pltpu.roll(v, HD // 2, 1)
    return jnp.where(lane < HD // 2, -rolled, rolled)


def tiles_of(total_rows):
    tile = min(TILE_M, total_rows)
    return tile, total_rows // tile


def qkv_kernel(shards, blocks, places_ref, *refs):
    token_refs, refs = refs[:shards], refs[shards:]
    weight_refs, refs = refs[:blocks], refs[blocks:]
    gain_ref, bias_ref, cos_ref, sin_ref, rows_ref, q_ref, kv_ref, scratch = refs
    width = q_ref.shape[1]
    tokens = cos_ref.shape[0]
    piece = min(32, tokens)
    low = 0
    for ref in token_refs:

        def norm(i, _, ref=ref, low=low):
            at = pl.multiple_of(i * piece, piece)
            wide = ref[pl.ds(at, piece), :].astype(F32)
            scale = lax.rsqrt(jnp.mean(wide * wide, axis=1, keepdims=True) + EPSILON)
            rows_ref[pl.ds(low + at, piece), :] = (wide * scale * gain_ref[...]).astype(BF)
            return 0

        lax.fori_loop(0, ref.shape[0] // piece, norm, 0)
        low += ref.shape[0]
    reorder(places_ref, [rows_ref], scratch, blocks)
    tile, count = tiles_of(rows_ref.shape[0])
    cos = jnp.concatenate([cos_ref[...]] * (tile // tokens), axis=0)
    sin = jnp.concatenate([sin_ref[...]] * (tile // tokens), axis=0)

    def step(m, _):
        at = pl.ds(pl.multiple_of(m * tile, tile), tile)
        rows = scratch[at, :]
        for part in range(3):
            cols = slice(part * width, (part + 1) * width)
            weight = jnp.concatenate([w[:, cols] for w in weight_refs], axis=0)
            out = jnp.dot(rows, weight, preferred_element_type=F32) + bias_ref[:, cols]
            if part == 2:
                kv_ref[at, width:] = out.astype(BF)
                continue
            for h in range(width // HD):
                head = out[:, h * HD : (h + 1) * HD]
                head = (head * cos + turn(head) * sin).astype(BF)
                if part == 0:
                    q_ref[at, h * HD : (h + 1) * HD] = head
                else:
                    kv_ref[at, h * HD : (h + 1) * HD] = head
        return 0

    lax.fori_loop(0, count, step, 0)


def qkv_call(places, shards, weights, gain, bias, cos, sin, width):
    tokens, depth = shards[0].shape
    total_rows = tokens * len(shards)
    return pl.pallas_call(
        functools.partial(qkv_kernel, len(shards), len(weights)),
        grid_spec=pltpu.PrefetchScalarGridSpec(
            num_scalar_prefetch=1,
            grid=(1,),
            in_specs=[whole(s) for s in shards]
            + [block_spec(w, 3 * width, lambda i: 0) for w in weights]
            + [whole(v) for v in (gain, bias, cos, sin)],
            out_specs=[
                pl.BlockSpec((total_rows, depth), lambda i, p: (0, 0)),
                pl.BlockSpec((total_rows, width), lambda i, p: (0, 0)),
                pl.BlockSpec((total_rows, 2 * width), lambda i, p: (0, 0)),
            ],
            scratch_shapes=[pltpu.VMEM((total_rows, depth), BF)],
        ),
        out_shape=[
            jax.ShapeDtypeStruct((total_rows, depth), BF),
            jax.ShapeDtypeStruct((total_rows, width), BF),
            jax.ShapeDtypeStruct((total_rows, 2 * width), BF),
        ],
        cost_estimate=cost(
            flops=2 * total_rows * depth * 3 * width,
            transcendentals=0,
            bytes_accessed=2 * (2 * total_rows * depth + depth * 3 * width),
        ),
        name="qkv_rope",
    )(places, *shards, *arrays(weights), gain, bias, cos, sin)


def up_kernel(shards, blocks, experts, info_ref, *refs):
    row_refs, refs = refs[:shards], refs[shards:]
    gate_refs, up_refs, refs = refs[:blocks], refs[blocks : 2 * blocks], refs[2 * blocks :]
    small_ref, chosen_ref, act_ref, gate_ref, up_ref, scale_ref, scratch = refs
    step_n = pl.program_id(0)
    own = info_ref[blocks]
    units = info_ref[blocks + 1]
    tile, count = tiles_of(scratch.shape[0])

    @pl.when(step_n == 0)
    def _():
        tokens = row_refs[0].shape[0]
        for k, ref in enumerate(row_refs):
            logits = lax.dot_general(
                ref[...], small_ref[...], (((1,), (1,)), ((), ())), preferred_element_type=F32
            )
            lane = lax.broadcasted_iota(jnp.int32, logits.shape, 1)
            kept = jnp.where(lane < experts, logits, NEGATIVE)
            raised = jnp.exp(kept - jnp.max(kept, axis=1, keepdims=True))
            prob = raised / jnp.sum(raised, axis=1, keepdims=True)
            chosen = chosen_ref[k * tokens : (k + 1) * tokens, :].astype(F32)
            routed = jnp.sum(jnp.where(lane == own, chosen, 0.0), axis=1, keepdims=True)
            gate = jnp.sum(jnp.where(lane == own, prob, 0.0), axis=1, keepdims=True) * routed
            sig = jax.nn.sigmoid(
                jnp.sum(jnp.where(lane == experts, logits, 0.0), axis=1, keepdims=True)
            )
            place = lax.broadcasted_iota(jnp.int32, (tokens, HD), 1)
            scale_ref[k * tokens : (k + 1) * tokens, :] = jnp.where(
                place == 0, gate, jnp.where(place == 1, sig, routed)
            )
        reorder(info_ref, row_refs, scratch, blocks)

    def step(m, _):
        at = pl.ds(pl.multiple_of(m * tile, tile), tile)
        rows = scratch[at, :]
        gate = jnp.dot(
            rows, jnp.concatenate([w[...] for w in gate_refs], axis=0), preferred_element_type=F32
        )
        up = jnp.dot(
            rows, jnp.concatenate([w[...] for w in up_refs], axis=0), preferred_element_type=F32
        )
        gate_ref[at, :] = gate
        up_ref[at, :] = up
        col = lax.broadcasted_iota(jnp.int32, gate.shape, 1) + step_n * gate.shape[1]
        scale = jnp.where(col < units, scale_ref[at, 0:1], scale_ref[at, 1:2])
        act_ref[at, :] = (gate * jax.nn.sigmoid(gate) * up * scale).astype(BF)
        return 0

    lax.fori_loop(0, count, step, 0)


def up_call(info, shards, gates, ups, small, chosen, experts):
    tokens, depth = shards[0].shape
    total_rows, cols = tokens * len(shards), gates[0][0].shape[2]
    out = pl.BlockSpec((total_rows, TILE_N), lambda i, p: (0, i))
    return pl.pallas_call(
        functools.partial(up_kernel, len(shards), len(gates), experts),
        grid_spec=pltpu.PrefetchScalarGridSpec(
            num_scalar_prefetch=1,
            grid=(pl.cdiv(cols, TILE_N),),
            in_specs=[whole(s) for s in shards]
            + [block_spec(w, TILE_N, lambda i: i) for w in gates + ups]
            + [whole(small), whole(chosen)],
            out_specs=[out, out, out, pl.BlockSpec((total_rows, HD), lambda i, p: (0, 0))],
            scratch_shapes=[pltpu.VMEM((total_rows, depth), BF)],
        ),
        out_shape=[
            jax.ShapeDtypeStruct((total_rows, cols), BF),
            jax.ShapeDtypeStruct((total_rows, cols), F32),
            jax.ShapeDtypeStruct((total_rows, cols), F32),
            jax.ShapeDtypeStruct((total_rows, HD), F32),
        ],
        cost_estimate=cost(
            flops=4 * total_rows * depth * cols,
            transcendentals=total_rows * cols,
            bytes_accessed=2 * (total_rows * depth + 2 * depth * cols) + 10 * total_rows * cols,
        ),
        name="expert_up",
    )(info, *shards, *arrays(gates + ups), small, chosen)


def down_back_kernel(shards, blocks, cols, info_ref, *refs):
    row_refs, refs = refs[:shards], refs[shards:]
    weight_refs, refs = refs[:blocks], refs[blocks:]
    gate_ref, up_ref, scale_ref, dgate_ref, dup_ref, sums_ref, scratch = refs
    step_n = pl.program_id(0)
    units = info_ref[blocks + 1]
    tile, count = tiles_of(scratch.shape[0])

    @pl.when(step_n == 0)
    def _():
        reorder(info_ref, row_refs, scratch, blocks)
        sums_ref[...] = jnp.zeros_like(sums_ref)

    def step(m, _):
        at = pl.ds(pl.multiple_of(m * tile, tile), tile)
        back = jnp.dot(
            scratch[at, :],
            jnp.concatenate([w[...] for w in weight_refs], axis=0),
            preferred_element_type=F32,
        )
        gate, up = gate_ref[at, :], up_ref[at, :]
        sig = jax.nn.sigmoid(gate)
        act = gate * sig
        col = lax.broadcasted_iota(jnp.int32, gate.shape, 1) + step_n * gate.shape[1]
        inside = col < units
        touched = act * up * back
        expert_sum = jnp.sum(jnp.where(inside, touched, 0.0), axis=1, keepdims=True)
        shared_sum = jnp.sum(
            jnp.where(jnp.logical_not(inside) & (col < cols), touched, 0.0), axis=1, keepdims=True
        )
        place = lax.broadcasted_iota(jnp.int32, (tile, HD), 1)
        sums_ref[at, :] += jnp.where(
            place == 0, expert_sum * scale_ref[at, 2:3], jnp.where(place == 1, shared_sum, 0.0)
        )
        scaled = back * jnp.where(inside, scale_ref[at, 0:1], scale_ref[at, 1:2])
        dup_ref[at, :] = (scaled * act).astype(BF)
        dgate_ref[at, :] = (scaled * up * sig * (1.0 + gate * (1.0 - sig))).astype(BF)
        return 0

    lax.fori_loop(0, count, step, 0)


def down_back_call(info, shards, weights, gate, up, scales):
    tokens, depth = shards[0].shape
    total_rows, cols = gate.shape
    out = pl.BlockSpec((total_rows, TILE_N), lambda i, p: (0, i))
    return pl.pallas_call(
        functools.partial(down_back_kernel, len(shards), len(weights), cols),
        grid_spec=pltpu.PrefetchScalarGridSpec(
            num_scalar_prefetch=1,
            grid=(pl.cdiv(cols, TILE_N),),
            in_specs=[whole(s) for s in shards]
            + [block_spec(w, TILE_N, lambda i: i) for w in weights]
            + [out, out, whole(scales)],
            out_specs=[out, out, whole(scales)],
            scratch_shapes=[pltpu.VMEM((total_rows, depth), BF)],
        ),
        out_shape=[
            jax.ShapeDtypeStruct((total_rows, cols), BF),
            jax.ShapeDtypeStruct((total_rows, cols), BF),
            jax.ShapeDtypeStruct((total_rows, HD), F32),
        ],
        cost_estimate=cost(
            flops=2 * total_rows * depth * cols,
            transcendentals=total_rows * cols,
            bytes_accessed=2 * (total_rows * depth + depth * cols) + 12 * total_rows * cols,
        ),
        name="down_back",
    )(info, *shards, *arrays(weights), gate, up, scales)


def out_back_kernel(shards, blocks, places_ref, *refs):
    row_refs, refs = refs[:shards], refs[shards:]
    weight_refs, (out_ref, rows_ref, scratch) = refs[:blocks], refs[blocks:]
    tokens = row_refs[0].shape[0]
    for k, ref in enumerate(row_refs):
        rows_ref[k * tokens : (k + 1) * tokens, :] = ref[...]
    reorder(places_ref, row_refs, scratch, blocks)
    tile, count = tiles_of(scratch.shape[0])

    def step(m, _):
        at = pl.ds(pl.multiple_of(m * tile, tile), tile)
        out_ref[at, :] = jnp.dot(
            scratch[at, :],
            jnp.concatenate([w[...] for w in weight_refs], axis=0),
            preferred_element_type=F32,
        ).astype(BF)
        return 0

    lax.fori_loop(0, count, step, 0)


def out_back_call(places, shards, weights, width):
    tokens, depth = shards[0].shape
    total_rows = tokens * len(shards)
    return pl.pallas_call(
        functools.partial(out_back_kernel, len(shards), len(weights)),
        grid_spec=pltpu.PrefetchScalarGridSpec(
            num_scalar_prefetch=1,
            grid=(1,),
            in_specs=[whole(s) for s in shards]
            + [block_spec(w, width, lambda i: 3) for w in weights],
            out_specs=[
                pl.BlockSpec((total_rows, width), lambda i, p: (0, 0)),
                pl.BlockSpec((total_rows, depth), lambda i, p: (0, 0)),
            ],
            scratch_shapes=[pltpu.VMEM((total_rows, depth), BF)],
        ),
        out_shape=[
            jax.ShapeDtypeStruct((total_rows, width), BF),
            jax.ShapeDtypeStruct((total_rows, depth), BF),
        ],
        cost_estimate=cost(
            flops=2 * total_rows * depth * width,
            transcendentals=0,
            bytes_accessed=2 * (2 * total_rows * depth + depth * width),
        ),
        name="out_back",
    )(places, *shards, *arrays(weights))


def home_kernel(pairs, indices, start, places_ref, *refs):
    blocks = len(indices) // pairs
    act_refs, refs = refs[:pairs], refs[pairs:]
    weight_refs, refs = refs[: pairs * blocks], refs[pairs * blocks :]
    keep_ref, away_ref, held, sems = refs
    size, cols = held.shape[2:]

    def copy(p, j, source, index):
        return pltpu.make_async_copy(
            source.at[index, :, start : start + cols], held.at[p, j], sems.at[p, j]
        )

    for j in range(blocks):
        for p in range(pairs):
            copy(p, j, weight_refs[p * blocks + j], indices[p * blocks + j]).start()
    half = keep_ref.shape[0]
    tile, count = tiles_of(half)

    def step(j, _):
        for p in range(pairs):
            copy(p, j, weight_refs[p * blocks], 0).wait()
        to = window(places_ref, j, size)
        for h, out_ref in enumerate((keep_ref, away_ref)):
            for m in range(count):
                at = slice(h * half + m * tile, h * half + (m + 1) * tile)
                out = functools.reduce(
                    jnp.add,
                    [
                        lax.dot_general(
                            act_refs[p][at, :],
                            held[p, j],
                            (((1,), (1,)), ((), ())),
                            preferred_element_type=F32,
                        )
                        for p in range(pairs)
                    ],
                )
                out_ref[m * tile : (m + 1) * tile, to] = out.astype(BF)
        return 0

    lax.fori_loop(0, blocks, step, 0)


def project_home(places, acts, weights, depth, start=0):
    total_rows, cols = acts[0].shape
    blocks, size = len(weights[0]), weights[0][0][0].shape[1]
    every = [w for blocks_of in weights for w in blocks_of]
    half = pl.BlockSpec((total_rows // 2, depth), lambda i, p: (0, 0))
    keep, away = pl.pallas_call(
        functools.partial(home_kernel, len(acts), [i for _, i in every], start),
        grid_spec=pltpu.PrefetchScalarGridSpec(
            num_scalar_prefetch=1,
            grid=(1,),
            in_specs=[whole(a) for a in acts]
            + [pl.BlockSpec(memory_space=pl.ANY)] * (len(acts) * blocks),
            out_specs=[half, half],
            scratch_shapes=[
                pltpu.VMEM((len(acts), blocks, size, cols), BF),
                pltpu.SemaphoreType.DMA((len(acts), blocks)),
            ],
        ),
        out_shape=[jax.ShapeDtypeStruct((total_rows // 2, depth), BF)] * 2,
        cost_estimate=cost(
            flops=2 * total_rows * depth * cols * len(acts),
            transcendentals=0,
            bytes_accessed=2 * (total_rows * depth + len(acts) * cols * (depth + total_rows)),
        ),
        name="project_home",
    )(places, *acts, *arrays(every))
    return keep, away


def weight_grad_kernel(n, lists, places_ref, *refs):
    row_refs, out_refs = [], refs[-(2 + n) :]
    at = 0
    for count in lists:
        row_refs.append(refs[at : at + count])
        at += count
    part_refs = refs[at : at + len(lists)]
    j = pl.program_id(0)
    low = 0
    for rows, part in zip(row_refs, part_refs):
        left = jnp.concatenate([r[...] for r in rows], axis=0)
        out = lax.dot_general(
            left, part[...], (((0,), (0,)), ((), ())), preferred_element_type=F32
        ).astype(BF)
        cols = slice(low, low + part.shape[1])
        low += part.shape[1]
        for g, ref in enumerate(out_refs):
            first = g * n if g < 2 else 2 * n + (g - 2) * 2
            last = first + (n if g < 2 else 2)

            @pl.when((j >= first) & (j < last))
            def _(ref=ref, out=out, cols=cols):
                ref[0, :, cols] = out


def weight_grad(order, pairs):
    n = lax.axis_size("ctx")
    blocks = 4 * n
    depth = pairs[0][0][0].shape[1]
    size = depth // blocks
    cols = sum(p.shape[1] for _, p in pairs)
    total_rows = pairs[0][1].shape[0]
    in_specs, operands = [], []
    for rows, _ in pairs:
        for r in rows:
            in_specs.append(pl.BlockSpec((r.shape[0], size), lambda j, o: (0, o[j])))
            operands.append(r)
    for _, part in pairs:
        in_specs.append(whole(part))
        operands.append(part)
    out_specs, out_shape = [], []
    for g in range(2 + n):
        first = g * n if g < 2 else 2 * n + (g - 2) * 2
        count = n if g < 2 else 2
        out_specs.append(
            pl.BlockSpec(
                (1, size, cols),
                lambda j, o, first=first, count=count: (
                    jnp.clip(j - first, 0, count - 1),
                    0,
                    0,
                ),
            )
        )
        out_shape.append(jax.ShapeDtypeStruct((count, size, cols), BF))
    return pl.pallas_call(
        functools.partial(weight_grad_kernel, n, [len(rows) for rows, _ in pairs]),
        grid_spec=pltpu.PrefetchScalarGridSpec(
            num_scalar_prefetch=1, grid=(blocks,), in_specs=in_specs, out_specs=out_specs
        ),
        out_shape=out_shape,
        cost_estimate=cost(
            flops=2 * total_rows * depth * cols,
            transcendentals=0,
            bytes_accessed=2 * (total_rows * (depth + cols) + depth * cols),
        ),
        name="weight_grad",
    )(order, *operands)


def probabilities(query, keys, length, x, scale):
    tokens, count = query.shape[0], keys.shape[0]
    scores = (
        lax.dot_general(query, keys, (((1,), (1,)), ((), ())), preferred_element_type=F32) * scale
    )
    row = lax.broadcasted_iota(jnp.int32, (tokens, count), 0) + x * tokens
    col = lax.broadcasted_iota(jnp.int32, (tokens, count), 1)
    place = jnp.zeros((tokens, count), jnp.int32)
    for s in range(count // tokens):
        inside = (col >= s * tokens) & (col < (s + 1) * tokens)
        place = jnp.where(inside, col - s * tokens + (x - s) * tokens, place)
    allowed = (place >= 0) & (place <= row) & (place < length)
    masked = jnp.where(allowed, scores, NEGATIVE)
    top = jnp.max(masked, axis=1, keepdims=True)
    weights = jnp.where(allowed, jnp.exp(masked - top), 0.0)
    return weights / jnp.sum(weights, axis=1, keepdims=True)


def attend_kernel(scale, info_ref, q_ref, *refs):
    kv_refs, out_ref = refs[:-1], refs[-1]
    group = pl.program_id(0)
    width = q_ref.shape[1]
    for h in range(width // HD):
        at = h * HD
        keys = jnp.concatenate([r[:, at : at + HD] for r in kv_refs], axis=0)
        values = jnp.concatenate([r[:, width + at : width + at + HD] for r in kv_refs], axis=0)
        prob = probabilities(
            q_ref[:, at : at + HD], keys, info_ref[group], info_ref[pl.num_programs(0)], scale
        )
        out_ref[:, at : at + HD] = jnp.dot(
            prob.astype(BF), values, preferred_element_type=F32
        ).astype(BF)


def attend_call(info, query, kvs, tokens, scale):
    total, width = query.shape
    groups = total // tokens
    return pl.pallas_call(
        functools.partial(attend_kernel, scale),
        grid_spec=pltpu.PrefetchScalarGridSpec(
            num_scalar_prefetch=1,
            grid=(groups,),
            in_specs=[pl.BlockSpec((tokens, width), lambda i, info: (i, 0))]
            + [pl.BlockSpec((tokens, 2 * width), lambda i, info: (i, 0)) for _ in kvs],
            out_specs=pl.BlockSpec((tokens, width), lambda i, info: (i, 0)),
        ),
        out_shape=jax.ShapeDtypeStruct((total, width), BF),
        cost_estimate=cost(
            flops=4 * total * width * tokens * len(kvs),
            transcendentals=total * tokens * len(kvs) * width // HD,
            bytes_accessed=2 * total * width * (2 + 2 * len(kvs)),
        ),
        name="attend",
    )(info, query, *kvs)


def unrope(grad, cos, sin):
    return grad * cos - turn(grad * sin)


def attend_back_kernel(scale, count, info_ref, q_ref, da_ref, *refs):
    kv_refs = refs[:count]
    cos_ref, sin_ref = refs[count : count + 2]
    dq_ref = refs[count + 2]
    dkv_refs = refs[count + 3 :]
    group = pl.program_id(0)
    tokens, width = q_ref.shape
    for h in range(width // HD):
        at = h * HD
        keys = jnp.concatenate([r[:, at : at + HD] for r in kv_refs], axis=0)
        values = jnp.concatenate([r[:, width + at : width + at + HD] for r in kv_refs], axis=0)
        query, grad = q_ref[:, at : at + HD], da_ref[:, at : at + HD]
        prob = probabilities(
            query, keys, info_ref[group], info_ref[pl.num_programs(0)], scale
        )
        dprob = lax.dot_general(
            grad, values, (((1,), (1,)), ((), ())), preferred_element_type=F32
        )
        row_dot = jnp.sum(prob * dprob, axis=1, keepdims=True)
        dscore = (prob * (dprob - row_dot)).astype(BF)
        dq = jnp.dot(dscore, keys, preferred_element_type=F32) * scale
        dq_ref[:, at : at + HD] = unrope(dq, cos_ref[:tokens], sin_ref[:tokens]).astype(BF)
        dk = (
            lax.dot_general(dscore, query, (((0,), (0,)), ((), ())), preferred_element_type=F32)
            * scale
        )
        dv = lax.dot_general(
            prob.astype(BF), grad, (((0,), (0,)), ((), ())), preferred_element_type=F32
        )
        for s in range(count):
            part = slice(s * tokens, (s + 1) * tokens)
            dkv_refs[s][:, at : at + HD] = unrope(dk[part], cos_ref[part], sin_ref[part]).astype(
                dkv_refs[s].dtype
            )
            dkv_refs[s][:, width + at : width + at + HD] = dv[part].astype(dkv_refs[s].dtype)


def attend_back_call(info, query, grad, kvs, cos, sin, tokens, scale):
    total, width = query.shape
    groups, count = total // tokens, len(kvs)
    one = pl.BlockSpec((tokens, width), lambda i, info: (i, 0))
    two = pl.BlockSpec((tokens, 2 * width), lambda i, info: (i, 0))
    table = pl.BlockSpec(cos.shape, lambda i, info: (0, 0))
    return pl.pallas_call(
        functools.partial(attend_back_kernel, scale, count),
        grid_spec=pltpu.PrefetchScalarGridSpec(
            num_scalar_prefetch=1,
            grid=(groups,),
            in_specs=[one, one] + [two] * count + [table, table],
            out_specs=[one] + [two] * count,
        ),
        out_shape=[jax.ShapeDtypeStruct((total, width), BF)]
        + [jax.ShapeDtypeStruct((total, 2 * width), F32 if s == 0 else BF) for s in range(count)],
        cost_estimate=cost(
            flops=10 * total * width * tokens * count,
            transcendentals=total * tokens * count * width // HD,
            bytes_accessed=2 * total * width * (3 + 5 * count),
        ),
        name="attend_back",
    )(info, query, grad, *kvs, cos, sin)


def rope_tables(positions):
    frequency = ROPE_BASE ** (-jnp.arange(0, HD, 2, dtype=F32) / HD)
    angles = positions[:, None] * frequency[None, :]
    return (
        jnp.concatenate([jnp.cos(angles), jnp.cos(angles)], axis=1),
        jnp.concatenate([jnp.sin(angles), jnp.sin(angles)], axis=1),
    )


def dot_t(a, b):
    return lax.dot_general(a, b, (((1,), (1,)), ((), ())), preferred_element_type=F32)


def norm_scale(values):
    return lax.rsqrt(jnp.mean(values * values, axis=1, keepdims=True) + EPSILON)


def norm_back(values, scale, gain, grads):
    weighted = grads * gain
    grad_values = scale * weighted - values * scale**3 * jnp.mean(
        weighted * values, axis=1, keepdims=True
    )
    return grad_values, jnp.sum(grads * values * scale, axis=0)


def body(
    tokens,
    teacher,
    lengths,
    routes,
    attn_gain,
    ffn_gain,
    router_weight,
    shared_gate,
    qkv_weight,
    qkv_bias,
    out_weight,
    shared_up,
    shared_down,
    expert_up,
    expert_down,
):
    tok_rows, model_width = tokens.shape[1:]
    nz, n = lax.axis_size("exp"), lax.axis_size("ctx")
    z, x, dp = lax.axis_index("exp"), lax.axis_index("ctx"), lax.axis_index("dp")
    c = dp % 2
    devices = lax.axis_size(("dp", "ctx", "exp"))
    seq_len = tok_rows * n
    experts = router_weight.shape[1]
    own_expert = 2 * z + c
    rows_w = qkv_weight.shape[0]
    width = qkv_weight.shape[2] // 2
    units, shared = expert_down.shape[2], shared_down.shape[1] // 2
    score_scale = HD ** (-0.5)
    first = c == 0

    def halves(v, axis):
        size = v.shape[axis] // 2
        low = lax.slice_in_dim(v, 0, size, axis=axis)
        high = lax.slice_in_dim(v, size, 2 * size, axis=axis)
        return jnp.where(first, low, high), jnp.where(first, high, low)

    token_mine = gather_exp(tokens[0])

    lanes = pl.cdiv(experts + 1, 16) * 16
    span = model_width // devices
    piece = jnp.concatenate(
        [router_weight.T, shared_gate[None], attn_gain[None], ffn_gain[None]], axis=0
    )
    held = pl.cdiv(experts + 3, 16) * 16
    piece = jnp.pad(piece, ((0, held - experts - 3), (0, tok_rows - span)))
    chosen = (
        (routes[0][None, :, :] == jnp.arange(lanes, dtype=jnp.int32)[:, None, None])
        .any(axis=2)
        .astype(BF)
    )
    grouped = gather_group(jnp.concatenate([piece, chosen], axis=0))
    vectors = gather_plane(grouped[:, :, : experts + 3, :span])
    chosen = grouped[:, :, held:]
    chosen = jnp.where(first, chosen, chosen[::-1])
    chosen_all = jnp.swapaxes(chosen, 2, 3).reshape(2 * nz * tok_rows, lanes)

    attn_halves = [
        jnp.concatenate([q[:, 0], q[:, 1], q[:, 2], o], axis=1)
        for q, o in zip(halves(qkv_weight, 2), halves(out_weight, 1))
    ]
    blank = jnp.zeros((rows_w, -(units + shared) % HD), BF)

    def pack(experts_of, shared_of):
        mine, other = [
            jnp.concatenate([e, s, blank], axis=1) for e, s in zip(experts_of, shared_of)
        ]
        return jnp.stack([mine, core_swap(other)])

    def up_pair(anchors, part):
        up_e, up_s = after((expert_up, shared_up), anchors)
        return pack(
            [v[:, 0] for v in halves(up_e[:, :, part * units : (part + 1) * units], 1)],
            halves(up_s[:, part], 1),
        )

    def down_pair(anchors):
        down_e, down_s = after((expert_down, shared_down), anchors)
        return pack([v[:, 0] for v in halves(down_e, 1)], halves(down_s, 1))

    attn_pair = jnp.stack([attn_halves[0], core_swap(attn_halves[1])])
    attn_near = weight_first(attn_pair)
    attn_far = weight_second(*attn_near)
    gate_pair = up_pair([attn_pair], 0)
    gate_near = weight_first(after((gate_pair,), attn_near)[0])
    token_mine, attn_near, attn_far, gate_pair, vectors = meet(
        token_mine, attn_near, attn_far, gate_pair, vectors
    )
    attn_weight = weight_blocks(attn_pair, *attn_near, *attn_far)
    vectors = vectors.transpose(4, 1, 2, 0, 3, 5).reshape(experts + 3, model_width)
    small = jnp.pad(vectors[: experts + 1], ((0, lanes - experts - 1), (0, 0)))
    attn_factor = vectors[experts + 1].astype(F32)[None]
    ffn_factor = vectors[experts + 2].astype(F32)[None]

    count_valid = jnp.sum(lengths).astype(F32)
    factor = lengths.shape[0] * seq_len / count_valid
    positions = x * tok_rows + jnp.arange(tok_rows, dtype=jnp.int32)
    own_length = lengths[dp * nz + z]
    valid_rows = (positions < own_length).astype(F32)[:, None]
    shard_dp = jnp.repeat(jnp.stack([dp, dp ^ 1]), nz)
    shard_z = jnp.tile(jnp.arange(nz, dtype=jnp.int32), 2)
    info = jnp.concatenate([lengths[shard_dp * nz + shard_z], x[None].astype(jnp.int32)])
    key_places = jnp.concatenate([positions - s * tok_rows for s in range(n)])
    cos_all, sin_all = rope_tables(key_places.astype(F32))
    cos, sin = cos_all[:tok_rows], sin_all[:tok_rows]

    def place(dy, dc, s):
        return (((dp // 2) ^ dy) * 2 + (c ^ dc)) * n + lax.rem(x + n - s, n)

    blocks = 4 * n
    places = jnp.stack(
        [place(dy, dc, s) for dy in range(2) for dc in range(2) for s in range(n)]
    ).astype(jnp.int32)
    order = jnp.stack(
        [place(dy, 0, s) for dy in range(2) for s in range(n)]
        + [place(dy, 1, s) for s in range(n) for dy in range(2)]
    ).astype(jnp.int32)
    facts = jnp.concatenate(
        [places, jnp.stack([own_expert, jnp.int32(units)]).astype(jnp.int32)]
    )

    inputs = tokens[0].astype(F32)
    attn_scale = norm_scale(inputs)
    bias = jnp.where(first, qkv_bias[:, :width], qkv_bias[:, width:])
    attn_rows, query, kv = qkv_call(
        places,
        both_cores(token_mine),
        attn_weight,
        attn_factor,
        bias.astype(F32).reshape(1, 3 * width),
        cos,
        sin,
        width,
    )
    kvs = [kv] + [
        lax.ppermute(kv, "ctx", [(i, i + s) for i in range(n - s)]) for s in range(1, n)
    ]
    upper_pair = up_pair([kv], 1)
    kvs, gate_near, upper_pair = meet(kvs, gate_near, upper_pair)
    gate_far = weight_second(*gate_near)
    upper_near = weight_first(upper_pair)
    attended = attend_call(info, query, kvs, tok_rows, score_scale)
    keep, away = project_home(places, [attended], [attn_weight], model_width, 3 * width)
    keep, away, gate_far = meet(keep, away, gate_far)
    gate_weight = weight_blocks(gate_pair, *gate_near, *gate_far)
    both, parts = home_start(keep, core_swap(away))
    lower_pair = down_pair([both])
    parts, upper_near, lower_pair = meet(parts, upper_near, lower_pair)
    upper_far = weight_second(*upper_near)
    lower_near = weight_first(lower_pair)
    hidden = inputs + total(parts)

    ffn_scale = norm_scale(hidden)
    normed_ffn = (hidden * ffn_scale * ffn_factor).astype(BF)
    ffn_mine, upper_far, lower_near = meet(gather_exp(normed_ffn), upper_far, lower_near)
    up_weight = weight_blocks(upper_pair, *upper_near, *upper_far)
    lower_far = weight_second(*lower_near)
    ffn_shards = both_cores(ffn_mine)
    act_scaled, gate_pre, up_pre, scales = up_call(
        facts, ffn_shards, gate_weight, up_weight, small, chosen_all, experts
    )
    down_weight = weight_blocks(lower_pair, *lower_near, *lower_far)
    keep, away = project_home(places, [act_scaled], [down_weight], model_width)
    _, parts = home_start(keep, core_swap(away))
    result = hidden + total(parts)
    grad_result = factor * valid_rows * (result - teacher[0])

    back_shards = gather_rows(grad_result.astype(BF))
    down_groups = weight_grad(order, [(back_shards, act_scaled)])
    down_moves = grad_first(down_groups)
    back_shards, down_groups = meet(back_shards, down_groups)
    grad_gate_pre, grad_up_pre, sums = down_back_call(
        facts, back_shards, down_weight, gate_pre, up_pre, scales
    )
    keep, away = project_home(
        places, [grad_gate_pre, grad_up_pre], [gate_weight, up_weight], model_width
    )
    got, down_moves = meet(core_swap(away), down_moves)
    both, parts = home_start(keep, got)
    own_col = (jnp.arange(experts, dtype=jnp.int32) == own_expert).astype(F32)[:, None]
    scalar_rows = jnp.concatenate(
        [own_col * sums[:, 0][None], sums[:, 1][None]], axis=0
    ).reshape(experts + 1, 2, nz, tok_rows)
    scalar_both = scalar_rows[:, 0] + core_swap(scalar_rows[:, 1])
    grad_gate_pre, grad_up_pre = after((grad_gate_pre, grad_up_pre), [both])
    gate_groups = weight_grad(order, [(ffn_shards, grad_gate_pre)])
    gate_moves = grad_first(gate_groups)
    (scalar_both,) = after((jnp.swapaxes(scalar_both, 0, 1),), [gate_groups])
    scalar_own = own_of(scalar_both, "exp", nz, z)
    down_kept, down_moves = grad_second(down_groups, *down_moves)
    parts, scalar_own, gate_groups, down_moves = meet(parts, scalar_own, gate_groups, down_moves)
    grad_normed = total(parts)

    own_logits = dot_t(normed_ffn, small)
    probs = jax.nn.softmax(own_logits[:, :experts], axis=1)
    sig = jax.nn.sigmoid(own_logits[:, experts])
    grad_probs = scalar_own[:experts].T
    grad_logits = probs * (grad_probs - jnp.sum(probs * grad_probs, axis=1, keepdims=True))
    grad_sig = scalar_own[experts] * sig * (1.0 - sig)
    grad_small = jnp.concatenate([grad_logits, grad_sig[:, None]], axis=1)
    normed_wide = normed_ffn.astype(F32)
    grad_small_full = lax.dot_general(
        grad_small, normed_wide, (((0,), (0,)), ((), ())), precision=HIGHEST
    )
    grad_normed = grad_normed + jnp.dot(
        grad_small, small[: experts + 1].astype(F32), precision=HIGHEST
    )
    grad_hidden_norm, grad_ffn_full = norm_back(hidden, ffn_scale, ffn_factor, grad_normed)
    grad_hidden = grad_result + grad_hidden_norm
    grad_hidden_low = grad_hidden.astype(BF)

    back_mine = gather_exp(grad_hidden_low)
    grad_up_pre = after((grad_up_pre,), [grad_hidden_low])[0]
    up_groups = weight_grad(order, [(ffn_shards, grad_up_pre)])
    back_mine, up_groups, gate_moves = meet(back_mine, up_groups, gate_moves)
    up_y = grad_first_y(up_groups)
    gate_kept, gate_moves = grad_second(gate_groups, *gate_moves)
    grad_attended, attn_back = out_back_call(places, both_cores(back_mine), attn_weight, width)
    grad_query, grad_kv, *sent = attend_back_call(
        info, query, grad_attended, kvs, cos_all, sin_all, tok_rows, score_scale
    )
    sent = [
        lax.ppermute(v, "ctx", [(i + s, i) for i in range(n - s)])
        for s, v in enumerate(sent, start=1)
    ]
    sent, gate_moves = meet(sent, gate_moves)
    up_ctx = grad_first_ctx(up_groups, [sent])
    grad_kv = total([grad_kv, *sent])
    grad_projected = jnp.concatenate([grad_query, grad_kv.astype(BF)], axis=1)
    keep, away = project_home(places, [grad_projected], [attn_weight], model_width)
    both, parts = home_start(keep, core_swap(away))
    up_y, up_ctx = after((up_y, up_ctx), [both])
    up_kept, up_moves = grad_second(up_groups, up_y, up_ctx)
    attn_groups = weight_grad(
        order,
        [
            ([attn_rows], after((grad_projected,), [up_y, up_ctx])[0]),
            ([attn_back], attended),
        ],
    )
    attn_moves = grad_first(attn_groups)
    down_kept, gate_kept = after((down_kept, gate_kept), [attn_groups])
    grad_down = grad_last(down_kept, down_moves)
    grad_gate = grad_last(gate_kept, gate_moves)
    bias_own = jnp.sum(grad_projected.astype(F32), axis=0).reshape(3, width)
    columns = 2 * nz
    column = lax.broadcasted_iota(jnp.int32, (3, columns * width), 1)
    bias_wide = jnp.where(column // width == own_expert, jnp.tile(bias_own, (1, columns)), 0.0)
    parts, attn_groups = meet(parts, attn_groups)
    grad_normed_attn = total(parts)
    grad_inputs_norm, grad_attn_full = norm_back(inputs, attn_scale, attn_factor, grad_normed_attn)
    grad_tokens = (grad_hidden + grad_inputs_norm)[None]
    vectors = jnp.concatenate(
        [bias_wide, grad_attn_full[None], grad_small_full, grad_ffn_full[None]], axis=0
    )
    vectors = scatter_everywhere(
        vectors.reshape(-1, 2, 2, n, nz, span).transpose(3, 1, 2, 4, 0, 5)
    )
    attn_kept, attn_moves = grad_second(attn_groups, *attn_moves)
    grad_up = grad_last(up_kept, up_moves)
    grad_attn = grad_last(attn_kept, attn_moves)

    def join(pair, axis):
        mine, theirs = pair
        return jnp.concatenate(
            [jnp.where(first, mine, theirs), jnp.where(first, theirs, mine)], axis=axis
        )

    grad_qkv = join([g[:, : 3 * width].reshape(rows_w, 3, width) for g in grad_attn], 2)
    grad_out = join([g[:, 3 * width :] for g in grad_attn], 1)
    grad_expert_up = join(
        [
            jnp.concatenate([g[:, :units], u[:, :units]], axis=1)[:, None]
            for g, u in zip(grad_gate, grad_up)
        ],
        1,
    )
    grad_shared_up = join(
        [
            jnp.concatenate([g[:, None, units : units + shared], u[:, None, units : units + shared]], axis=1)
            for g, u in zip(grad_gate, grad_up)
        ],
        2,
    )
    grad_expert_down = join([g[:, None, :units] for g in grad_down], 1)
    grad_shared_down = join([g[:, units : units + shared] for g in grad_down], 1)
    attn_own, ffn_own = vectors[:4], vectors[4:]
    return (
        result.astype(BF)[None],
        grad_tokens,
        attn_own[3],
        ffn_own[experts + 1],
        ffn_own[:experts].T,
        ffn_own[experts],
        grad_qkv,
        jnp.stack([attn_own[0], attn_own[2]]),
        attn_own[1],
        grad_out,
        grad_shared_up,
        grad_shared_down,
        grad_expert_up,
        grad_expert_down,
    )


def solution(mesh):
    every = ("dp", "ctx", "exp")
    return jax.shard_map(
        body,
        mesh=mesh,
        in_specs=(
            P(("dp", "exp"), "ctx", None),
            P(("dp", "exp"), "ctx", None),
            P(),
            P(("dp", "exp"), "ctx", None),
            P(every),
            P(every),
            P(every, None),
            P(every),
            P(("dp", "ctx"), None, "exp"),
            P(None, "exp"),
            P(("dp", "ctx"), "exp"),
            P(("dp", "ctx"), None, "exp"),
            P(("dp", "ctx"), "exp"),
            P(("dp", "ctx"), "exp", None),
            P(("dp", "ctx"), "exp", None),
        ),
        out_specs=(
            P(("dp", "exp"), "ctx", None),
            P(("dp", "exp"), "ctx", None),
            P(every),
            P(every),
            P(every, None),
            P(every),
            P(("dp", "ctx"), None, "exp"),
            P(None, every),
            P(every),
            P(("dp", "ctx"), "exp"),
            P(("dp", "ctx"), None, "exp"),
            P(("dp", "ctx"), "exp"),
            P(("dp", "ctx"), "exp", None),
            P(("dp", "ctx"), "exp", None),
        ),
        check_vma=False,
    )
```

```python
import functools

import jax
import jax.numpy as jnp
from jax import lax
from jax.experimental import pallas as pl
from jax.experimental.pallas import tpu as pltpu
from jax.sharding import PartitionSpec as P

HD = 128
EPSILON = 1e-06
ROPE_BASE = 1000000.0
NEGATIVE = -1e30
HIGHEST = lax.Precision.HIGHEST
BF = jnp.bfloat16
F32 = jnp.float32
TILE_M = 512
TILE_N = 256
PACE = 8


def core_swap(v):
    n = lax.axis_size("dp")
    return lax.ppermute(v, "dp", [(i, i ^ 1) for i in range(n)])


def y_swap(v):
    n = lax.axis_size("dp")
    return lax.ppermute(v, "dp", [(i, i ^ 2) for i in range(n)])


def shift(v, axis, s):
    n = lax.axis_size(axis)
    return lax.ppermute(v, axis, [(i, (i + s) % n) for i in range(n)])


def after(values, anchors):
    return lax.optimization_barrier((tuple(values), tuple(anchors)))[0]


def meet(*trees):
    return lax.optimization_barrier(trees)


def exchange(v):
    return lax.all_to_all(v, "exp", split_axis=0, concat_axis=0, tiled=True)


def gather_exp(v):
    nz = lax.axis_size("exp")
    wide = jnp.broadcast_to(v[None], (nz, *v.shape)).reshape(nz * v.shape[0], *v.shape[1:])
    return exchange(wide)


def gather_rows(v):
    return both_cores(gather_exp(v))


def both_cores(mine):
    return [mine, core_swap(mine)]


def home_start(keep, got):
    nz = lax.axis_size("exp")
    both = (keep.astype(F32) + got.astype(F32)).astype(keep.dtype)
    return both, list(exchange(both).reshape(nz, keep.shape[0] // nz, *keep.shape[1:]))


def total(parts):
    return functools.reduce(jnp.add, [p.astype(F32) for p in parts])


def sum_shifts(v, axis):
    return functools.reduce(
        jnp.add, [v] + [shift(v, axis, s) for s in range(1, lax.axis_size(axis))]
    )


def spread(v, size, index):
    place = lax.broadcasted_iota(jnp.int32, (size, *(1,) * v.ndim), 0)
    return jnp.where(place == index, v[None], jnp.zeros((), v.dtype))


def gather_group(v):
    v = sum_shifts(spread(v, lax.axis_size("exp"), lax.axis_index("exp")), "exp")
    v = spread(v, 2, lax.axis_index("dp") % 2)
    return v + core_swap(v)


def gather_plane(v):
    v = spread(v, 2, lax.axis_index("dp") // 2)
    v = v + y_swap(v)
    return sum_shifts(spread(v, lax.axis_size("ctx"), lax.axis_index("ctx")), "ctx")


def own_of(v, axis, size, index):
    return total(
        [
            shift(lax.dynamic_index_in_dim(v, lax.rem(index + s, size), 0, False), axis, s)
            if s
            else lax.dynamic_index_in_dim(v, index, 0, False)
            for s in range(size)
        ]
    )


def scatter_everywhere(v):
    y, c = lax.axis_index("dp") // 2, lax.axis_index("dp") % 2
    v = own_of(v, "ctx", lax.axis_size("ctx"), lax.axis_index("ctx"))
    pick = lax.dynamic_index_in_dim
    v = pick(v, y, 0, False) + y_swap(pick(v, 1 - y, 0, False))
    v = pick(v, c, 0, False) + core_swap(pick(v, 1 - c, 0, False))
    return own_of(v, "exp", lax.axis_size("exp"), lax.axis_index("exp"))


def weight_ctx(pair):
    return [shift(pair, "ctx", s) for s in range(1, lax.axis_size("ctx"))]


def weight_first(pair):
    return weight_ctx(pair), y_swap(pair)


def weight_second(px, py):
    n = lax.axis_size("ctx")
    return [y_swap(v[0])[None] for v in px], [shift(py[1], "ctx", s)[None] for s in range(1, n)]


def weight_blocks(pair, px, py, axy, bxy):
    near = [pair, *px]
    return (
        [(v, 0) for v in near]
        + [(v, 1) for v in near]
        + [(py, 0)]
        + [(v, 0) for v in axy]
        + [(py, 1)]
        + [(v, 0) for v in bxy]
    )


def block_spec(block, cols, at):
    array, index = block
    return pl.BlockSpec((None, array.shape[1], cols), lambda i, p: (index, 0, at(i)))


def arrays(blocks):
    return [array for array, _ in blocks]


def grad_first_y(groups):
    return y_swap(groups[1])


def grad_first_ctx(groups, anchors=()):
    lines = list(groups[3:])
    if anchors:
        lines = after(lines, anchors)
    return [shift(v, "ctx", -s) for s, v in enumerate(lines, start=1)]


def grad_first(groups):
    return grad_first_y(groups), grad_first_ctx(groups)


def grad_addends(groups, far, sent):
    near, _, line, *_ = groups
    lines = [line, *sent]
    kept = ([near[0], far[0]], [v[0] for v in lines])
    onward = (
        [total([near[s], far[s]]).astype(BF) for s in range(1, near.shape[0])],
        total([v[1] for v in lines]).astype(BF),
    )
    return kept, onward


def grad_moves(onward):
    return [shift(v, "ctx", -s) for s, v in enumerate(onward[0], start=1)], [y_swap(onward[1])]


def grad_second(groups, far, sent):
    kept, onward = grad_addends(groups, far, sent)
    return kept, grad_moves(onward)


def grad_last(kept, sent):
    mine, theirs = total(kept[0] + sent[0]), total(kept[1] + sent[1])
    return mine, core_swap(theirs.astype(BF)).astype(F32)


def cost(flops, transcendentals, bytes_accessed):
    return pl.CostEstimate(
        flops=flops // PACE,
        transcendentals=transcendentals // PACE,
        bytes_accessed=bytes_accessed // PACE,
    )


def whole(v):
    return pl.BlockSpec(v.shape, lambda *_: (0,) * v.ndim)


def window(places_ref, j, size):
    return pl.ds(pl.multiple_of(places_ref[j] * size, size), size)


def reorder(places_ref, row_refs, scratch, blocks):
    start = 0
    size = scratch.shape[1] // blocks
    for ref in row_refs:
        rows = ref.shape[0]
        for j in range(blocks):
            scratch[start : start + rows, j * size : (j + 1) * size] = ref[
                :, window(places_ref, j, size)
            ]
        start += rows


def turn(v):
    lane = lax.broadcasted_iota(jnp.int32, v.shape, 1)
    rolled = pltpu.roll(v, HD // 2, 1)
    return jnp.where(lane < HD // 2, -rolled, rolled)


def tiles_of(total_rows):
    tile = min(TILE_M, total_rows)
    return tile, total_rows // tile


def qkv_kernel(shards, blocks, places_ref, *refs):
    token_refs, refs = refs[:shards], refs[shards:]
    weight_refs, refs = refs[:blocks], refs[blocks:]
    gain_ref, bias_ref, cos_ref, sin_ref, rows_ref, q_ref, kv_ref, scratch = refs
    width = q_ref.shape[1]
    tokens = cos_ref.shape[0]
    piece = min(32, tokens)
    low = 0
    for ref in token_refs:

        def norm(i, _, ref=ref, low=low):
            at = pl.multiple_of(i * piece, piece)
            wide = ref[pl.ds(at, piece), :].astype(F32)
            scale = lax.rsqrt(jnp.mean(wide * wide, axis=1, keepdims=True) + EPSILON)
            rows_ref[pl.ds(low + at, piece), :] = (wide * scale * gain_ref[...]).astype(BF)
            return 0

        lax.fori_loop(0, ref.shape[0] // piece, norm, 0)
        low += ref.shape[0]
    reorder(places_ref, [rows_ref], scratch, blocks)
    tile, count = tiles_of(rows_ref.shape[0])
    cos = jnp.concatenate([cos_ref[...]] * (tile // tokens), axis=0)
    sin = jnp.concatenate([sin_ref[...]] * (tile // tokens), axis=0)

    def step(m, _):
        at = pl.ds(pl.multiple_of(m * tile, tile), tile)
        rows = scratch[at, :]
        for part in range(3):
            cols = slice(part * width, (part + 1) * width)
            weight = jnp.concatenate([w[:, cols] for w in weight_refs], axis=0)
            out = jnp.dot(rows, weight, preferred_element_type=F32) + bias_ref[:, cols]
            if part == 2:
                kv_ref[at, width:] = out.astype(BF)
                continue
            for h in range(width // HD):
                head = out[:, h * HD : (h + 1) * HD]
                head = (head * cos + turn(head) * sin).astype(BF)
                if part == 0:
                    q_ref[at, h * HD : (h + 1) * HD] = head
                else:
                    kv_ref[at, h * HD : (h + 1) * HD] = head
        return 0

    lax.fori_loop(0, count, step, 0)


def qkv_call(places, shards, weights, gain, bias, cos, sin, width):
    tokens, depth = shards[0].shape
    total_rows = tokens * len(shards)
    return pl.pallas_call(
        functools.partial(qkv_kernel, len(shards), len(weights)),
        grid_spec=pltpu.PrefetchScalarGridSpec(
            num_scalar_prefetch=1,
            grid=(1,),
            in_specs=[whole(s) for s in shards]
            + [block_spec(w, 3 * width, lambda i: 0) for w in weights]
            + [whole(v) for v in (gain, bias, cos, sin)],
            out_specs=[
                pl.BlockSpec((total_rows, depth), lambda i, p: (0, 0)),
                pl.BlockSpec((total_rows, width), lambda i, p: (0, 0)),
                pl.BlockSpec((total_rows, 2 * width), lambda i, p: (0, 0)),
            ],
            scratch_shapes=[pltpu.VMEM((total_rows, depth), BF)],
        ),
        out_shape=[
            jax.ShapeDtypeStruct((total_rows, depth), BF),
            jax.ShapeDtypeStruct((total_rows, width), BF),
            jax.ShapeDtypeStruct((total_rows, 2 * width), BF),
        ],
        cost_estimate=cost(
            flops=2 * total_rows * depth * 3 * width,
            transcendentals=0,
            bytes_accessed=2 * (2 * total_rows * depth + depth * 3 * width),
        ),
        name="qkv_rope",
    )(places, *shards, *arrays(weights), gain, bias, cos, sin)


def up_kernel(shards, blocks, experts, info_ref, *refs):
    row_refs, refs = refs[:shards], refs[shards:]
    gate_refs, up_refs, refs = refs[:blocks], refs[blocks : 2 * blocks], refs[2 * blocks :]
    small_ref, chosen_ref, act_ref, silu_ref, slope_ref, plain_ref, scale_ref, scratch = refs
    step_n = pl.program_id(0)
    own = info_ref[blocks]
    units = info_ref[blocks + 1]
    tile, count = tiles_of(scratch.shape[0])

    @pl.when(step_n == 0)
    def _():
        tokens = row_refs[0].shape[0]
        for k, ref in enumerate(row_refs):
            logits = lax.dot_general(
                ref[...], small_ref[...], (((1,), (1,)), ((), ())), preferred_element_type=F32
            )
            lane = lax.broadcasted_iota(jnp.int32, logits.shape, 1)
            kept = jnp.where(lane < experts, logits, NEGATIVE)
            raised = jnp.exp(kept - jnp.max(kept, axis=1, keepdims=True))
            prob = raised / jnp.sum(raised, axis=1, keepdims=True)
            chosen = chosen_ref[k * tokens : (k + 1) * tokens, :].astype(F32)
            routed = jnp.sum(jnp.where(lane == own, chosen, 0.0), axis=1, keepdims=True)
            gate = jnp.sum(jnp.where(lane == own, prob, 0.0), axis=1, keepdims=True) * routed
            sig = jax.nn.sigmoid(
                jnp.sum(jnp.where(lane == experts, logits, 0.0), axis=1, keepdims=True)
            )
            place = lax.broadcasted_iota(jnp.int32, (tokens, HD), 1)
            scale_ref[k * tokens : (k + 1) * tokens, :] = jnp.where(
                place == 0, gate, jnp.where(place == 1, sig, routed)
            )
        reorder(info_ref, row_refs, scratch, blocks)

    for m in range(count):
        at = slice(m * tile, (m + 1) * tile)
        rows = scratch[at, :]
        gate = jnp.dot(
            rows, jnp.concatenate([w[...] for w in gate_refs], axis=0), preferred_element_type=F32
        )
        up = jnp.dot(
            rows, jnp.concatenate([w[...] for w in up_refs], axis=0), preferred_element_type=F32
        )
        sig = jax.nn.sigmoid(gate)
        act = gate * sig
        plain = act * up
        silu_ref[at, :] = act.astype(BF)
        slope_ref[at, :] = (up * (sig + act * (1.0 - sig))).astype(BF)
        plain_ref[at, :] = plain.astype(BF)
        for h in range(TILE_N // HD):
            cols = slice(h * HD, (h + 1) * HD)
            expert = step_n * (TILE_N // HD) + h < units // HD
            scale = jnp.where(expert, scale_ref[at, 0:1], scale_ref[at, 1:2])
            act_ref[at, cols] = (plain[:, cols] * scale).astype(BF)


def up_call(info, shards, gates, ups, small, chosen, experts):
    tokens, depth = shards[0].shape
    total_rows, cols = tokens * len(shards), gates[0][0].shape[2]
    out = pl.BlockSpec((total_rows, TILE_N), lambda i, p: (0, i))
    return pl.pallas_call(
        functools.partial(up_kernel, len(shards), len(gates), experts),
        grid_spec=pltpu.PrefetchScalarGridSpec(
            num_scalar_prefetch=1,
            grid=(pl.cdiv(cols, TILE_N),),
            in_specs=[whole(s) for s in shards]
            + [block_spec(w, TILE_N, lambda i: i) for w in gates + ups]
            + [whole(small), whole(chosen)],
            out_specs=[out] * 4 + [pl.BlockSpec((total_rows, HD), lambda i, p: (0, 0))],
            scratch_shapes=[pltpu.VMEM((total_rows, depth), BF)],
        ),
        out_shape=[jax.ShapeDtypeStruct((total_rows, cols), BF)] * 4
        + [jax.ShapeDtypeStruct((total_rows, HD), F32)],
        cost_estimate=cost(
            flops=4 * total_rows * depth * cols,
            transcendentals=total_rows * cols,
            bytes_accessed=2 * (total_rows * depth + 2 * depth * cols) + 8 * total_rows * cols,
        ),
        name="expert_up",
    )(info, *shards, *arrays(gates + ups), small, chosen)


def down_back_kernel(shards, blocks, cols, info_ref, *refs):
    row_refs, refs = refs[:shards], refs[shards:]
    weight_refs, refs = refs[:blocks], refs[blocks:]
    silu_ref, slope_ref, plain_ref, scale_ref, dgate_ref, dup_ref, sums_ref, scratch, sums = refs
    step_n = pl.program_id(0)
    units = info_ref[blocks + 1]
    tile, count = tiles_of(scratch.shape[0])

    @pl.when(step_n == 0)
    def _():
        reorder(info_ref, row_refs, scratch, blocks)
        sums[...] = jnp.zeros_like(sums)

    for m in range(count):
        at = slice(m * tile, (m + 1) * tile)
        back = jnp.dot(
            scratch[at, :],
            jnp.concatenate([w[...] for w in weight_refs], axis=0),
            preferred_element_type=F32,
        )
        for h in range(TILE_N // HD):
            lane = slice(h * HD, (h + 1) * HD)
            group = step_n * (TILE_N // HD) + h
            expert = group < units // HD
            part = back[:, lane]
            touched = jnp.where(group < cols // HD, part * plain_ref[at, lane].astype(F32), 0.0)
            kind = jnp.where(expert, 0, 1)
            sums[kind, at, :] += touched
            scaled = part * jnp.where(expert, scale_ref[at, 0:1], scale_ref[at, 1:2])
            dup_ref[at, lane] = (scaled * silu_ref[at, lane].astype(F32)).astype(BF)
            dgate_ref[at, lane] = (scaled * slope_ref[at, lane].astype(F32)).astype(BF)

    @pl.when(step_n == pl.num_programs(0) - 1)
    def _():
        for m in range(count):
            at = slice(m * tile, (m + 1) * tile)
            place = lax.broadcasted_iota(jnp.int32, (tile, HD), 1)
            expert_sum = jnp.sum(sums[0, at, :], axis=1, keepdims=True) * scale_ref[at, 2:3]
            shared_sum = jnp.sum(sums[1, at, :], axis=1, keepdims=True)
            sums_ref[at, :] = jnp.where(
                place == 0, expert_sum, jnp.where(place == 1, shared_sum, 0.0)
            )


def down_back_call(info, shards, weights, silu, slope, plain, scales):
    tokens, depth = shards[0].shape
    total_rows, cols = silu.shape
    out = pl.BlockSpec((total_rows, TILE_N), lambda i, p: (0, i))
    return pl.pallas_call(
        functools.partial(down_back_kernel, len(shards), len(weights), cols),
        grid_spec=pltpu.PrefetchScalarGridSpec(
            num_scalar_prefetch=1,
            grid=(pl.cdiv(cols, TILE_N),),
            in_specs=[whole(s) for s in shards]
            + [block_spec(w, TILE_N, lambda i: i) for w in weights]
            + [out, out, out, whole(scales)],
            out_specs=[out, out, whole(scales)],
            scratch_shapes=[
                pltpu.VMEM((total_rows, depth), BF),
                pltpu.VMEM((2, total_rows, HD), F32),
            ],
        ),
        out_shape=[
            jax.ShapeDtypeStruct((total_rows, cols), BF),
            jax.ShapeDtypeStruct((total_rows, cols), BF),
            jax.ShapeDtypeStruct((total_rows, HD), F32),
        ],
        cost_estimate=cost(
            flops=2 * total_rows * depth * cols,
            transcendentals=0,
            bytes_accessed=2 * (total_rows * depth + depth * cols) + 10 * total_rows * cols,
        ),
        name="down_back",
    )(info, *shards, *arrays(weights), silu, slope, plain, scales)


def out_back_kernel(shards, blocks, places_ref, *refs):
    row_refs, refs = refs[:shards], refs[shards:]
    weight_refs, (out_ref, rows_ref, scratch) = refs[:blocks], refs[blocks:]
    tokens = row_refs[0].shape[0]
    for k, ref in enumerate(row_refs):
        rows_ref[k * tokens : (k + 1) * tokens, :] = ref[...]
    reorder(places_ref, row_refs, scratch, blocks)
    tile, count = tiles_of(scratch.shape[0])

    def step(m, _):
        at = pl.ds(pl.multiple_of(m * tile, tile), tile)
        out_ref[at, :] = jnp.dot(
            scratch[at, :],
            jnp.concatenate([w[...] for w in weight_refs], axis=0),
            preferred_element_type=F32,
        ).astype(BF)
        return 0

    lax.fori_loop(0, count, step, 0)


def out_back_call(places, shards, weights, width):
    tokens, depth = shards[0].shape
    total_rows = tokens * len(shards)
    return pl.pallas_call(
        functools.partial(out_back_kernel, len(shards), len(weights)),
        grid_spec=pltpu.PrefetchScalarGridSpec(
            num_scalar_prefetch=1,
            grid=(1,),
            in_specs=[whole(s) for s in shards]
            + [block_spec(w, width, lambda i: 3) for w in weights],
            out_specs=[
                pl.BlockSpec((total_rows, width), lambda i, p: (0, 0)),
                pl.BlockSpec((total_rows, depth), lambda i, p: (0, 0)),
            ],
            scratch_shapes=[pltpu.VMEM((total_rows, depth), BF)],
        ),
        out_shape=[
            jax.ShapeDtypeStruct((total_rows, width), BF),
            jax.ShapeDtypeStruct((total_rows, depth), BF),
        ],
        cost_estimate=cost(
            flops=2 * total_rows * depth * width,
            transcendentals=0,
            bytes_accessed=2 * (2 * total_rows * depth + depth * width),
        ),
        name="out_back",
    )(places, *shards, *arrays(weights))


def home_kernel(pairs, indices, start, places_ref, *refs):
    blocks = len(indices) // pairs
    act_refs, refs = refs[:pairs], refs[pairs:]
    weight_refs, refs = refs[: pairs * blocks], refs[pairs * blocks :]
    keep_ref, away_ref, held, sems = refs
    size, cols = held.shape[2:]

    def copy(p, j, source, index):
        return pltpu.make_async_copy(
            source.at[index, :, start : start + cols], held.at[p, j], sems.at[p, j]
        )

    for j in range(blocks):
        for p in range(pairs):
            copy(p, j, weight_refs[p * blocks + j], indices[p * blocks + j]).start()
    half = keep_ref.shape[0]
    tile, count = tiles_of(half)

    def step(j, _):
        for p in range(pairs):
            copy(p, j, weight_refs[p * blocks], 0).wait()
        to = window(places_ref, j, size)
        for h, out_ref in enumerate((keep_ref, away_ref)):
            for m in range(count):
                at = slice(h * half + m * tile, h * half + (m + 1) * tile)
                out = functools.reduce(
                    jnp.add,
                    [
                        lax.dot_general(
                            act_refs[p][at, :],
                            held[p, j],
                            (((1,), (1,)), ((), ())),
                            preferred_element_type=F32,
                        )
                        for p in range(pairs)
                    ],
                )
                out_ref[m * tile : (m + 1) * tile, to] = out.astype(BF)
        return 0

    lax.fori_loop(0, blocks, step, 0)


def project_home(places, acts, weights, depth, start=0):
    total_rows, cols = acts[0].shape
    blocks, size = len(weights[0]), weights[0][0][0].shape[1]
    every = [w for blocks_of in weights for w in blocks_of]
    half = pl.BlockSpec((total_rows // 2, depth), lambda i, p: (0, 0))
    keep, away = pl.pallas_call(
        functools.partial(home_kernel, len(acts), [i for _, i in every], start),
        grid_spec=pltpu.PrefetchScalarGridSpec(
            num_scalar_prefetch=1,
            grid=(1,),
            in_specs=[whole(a) for a in acts]
            + [pl.BlockSpec(memory_space=pl.ANY)] * (len(acts) * blocks),
            out_specs=[half, half],
            scratch_shapes=[
                pltpu.VMEM((len(acts), blocks, size, cols), BF),
                pltpu.SemaphoreType.DMA((len(acts), blocks)),
            ],
        ),
        out_shape=[jax.ShapeDtypeStruct((total_rows // 2, depth), BF)] * 2,
        cost_estimate=cost(
            flops=2 * total_rows * depth * cols * len(acts),
            transcendentals=0,
            bytes_accessed=2 * (total_rows * depth + len(acts) * cols * (depth + total_rows)),
        ),
        name="project_home",
    )(places, *acts, *arrays(every))
    return keep, away


def weight_grad_kernel(n, lists, places_ref, *refs):
    row_refs, out_refs = [], refs[-(2 + n) :]
    at = 0
    for count in lists:
        row_refs.append(refs[at : at + count])
        at += count
    part_refs = refs[at : at + len(lists)]
    j = pl.program_id(0)
    low = 0
    for rows, part in zip(row_refs, part_refs):
        left = jnp.concatenate([r[...] for r in rows], axis=0)
        out = lax.dot_general(
            left, part[...], (((0,), (0,)), ((), ())), preferred_element_type=F32
        ).astype(BF)
        cols = slice(low, low + part.shape[1])
        low += part.shape[1]
        for g, ref in enumerate(out_refs):
            first = g * n if g < 2 else 2 * n + (g - 2) * 2
            last = first + (n if g < 2 else 2)

            @pl.when((j >= first) & (j < last))
            def _(ref=ref, out=out, cols=cols):
                ref[0, :, cols] = out


def weight_grad(order, pairs):
    n = lax.axis_size("ctx")
    blocks = 4 * n
    depth = pairs[0][0][0].shape[1]
    size = depth // blocks
    cols = sum(p.shape[1] for _, p in pairs)
    total_rows = pairs[0][1].shape[0]
    in_specs, operands = [], []
    for rows, _ in pairs:
        for r in rows:
            in_specs.append(pl.BlockSpec((r.shape[0], size), lambda j, o: (0, o[j])))
            operands.append(r)
    for _, part in pairs:
        in_specs.append(whole(part))
        operands.append(part)
    out_specs, out_shape = [], []
    for g in range(2 + n):
        first = g * n if g < 2 else 2 * n + (g - 2) * 2
        count = n if g < 2 else 2
        out_specs.append(
            pl.BlockSpec(
                (1, size, cols),
                lambda j, o, first=first, count=count: (
                    jnp.clip(j - first, 0, count - 1),
                    0,
                    0,
                ),
            )
        )
        out_shape.append(jax.ShapeDtypeStruct((count, size, cols), BF))
    return pl.pallas_call(
        functools.partial(weight_grad_kernel, n, [len(rows) for rows, _ in pairs]),
        grid_spec=pltpu.PrefetchScalarGridSpec(
            num_scalar_prefetch=1, grid=(blocks,), in_specs=in_specs, out_specs=out_specs
        ),
        out_shape=out_shape,
        cost_estimate=cost(
            flops=2 * total_rows * depth * cols,
            transcendentals=0,
            bytes_accessed=2 * (total_rows * (depth + cols) + depth * cols),
        ),
        name="weight_grad",
    )(order, *operands)


def allowed_keys(tokens, count, length, x):
    row = lax.broadcasted_iota(jnp.int32, (tokens, tokens), 0) + x * tokens
    col = lax.broadcasted_iota(jnp.int32, (tokens, tokens), 1)
    parts = []
    for s in range(count):
        place = col + (x - s) * tokens
        parts.append((place >= 0) & (place <= row) & (place < length))
    return jnp.concatenate(parts, axis=1)


def probabilities(query, keys, allowed, scale):
    scores = (
        lax.dot_general(query, keys, (((1,), (1,)), ((), ())), preferred_element_type=F32) * scale
    )
    masked = jnp.where(allowed, scores, NEGATIVE)
    top = jnp.max(masked, axis=1, keepdims=True)
    weights = jnp.where(allowed, jnp.exp(masked - top), 0.0)
    return weights / jnp.sum(weights, axis=1, keepdims=True)


def attend_kernel(scale, info_ref, q_ref, *refs):
    kv_refs, out_ref = refs[:-1], refs[-1]
    group = pl.program_id(0)
    tokens, width = q_ref.shape
    allowed = allowed_keys(tokens, len(kv_refs), info_ref[group], info_ref[pl.num_programs(0)])
    for h in range(width // HD):
        at = h * HD
        keys = jnp.concatenate([r[:, at : at + HD] for r in kv_refs], axis=0)
        values = jnp.concatenate([r[:, width + at : width + at + HD] for r in kv_refs], axis=0)
        prob = probabilities(q_ref[:, at : at + HD], keys, allowed, scale)
        out_ref[:, at : at + HD] = jnp.dot(
            prob.astype(BF), values, preferred_element_type=F32
        ).astype(BF)


def attend_call(info, query, kvs, tokens, scale):
    total, width = query.shape
    groups = total // tokens
    return pl.pallas_call(
        functools.partial(attend_kernel, scale),
        grid_spec=pltpu.PrefetchScalarGridSpec(
            num_scalar_prefetch=1,
            grid=(groups,),
            in_specs=[pl.BlockSpec((tokens, width), lambda i, info: (i, 0))]
            + [pl.BlockSpec((tokens, 2 * width), lambda i, info: (i, 0)) for _ in kvs],
            out_specs=pl.BlockSpec((tokens, width), lambda i, info: (i, 0)),
        ),
        out_shape=jax.ShapeDtypeStruct((total, width), BF),
        cost_estimate=cost(
            flops=4 * total * width * tokens * len(kvs),
            transcendentals=total * tokens * len(kvs) * width // HD,
            bytes_accessed=2 * total * width * (2 + 2 * len(kvs)),
        ),
        name="attend",
    )(info, query, *kvs)


def unrope(grad, cos, sin):
    return grad * cos - turn(grad * sin)


def attend_back_kernel(scale, count, info_ref, q_ref, da_ref, *refs):
    kv_refs = refs[:count]
    cos_ref, sin_ref = refs[count : count + 2]
    dq_ref = refs[count + 2]
    dkv_refs = refs[count + 3 :]
    group = pl.program_id(0)
    tokens, width = q_ref.shape
    allowed = allowed_keys(tokens, count, info_ref[group], info_ref[pl.num_programs(0)])
    for h in range(width // HD):
        at = h * HD
        keys = jnp.concatenate([r[:, at : at + HD] for r in kv_refs], axis=0)
        values = jnp.concatenate([r[:, width + at : width + at + HD] for r in kv_refs], axis=0)
        query, grad = q_ref[:, at : at + HD], da_ref[:, at : at + HD]
        prob = probabilities(query, keys, allowed, scale)
        dprob = lax.dot_general(
            grad, values, (((1,), (1,)), ((), ())), preferred_element_type=F32
        )
        row_dot = jnp.sum(prob * dprob, axis=1, keepdims=True)
        dscore = (prob * (dprob - row_dot)).astype(BF)
        dq = jnp.dot(dscore, keys, preferred_element_type=F32) * scale
        dq_ref[:, at : at + HD] = unrope(dq, cos_ref[:tokens], sin_ref[:tokens]).astype(BF)
        dk = (
            lax.dot_general(dscore, query, (((0,), (0,)), ((), ())), preferred_element_type=F32)
            * scale
        )
        dv = lax.dot_general(
            prob.astype(BF), grad, (((0,), (0,)), ((), ())), preferred_element_type=F32
        )
        for s in range(count):
            part = slice(s * tokens, (s + 1) * tokens)
            dkv_refs[s][:, at : at + HD] = unrope(dk[part], cos_ref[part], sin_ref[part]).astype(
                dkv_refs[s].dtype
            )
            dkv_refs[s][:, width + at : width + at + HD] = dv[part].astype(dkv_refs[s].dtype)


def attend_back_call(info, query, grad, kvs, cos, sin, tokens, scale):
    total, width = query.shape
    groups, count = total // tokens, len(kvs)
    one = pl.BlockSpec((tokens, width), lambda i, info: (i, 0))
    two = pl.BlockSpec((tokens, 2 * width), lambda i, info: (i, 0))
    table = pl.BlockSpec(cos.shape, lambda i, info: (0, 0))
    return pl.pallas_call(
        functools.partial(attend_back_kernel, scale, count),
        grid_spec=pltpu.PrefetchScalarGridSpec(
            num_scalar_prefetch=1,
            grid=(groups,),
            in_specs=[one, one] + [two] * count + [table, table],
            out_specs=[one] + [two] * count,
        ),
        out_shape=[jax.ShapeDtypeStruct((total, width), BF)]
        + [jax.ShapeDtypeStruct((total, 2 * width), F32 if s == 0 else BF) for s in range(count)],
        cost_estimate=cost(
            flops=10 * total * width * tokens * count,
            transcendentals=total * tokens * count * width // HD,
            bytes_accessed=2 * total * width * (3 + 5 * count),
        ),
        name="attend_back",
    )(info, query, grad, *kvs, cos, sin)


def rope_tables(positions):
    frequency = ROPE_BASE ** (-jnp.arange(0, HD, 2, dtype=F32) / HD)
    angles = positions[:, None] * frequency[None, :]
    return (
        jnp.concatenate([jnp.cos(angles), jnp.cos(angles)], axis=1),
        jnp.concatenate([jnp.sin(angles), jnp.sin(angles)], axis=1),
    )


def dot_t(a, b):
    return lax.dot_general(a, b, (((1,), (1,)), ((), ())), preferred_element_type=F32)


def norm_scale(values):
    return lax.rsqrt(jnp.mean(values * values, axis=1, keepdims=True) + EPSILON)


def norm_back(values, scale, gain, grads):
    weighted = grads * gain
    grad_values = scale * weighted - values * scale**3 * jnp.mean(
        weighted * values, axis=1, keepdims=True
    )
    return grad_values, jnp.sum(grads * values * scale, axis=0)


def body(
    tokens,
    teacher,
    lengths,
    routes,
    attn_gain,
    ffn_gain,
    router_weight,
    shared_gate,
    qkv_weight,
    qkv_bias,
    out_weight,
    shared_up,
    shared_down,
    expert_up,
    expert_down,
):
    tok_rows, model_width = tokens.shape[1:]
    nz, n = lax.axis_size("exp"), lax.axis_size("ctx")
    z, x, dp = lax.axis_index("exp"), lax.axis_index("ctx"), lax.axis_index("dp")
    c = dp % 2
    devices = lax.axis_size(("dp", "ctx", "exp"))
    seq_len = tok_rows * n
    experts = router_weight.shape[1]
    own_expert = 2 * z + c
    rows_w = qkv_weight.shape[0]
    width = qkv_weight.shape[2] // 2
    units, shared = expert_down.shape[2], shared_down.shape[1] // 2
    score_scale = HD ** (-0.5)
    first = c == 0

    def halves(v, axis):
        size = v.shape[axis] // 2
        low = lax.slice_in_dim(v, 0, size, axis=axis)
        high = lax.slice_in_dim(v, size, 2 * size, axis=axis)
        return jnp.where(first, low, high), jnp.where(first, high, low)

    token_mine = gather_exp(tokens[0])

    lanes = pl.cdiv(experts + 1, 16) * 16
    span = model_width // devices
    piece = jnp.concatenate(
        [router_weight.T, shared_gate[None], attn_gain[None], ffn_gain[None]], axis=0
    )
    held = pl.cdiv(experts + 3, 16) * 16
    piece = jnp.pad(piece, ((0, held - experts - 3), (0, tok_rows - span)))
    chosen = (
        (routes[0][None, :, :] == jnp.arange(lanes, dtype=jnp.int32)[:, None, None])
        .any(axis=2)
        .astype(BF)
    )
    grouped = gather_group(jnp.concatenate([piece, chosen], axis=0))
    vectors = gather_plane(grouped[:, :, : experts + 3, :span])
    chosen = grouped[:, :, held:]
    chosen = jnp.where(first, chosen, chosen[::-1])
    chosen_all = jnp.swapaxes(chosen, 2, 3).reshape(2 * nz * tok_rows, lanes)

    attn_halves = [
        jnp.concatenate([q[:, 0], q[:, 1], q[:, 2], o], axis=1)
        for q, o in zip(halves(qkv_weight, 2), halves(out_weight, 1))
    ]
    blank = jnp.zeros((rows_w, -(units + shared) % HD), BF)

    def pack(experts_of, shared_of):
        mine, other = [
            jnp.concatenate([e, s, blank], axis=1) for e, s in zip(experts_of, shared_of)
        ]
        return jnp.stack([mine, core_swap(other)])

    def up_pair(anchors, part):
        up_e, up_s = after((expert_up, shared_up), anchors)
        return pack(
            [v[:, 0] for v in halves(up_e[:, :, part * units : (part + 1) * units], 1)],
            halves(up_s[:, part], 1),
        )

    def down_pair(anchors):
        down_e, down_s = after((expert_down, shared_down), anchors)
        return pack([v[:, 0] for v in halves(down_e, 1)], halves(down_s, 1))

    attn_pair = jnp.stack([attn_halves[0], core_swap(attn_halves[1])])
    attn_near = weight_first(attn_pair)
    attn_far = weight_second(*attn_near)
    gate_pair = up_pair([attn_pair], 0)
    gate_near = weight_first(after((gate_pair,), attn_near)[0])
    token_mine, attn_near, attn_far, gate_pair, vectors = meet(
        token_mine, attn_near, attn_far, gate_pair, vectors
    )
    attn_weight = weight_blocks(attn_pair, *attn_near, *attn_far)
    vectors = vectors.transpose(4, 1, 2, 0, 3, 5).reshape(experts + 3, model_width)
    small = jnp.pad(vectors[: experts + 1], ((0, lanes - experts - 1), (0, 0)))
    attn_factor = vectors[experts + 1].astype(F32)[None]
    ffn_factor = vectors[experts + 2].astype(F32)[None]

    count_valid = jnp.sum(lengths).astype(F32)
    factor = lengths.shape[0] * seq_len / count_valid
    positions = x * tok_rows + jnp.arange(tok_rows, dtype=jnp.int32)
    own_length = lengths[dp * nz + z]
    valid_rows = (positions < own_length).astype(F32)[:, None]
    shard_dp = jnp.repeat(jnp.stack([dp, dp ^ 1]), nz)
    shard_z = jnp.tile(jnp.arange(nz, dtype=jnp.int32), 2)
    info = jnp.concatenate([lengths[shard_dp * nz + shard_z], x[None].astype(jnp.int32)])
    key_places = jnp.concatenate([positions - s * tok_rows for s in range(n)])
    cos_all, sin_all = rope_tables(key_places.astype(F32))
    cos, sin = cos_all[:tok_rows], sin_all[:tok_rows]

    def place(dy, dc, s):
        return (((dp // 2) ^ dy) * 2 + (c ^ dc)) * n + lax.rem(x + n - s, n)

    blocks = 4 * n
    places = jnp.stack(
        [place(dy, dc, s) for dy in range(2) for dc in range(2) for s in range(n)]
    ).astype(jnp.int32)
    order = jnp.stack(
        [place(dy, 0, s) for dy in range(2) for s in range(n)]
        + [place(dy, 1, s) for s in range(n) for dy in range(2)]
    ).astype(jnp.int32)
    facts = jnp.concatenate(
        [places, jnp.stack([own_expert, jnp.int32(units)]).astype(jnp.int32)]
    )

    inputs = tokens[0].astype(F32)
    attn_scale = norm_scale(inputs)
    bias = jnp.where(first, qkv_bias[:, :width], qkv_bias[:, width:])
    attn_rows, query, kv = qkv_call(
        places,
        both_cores(token_mine),
        attn_weight,
        attn_factor,
        bias.astype(F32).reshape(1, 3 * width),
        cos,
        sin,
        width,
    )
    kvs = [kv] + [
        lax.ppermute(kv, "ctx", [(i, i + s) for i in range(n - s)]) for s in range(1, n)
    ]
    upper_pair = up_pair([kv], 1)
    kvs, gate_near, upper_pair = meet(kvs, gate_near, upper_pair)
    gate_far = weight_second(*gate_near)
    upper_near = weight_first(upper_pair)
    attended = attend_call(info, query, kvs, tok_rows, score_scale)
    keep, away = project_home(places, [attended], [attn_weight], model_width, 3 * width)
    keep, away, gate_far = meet(keep, away, gate_far)
    gate_weight = weight_blocks(gate_pair, *gate_near, *gate_far)
    both, parts = home_start(keep, core_swap(away))
    lower_pair = down_pair([both])
    parts, upper_near, lower_pair = meet(parts, upper_near, lower_pair)
    upper_far = weight_second(*upper_near)
    lower_near = weight_first(lower_pair)
    hidden = inputs + total(parts)

    ffn_scale = norm_scale(hidden)
    normed_ffn = (hidden * ffn_scale * ffn_factor).astype(BF)
    ffn_mine, upper_far, lower_near = meet(gather_exp(normed_ffn), upper_far, lower_near)
    up_weight = weight_blocks(upper_pair, *upper_near, *upper_far)
    lower_far = weight_second(*lower_near)
    ffn_shards = both_cores(ffn_mine)
    act_scaled, silu, slope, plain, scales = up_call(
        facts, ffn_shards, gate_weight, up_weight, small, chosen_all, experts
    )
    down_weight = weight_blocks(lower_pair, *lower_near, *lower_far)
    keep, away = project_home(places, [act_scaled], [down_weight], model_width)
    _, parts = home_start(keep, core_swap(away))
    result = hidden + total(parts)
    grad_result = factor * valid_rows * (result - teacher[0])

    back_shards = gather_rows(grad_result.astype(BF))
    down_groups = weight_grad(order, [(back_shards, act_scaled)])
    down_moves = grad_first(down_groups)
    back_shards, down_groups = meet(back_shards, down_groups)
    grad_gate_pre, grad_up_pre, sums = down_back_call(
        facts, back_shards, down_weight, silu, slope, plain, scales
    )
    keep, away = project_home(
        places, [grad_gate_pre, grad_up_pre], [gate_weight, up_weight], model_width
    )
    got, down_moves = meet(core_swap(away), down_moves)
    both, parts = home_start(keep, got)
    own_col = (jnp.arange(experts, dtype=jnp.int32) == own_expert).astype(F32)[:, None]
    scalar_rows = jnp.concatenate(
        [own_col * sums[:, 0][None], sums[:, 1][None]], axis=0
    ).reshape(experts + 1, 2, nz, tok_rows)
    scalar_both = scalar_rows[:, 0] + core_swap(scalar_rows[:, 1])
    grad_gate_pre, grad_up_pre = after((grad_gate_pre, grad_up_pre), [both])
    wide_groups = weight_grad(order, [(ffn_shards, grad_gate_pre), (ffn_shards, grad_up_pre)])
    wide_moves = grad_first(wide_groups)
    (scalar_both,) = after((jnp.swapaxes(scalar_both, 0, 1),), [wide_groups])
    scalar_own = own_of(scalar_both, "exp", nz, z)
    down_kept, down_moves = grad_second(down_groups, *down_moves)
    parts, scalar_own, wide_groups, down_moves = meet(parts, scalar_own, wide_groups, down_moves)
    grad_normed = total(parts)

    own_logits = dot_t(normed_ffn, small)
    probs = jax.nn.softmax(own_logits[:, :experts], axis=1)
    sig = jax.nn.sigmoid(own_logits[:, experts])
    grad_probs = scalar_own[:experts].T
    grad_logits = probs * (grad_probs - jnp.sum(probs * grad_probs, axis=1, keepdims=True))
    grad_sig = scalar_own[experts] * sig * (1.0 - sig)
    grad_small = jnp.concatenate([grad_logits, grad_sig[:, None]], axis=1)
    normed_wide = normed_ffn.astype(F32)
    grad_small_full = lax.dot_general(
        grad_small, normed_wide, (((0,), (0,)), ((), ())), precision=HIGHEST
    )
    grad_normed = grad_normed + jnp.dot(
        grad_small, small[: experts + 1].astype(F32), precision=HIGHEST
    )
    grad_hidden_norm, grad_ffn_full = norm_back(hidden, ffn_scale, ffn_factor, grad_normed)
    grad_hidden = grad_result + grad_hidden_norm
    grad_hidden_low = grad_hidden.astype(BF)

    down_kept, down_moves = after((down_kept, down_moves), [grad_hidden_low])
    back_mine, grad_down = meet(gather_exp(grad_hidden_low), grad_last(down_kept, down_moves))
    grad_attended, attn_back = out_back_call(places, both_cores(back_mine), attn_weight, width)
    grad_query, grad_kv, *sent = attend_back_call(
        info, query, grad_attended, kvs, cos_all, sin_all, tok_rows, score_scale
    )
    sent = [
        lax.ppermute(v, "ctx", [(i + s, i) for i in range(n - s)])
        for s, v in enumerate(sent, start=1)
    ]
    wide_kept, onward = grad_addends(wide_groups, *after(wide_moves, [grad_query]))
    sent, onward = meet(sent, onward)
    wide_moves = grad_moves(onward)
    grad_kv = total([grad_kv, *sent])
    grad_projected = jnp.concatenate([grad_query, grad_kv.astype(BF)], axis=1)
    keep, away = project_home(places, [grad_projected], [attn_weight], model_width)
    both, parts = home_start(keep, core_swap(away))
    attn_groups = weight_grad(
        order,
        [
            ([attn_rows], after((grad_projected,), [both])[0]),
            ([attn_back], attended),
        ],
    )
    attn_moves = grad_first(attn_groups)
    bias_own = jnp.sum(grad_projected.astype(F32), axis=0).reshape(3, width)
    columns = 2 * nz
    column = lax.broadcasted_iota(jnp.int32, (3, columns * width), 1)
    bias_wide = jnp.where(column // width == own_expert, jnp.tile(bias_own, (1, columns)), 0.0)
    parts, attn_groups = meet(parts, attn_groups)
    grad_normed_attn = total(parts)
    grad_inputs_norm, grad_attn_full = norm_back(inputs, attn_scale, attn_factor, grad_normed_attn)
    grad_tokens = (grad_hidden + grad_inputs_norm)[None]
    vectors = jnp.concatenate(
        [bias_wide, grad_attn_full[None], grad_small_full, grad_ffn_full[None]], axis=0
    )
    vectors = scatter_everywhere(
        vectors.reshape(-1, 2, 2, n, nz, span).transpose(3, 1, 2, 4, 0, 5)
    )
    attn_kept, attn_moves = grad_second(attn_groups, *attn_moves)
    grad_wide = grad_last(wide_kept, wide_moves)
    grad_gate = [g[:, : act_scaled.shape[1]] for g in grad_wide]
    grad_up = [g[:, act_scaled.shape[1] :] for g in grad_wide]
    grad_attn = grad_last(attn_kept, attn_moves)

    def join(pair, axis):
        mine, theirs = pair
        return jnp.concatenate(
            [jnp.where(first, mine, theirs), jnp.where(first, theirs, mine)], axis=axis
        )

    grad_qkv = join([g[:, : 3 * width].reshape(rows_w, 3, width) for g in grad_attn], 2)
    grad_out = join([g[:, 3 * width :] for g in grad_attn], 1)
    grad_expert_up = join(
        [
            jnp.concatenate([g[:, :units], u[:, :units]], axis=1)[:, None]
            for g, u in zip(grad_gate, grad_up)
        ],
        1,
    )
    grad_shared_up = join(
        [
            jnp.concatenate([g[:, None, units : units + shared], u[:, None, units : units + shared]], axis=1)
            for g, u in zip(grad_gate, grad_up)
        ],
        2,
    )
    grad_expert_down = join([g[:, None, :units] for g in grad_down], 1)
    grad_shared_down = join([g[:, units : units + shared] for g in grad_down], 1)
    attn_own, ffn_own = vectors[:4], vectors[4:]
    return (
        result.astype(BF)[None],
        grad_tokens,
        attn_own[3],
        ffn_own[experts + 1],
        ffn_own[:experts].T,
        ffn_own[experts],
        grad_qkv,
        jnp.stack([attn_own[0], attn_own[2]]),
        attn_own[1],
        grad_out,
        grad_shared_up,
        grad_shared_down,
        grad_expert_up,
        grad_expert_down,
    )


def solution(mesh):
    every = ("dp", "ctx", "exp")
    return jax.shard_map(
        body,
        mesh=mesh,
        in_specs=(
            P(("dp", "exp"), "ctx", None),
            P(("dp", "exp"), "ctx", None),
            P(),
            P(("dp", "exp"), "ctx", None),
            P(every),
            P(every),
            P(every, None),
            P(every),
            P(("dp", "ctx"), None, "exp"),
            P(None, "exp"),
            P(("dp", "ctx"), "exp"),
            P(("dp", "ctx"), None, "exp"),
            P(("dp", "ctx"), "exp"),
            P(("dp", "ctx"), "exp", None),
            P(("dp", "ctx"), "exp", None),
        ),
        out_specs=(
            P(("dp", "exp"), "ctx", None),
            P(("dp", "exp"), "ctx", None),
            P(every),
            P(every),
            P(every, None),
            P(every),
            P(("dp", "ctx"), None, "exp"),
            P(None, every),
            P(every),
            P(("dp", "ctx"), "exp"),
            P(("dp", "ctx"), None, "exp"),
            P(("dp", "ctx"), "exp"),
            P(("dp", "ctx"), "exp", None),
            P(("dp", "ctx"), "exp", None),
        ),
        check_vma=False,
    )
```

```python
import functools

import jax
import jax.numpy as jnp
from jax import lax
from jax.experimental import pallas as pl
from jax.experimental.pallas import tpu as pltpu
from jax.sharding import PartitionSpec as P

HD = 128
EPSILON = 1e-06
ROPE_BASE = 1000000.0
NEGATIVE = -1e30
HIGHEST = lax.Precision.HIGHEST
BF = jnp.bfloat16
F32 = jnp.float32
TILE_M = 512
TILE_N = 256
PACE = 8


def core_swap(v):
    n = lax.axis_size("dp")
    return lax.ppermute(v, "dp", [(i, i ^ 1) for i in range(n)])


def y_swap(v):
    n = lax.axis_size("dp")
    return lax.ppermute(v, "dp", [(i, i ^ 2) for i in range(n)])


def shift(v, axis, s):
    n = lax.axis_size(axis)
    return lax.ppermute(v, axis, [(i, (i + s) % n) for i in range(n)])


def after(values, anchors):
    return lax.optimization_barrier((tuple(values), tuple(anchors)))[0]


def meet(*trees):
    return lax.optimization_barrier(trees)


def exchange(v):
    return lax.all_to_all(v, "exp", split_axis=0, concat_axis=0, tiled=True)


def gather_exp(v):
    nz = lax.axis_size("exp")
    wide = jnp.broadcast_to(v[None], (nz, *v.shape)).reshape(nz * v.shape[0], *v.shape[1:])
    return exchange(wide)


def gather_rows(v):
    return both_cores(gather_exp(v))


def both_cores(mine):
    return [mine, core_swap(mine)]


def home_start(keep, got):
    nz = lax.axis_size("exp")
    both = (keep.astype(F32) + got.astype(F32)).astype(keep.dtype)
    return both, list(exchange(both).reshape(nz, keep.shape[0] // nz, *keep.shape[1:]))


def total(parts):
    return functools.reduce(jnp.add, [p.astype(F32) for p in parts])


def sum_shifts(v, axis):
    return functools.reduce(
        jnp.add, [v] + [shift(v, axis, s) for s in range(1, lax.axis_size(axis))]
    )


def spread(v, size, index):
    place = lax.broadcasted_iota(jnp.int32, (size, *(1,) * v.ndim), 0)
    return jnp.where(place == index, v[None], jnp.zeros((), v.dtype))


def gather_group(v):
    v = sum_shifts(spread(v, lax.axis_size("exp"), lax.axis_index("exp")), "exp")
    v = spread(v, 2, lax.axis_index("dp") % 2)
    return v + core_swap(v)


def gather_plane(v):
    v = spread(v, 2, lax.axis_index("dp") // 2)
    v = v + y_swap(v)
    return sum_shifts(spread(v, lax.axis_size("ctx"), lax.axis_index("ctx")), "ctx")


def own_of(v, axis, size, index):
    return total(
        [
            shift(lax.dynamic_index_in_dim(v, lax.rem(index + s, size), 0, False), axis, s)
            if s
            else lax.dynamic_index_in_dim(v, index, 0, False)
            for s in range(size)
        ]
    )


def scatter_everywhere(v):
    y, c = lax.axis_index("dp") // 2, lax.axis_index("dp") % 2
    v = own_of(v, "ctx", lax.axis_size("ctx"), lax.axis_index("ctx"))
    pick = lax.dynamic_index_in_dim
    v = pick(v, y, 0, False) + y_swap(pick(v, 1 - y, 0, False))
    v = pick(v, c, 0, False) + core_swap(pick(v, 1 - c, 0, False))
    return own_of(v, "exp", lax.axis_size("exp"), lax.axis_index("exp"))


def weight_ctx(pair):
    return [shift(pair, "ctx", s) for s in range(1, lax.axis_size("ctx"))]


def weight_first(pair):
    return weight_ctx(pair), y_swap(pair)


def weight_second(px, py):
    n = lax.axis_size("ctx")
    return [y_swap(v[0])[None] for v in px], [shift(py[1], "ctx", s)[None] for s in range(1, n)]


def weight_blocks(pair, px, py, axy, bxy):
    near = [pair, *px]
    return (
        [(v, 0) for v in near]
        + [(v, 1) for v in near]
        + [(py, 0)]
        + [(v, 0) for v in axy]
        + [(py, 1)]
        + [(v, 0) for v in bxy]
    )


def block_spec(block, cols, at):
    array, index = block
    return pl.BlockSpec((None, array.shape[1], cols), lambda i, p: (index, 0, at(i)))


def arrays(blocks):
    return [array for array, _ in blocks]


def grad_first_y(groups):
    return y_swap(groups[1])


def grad_first_ctx(groups, anchors=()):
    lines = list(groups[3:])
    if anchors:
        lines = after(lines, anchors)
    return [shift(v, "ctx", -s) for s, v in enumerate(lines, start=1)]


def grad_first(groups):
    return grad_first_y(groups), grad_first_ctx(groups)


def grad_addends(groups, far, sent):
    near, _, line, *_ = groups
    lines = [line, *sent]
    kept = ([near[0], far[0]], [v[0] for v in lines])
    onward = (
        [total([near[s], far[s]]).astype(BF) for s in range(1, near.shape[0])],
        total([v[1] for v in lines]).astype(BF),
    )
    return kept, onward


def grad_moves(onward):
    return [shift(v, "ctx", -s) for s, v in enumerate(onward[0], start=1)], [y_swap(onward[1])]


def grad_second(groups, far, sent):
    kept, onward = grad_addends(groups, far, sent)
    return kept, grad_moves(onward)


def grad_last(kept, sent):
    mine, theirs = total(kept[0] + sent[0]), total(kept[1] + sent[1])
    return mine, core_swap(theirs.astype(BF)).astype(F32)


def cost(flops, transcendentals, bytes_accessed):
    return pl.CostEstimate(
        flops=flops // PACE,
        transcendentals=transcendentals // PACE,
        bytes_accessed=bytes_accessed // PACE,
    )


def whole(v):
    return pl.BlockSpec(v.shape, lambda *_: (0,) * v.ndim)


def window(places_ref, j, size):
    return pl.ds(pl.multiple_of(places_ref[j] * size, size), size)


def reorder(places_ref, row_refs, scratch, blocks):
    start = 0
    size = scratch.shape[1] // blocks
    for ref in row_refs:
        rows = ref.shape[0]
        for j in range(blocks):
            scratch[start : start + rows, j * size : (j + 1) * size] = ref[
                :, window(places_ref, j, size)
            ]
        start += rows


def turn(v):
    lane = lax.broadcasted_iota(jnp.int32, v.shape, 1)
    rolled = pltpu.roll(v, HD // 2, 1)
    return jnp.where(lane < HD // 2, -rolled, rolled)


def tiles_of(total_rows):
    tile = min(TILE_M, total_rows)
    return tile, total_rows // tile


def qkv_kernel(shards, blocks, places_ref, *refs):
    token_refs, refs = refs[:shards], refs[shards:]
    weight_refs, refs = refs[:blocks], refs[blocks:]
    gain_ref, bias_ref, cos_ref, sin_ref, rows_ref, q_ref, kv_ref, scratch = refs
    width = q_ref.shape[1]
    tokens = cos_ref.shape[0]
    piece = min(32, tokens)
    low = 0
    for ref in token_refs:

        def norm(i, _, ref=ref, low=low):
            at = pl.multiple_of(i * piece, piece)
            wide = ref[pl.ds(at, piece), :].astype(F32)
            scale = lax.rsqrt(jnp.mean(wide * wide, axis=1, keepdims=True) + EPSILON)
            rows_ref[pl.ds(low + at, piece), :] = (wide * scale * gain_ref[...]).astype(BF)
            return 0

        lax.fori_loop(0, ref.shape[0] // piece, norm, 0)
        low += ref.shape[0]
    reorder(places_ref, [rows_ref], scratch, blocks)
    tile, count = tiles_of(rows_ref.shape[0])
    cos = jnp.concatenate([cos_ref[...]] * (tile // tokens), axis=0)
    sin = jnp.concatenate([sin_ref[...]] * (tile // tokens), axis=0)

    def step(m, _):
        at = pl.ds(pl.multiple_of(m * tile, tile), tile)
        rows = scratch[at, :]
        for part in range(3):
            cols = slice(part * width, (part + 1) * width)
            weight = jnp.concatenate([w[:, cols] for w in weight_refs], axis=0)
            out = jnp.dot(rows, weight, preferred_element_type=F32) + bias_ref[:, cols]
            if part == 2:
                kv_ref[at, width:] = out.astype(BF)
                continue
            for h in range(width // HD):
                head = out[:, h * HD : (h + 1) * HD]
                head = (head * cos + turn(head) * sin).astype(BF)
                if part == 0:
                    q_ref[at, h * HD : (h + 1) * HD] = head
                else:
                    kv_ref[at, h * HD : (h + 1) * HD] = head
        return 0

    lax.fori_loop(0, count, step, 0)


def qkv_call(places, shards, weights, gain, bias, cos, sin, width):
    tokens, depth = shards[0].shape
    total_rows = tokens * len(shards)
    return pl.pallas_call(
        functools.partial(qkv_kernel, len(shards), len(weights)),
        grid_spec=pltpu.PrefetchScalarGridSpec(
            num_scalar_prefetch=1,
            grid=(1,),
            in_specs=[whole(s) for s in shards]
            + [block_spec(w, 3 * width, lambda i: 0) for w in weights]
            + [whole(v) for v in (gain, bias, cos, sin)],
            out_specs=[
                pl.BlockSpec((total_rows, depth), lambda i, p: (0, 0)),
                pl.BlockSpec((total_rows, width), lambda i, p: (0, 0)),
                pl.BlockSpec((total_rows, 2 * width), lambda i, p: (0, 0)),
            ],
            scratch_shapes=[pltpu.VMEM((total_rows, depth), BF)],
        ),
        out_shape=[
            jax.ShapeDtypeStruct((total_rows, depth), BF),
            jax.ShapeDtypeStruct((total_rows, width), BF),
            jax.ShapeDtypeStruct((total_rows, 2 * width), BF),
        ],
        cost_estimate=cost(
            flops=2 * total_rows * depth * 3 * width,
            transcendentals=0,
            bytes_accessed=2 * (2 * total_rows * depth + depth * 3 * width),
        ),
        name="qkv_rope",
    )(places, *shards, *arrays(weights), gain, bias, cos, sin)


def up_kernel(shards, blocks, experts, info_ref, *refs):
    row_refs, refs = refs[:shards], refs[shards:]
    gate_refs, up_refs, refs = refs[:blocks], refs[blocks : 2 * blocks], refs[2 * blocks :]
    small_ref, chosen_ref, act_ref, silu_ref, slope_ref, plain_ref, scale_ref, scratch = refs
    step_n = pl.program_id(0)
    own = info_ref[blocks]
    units = info_ref[blocks + 1]
    tile, count = tiles_of(scratch.shape[0])

    @pl.when(step_n == 0)
    def _():
        tokens = row_refs[0].shape[0]
        for k, ref in enumerate(row_refs):
            logits = lax.dot_general(
                ref[...], small_ref[...], (((1,), (1,)), ((), ())), preferred_element_type=F32
            )
            lane = lax.broadcasted_iota(jnp.int32, logits.shape, 1)
            kept = jnp.where(lane < experts, logits, NEGATIVE)
            raised = jnp.exp(kept - jnp.max(kept, axis=1, keepdims=True))
            prob = raised / jnp.sum(raised, axis=1, keepdims=True)
            chosen = chosen_ref[k * tokens : (k + 1) * tokens, :].astype(F32)
            routed = jnp.sum(jnp.where(lane == own, chosen, 0.0), axis=1, keepdims=True)
            gate = jnp.sum(jnp.where(lane == own, prob, 0.0), axis=1, keepdims=True) * routed
            sig = jax.nn.sigmoid(
                jnp.sum(jnp.where(lane == experts, logits, 0.0), axis=1, keepdims=True)
            )
            place = lax.broadcasted_iota(jnp.int32, (tokens, HD), 1)
            scale_ref[k * tokens : (k + 1) * tokens, :] = jnp.where(
                place == 0, gate, jnp.where(place == 1, sig, routed)
            )
        reorder(info_ref, row_refs, scratch, blocks)

    for m in range(count):
        at = slice(m * tile, (m + 1) * tile)
        rows = scratch[at, :]
        gate = jnp.dot(
            rows, jnp.concatenate([w[...] for w in gate_refs], axis=0), preferred_element_type=F32
        )
        up = jnp.dot(
            rows, jnp.concatenate([w[...] for w in up_refs], axis=0), preferred_element_type=F32
        )
        sig = jax.nn.sigmoid(gate)
        act = gate * sig
        plain = act * up
        silu_ref[at, :] = act.astype(BF)
        slope_ref[at, :] = (up * (sig + act * (1.0 - sig))).astype(BF)
        plain_ref[at, :] = plain.astype(BF)
        for h in range(TILE_N // HD):
            cols = slice(h * HD, (h + 1) * HD)
            expert = step_n * (TILE_N // HD) + h < units // HD
            scale = jnp.where(expert, scale_ref[at, 0:1], scale_ref[at, 1:2])
            act_ref[at, cols] = (plain[:, cols] * scale).astype(BF)


def up_call(info, shards, gates, ups, small, chosen, experts):
    tokens, depth = shards[0].shape
    total_rows, cols = tokens * len(shards), gates[0][0].shape[2]
    out = pl.BlockSpec((total_rows, TILE_N), lambda i, p: (0, i))
    return pl.pallas_call(
        functools.partial(up_kernel, len(shards), len(gates), experts),
        grid_spec=pltpu.PrefetchScalarGridSpec(
            num_scalar_prefetch=1,
            grid=(pl.cdiv(cols, TILE_N),),
            in_specs=[whole(s) for s in shards]
            + [block_spec(w, TILE_N, lambda i: i) for w in gates + ups]
            + [whole(small), whole(chosen)],
            out_specs=[out] * 4 + [pl.BlockSpec((total_rows, HD), lambda i, p: (0, 0))],
            scratch_shapes=[pltpu.VMEM((total_rows, depth), BF)],
        ),
        out_shape=[jax.ShapeDtypeStruct((total_rows, cols), BF)] * 4
        + [jax.ShapeDtypeStruct((total_rows, HD), F32)],
        cost_estimate=cost(
            flops=4 * total_rows * depth * cols,
            transcendentals=total_rows * cols,
            bytes_accessed=2 * (total_rows * depth + 2 * depth * cols) + 8 * total_rows * cols,
        ),
        name="expert_up",
    )(info, *shards, *arrays(gates + ups), small, chosen)


def down_back_kernel(shards, blocks, cols, info_ref, *refs):
    row_refs, refs = refs[:shards], refs[shards:]
    weight_refs, refs = refs[:blocks], refs[blocks:]
    silu_ref, slope_ref, plain_ref, scale_ref, dgate_ref, dup_ref, sums_ref, scratch, sums = refs
    step_n = pl.program_id(0)
    units = info_ref[blocks + 1]
    tile, count = tiles_of(scratch.shape[0])

    @pl.when(step_n == 0)
    def _():
        reorder(info_ref, row_refs, scratch, blocks)
        sums[...] = jnp.zeros_like(sums)

    for m in range(count):
        at = slice(m * tile, (m + 1) * tile)
        back = jnp.dot(
            scratch[at, :],
            jnp.concatenate([w[...] for w in weight_refs], axis=0),
            preferred_element_type=F32,
        )
        for h in range(TILE_N // HD):
            lane = slice(h * HD, (h + 1) * HD)
            group = step_n * (TILE_N // HD) + h
            expert = group < units // HD
            part = back[:, lane]
            touched = jnp.where(group < cols // HD, part * plain_ref[at, lane].astype(F32), 0.0)
            kind = jnp.where(expert, 0, 1)
            sums[kind, at, :] += touched
            scaled = part * jnp.where(expert, scale_ref[at, 0:1], scale_ref[at, 1:2])
            dup_ref[at, lane] = (scaled * silu_ref[at, lane].astype(F32)).astype(BF)
            dgate_ref[at, lane] = (scaled * slope_ref[at, lane].astype(F32)).astype(BF)

    @pl.when(step_n == pl.num_programs(0) - 1)
    def _():
        for m in range(count):
            at = slice(m * tile, (m + 1) * tile)
            place = lax.broadcasted_iota(jnp.int32, (tile, HD), 1)
            expert_sum = jnp.sum(sums[0, at, :], axis=1, keepdims=True) * scale_ref[at, 2:3]
            shared_sum = jnp.sum(sums[1, at, :], axis=1, keepdims=True)
            sums_ref[at, :] = jnp.where(
                place == 0, expert_sum, jnp.where(place == 1, shared_sum, 0.0)
            )


def down_back_call(info, shards, weights, silu, slope, plain, scales):
    tokens, depth = shards[0].shape
    total_rows, cols = silu.shape
    out = pl.BlockSpec((total_rows, TILE_N), lambda i, p: (0, i))
    return pl.pallas_call(
        functools.partial(down_back_kernel, len(shards), len(weights), cols),
        grid_spec=pltpu.PrefetchScalarGridSpec(
            num_scalar_prefetch=1,
            grid=(pl.cdiv(cols, TILE_N),),
            in_specs=[whole(s) for s in shards]
            + [block_spec(w, TILE_N, lambda i: i) for w in weights]
            + [out, out, out, whole(scales)],
            out_specs=[out, out, whole(scales)],
            scratch_shapes=[
                pltpu.VMEM((total_rows, depth), BF),
                pltpu.VMEM((2, total_rows, HD), F32),
            ],
        ),
        out_shape=[
            jax.ShapeDtypeStruct((total_rows, cols), BF),
            jax.ShapeDtypeStruct((total_rows, cols), BF),
            jax.ShapeDtypeStruct((total_rows, HD), F32),
        ],
        cost_estimate=cost(
            flops=2 * total_rows * depth * cols,
            transcendentals=0,
            bytes_accessed=2 * (total_rows * depth + depth * cols) + 10 * total_rows * cols,
        ),
        name="down_back",
    )(info, *shards, *arrays(weights), silu, slope, plain, scales)


def out_back_kernel(shards, blocks, places_ref, *refs):
    row_refs, refs = refs[:shards], refs[shards:]
    weight_refs, (out_ref, rows_ref, scratch) = refs[:blocks], refs[blocks:]
    tokens = row_refs[0].shape[0]
    for k, ref in enumerate(row_refs):
        rows_ref[k * tokens : (k + 1) * tokens, :] = ref[...]
    reorder(places_ref, row_refs, scratch, blocks)
    tile, count = tiles_of(scratch.shape[0])

    def step(m, _):
        at = pl.ds(pl.multiple_of(m * tile, tile), tile)
        out_ref[at, :] = jnp.dot(
            scratch[at, :],
            jnp.concatenate([w[...] for w in weight_refs], axis=0),
            preferred_element_type=F32,
        ).astype(BF)
        return 0

    lax.fori_loop(0, count, step, 0)


def out_back_call(places, shards, weights, width):
    tokens, depth = shards[0].shape
    total_rows = tokens * len(shards)
    return pl.pallas_call(
        functools.partial(out_back_kernel, len(shards), len(weights)),
        grid_spec=pltpu.PrefetchScalarGridSpec(
            num_scalar_prefetch=1,
            grid=(1,),
            in_specs=[whole(s) for s in shards]
            + [block_spec(w, width, lambda i: 3) for w in weights],
            out_specs=[
                pl.BlockSpec((total_rows, width), lambda i, p: (0, 0)),
                pl.BlockSpec((total_rows, depth), lambda i, p: (0, 0)),
            ],
            scratch_shapes=[pltpu.VMEM((total_rows, depth), BF)],
        ),
        out_shape=[
            jax.ShapeDtypeStruct((total_rows, width), BF),
            jax.ShapeDtypeStruct((total_rows, depth), BF),
        ],
        cost_estimate=cost(
            flops=2 * total_rows * depth * width,
            transcendentals=0,
            bytes_accessed=2 * (2 * total_rows * depth + depth * width),
        ),
        name="out_back",
    )(places, *shards, *arrays(weights))


def home_kernel(pairs, indices, start, places_ref, *refs):
    blocks = len(indices) // pairs
    act_refs, refs = refs[:pairs], refs[pairs:]
    weight_refs, refs = refs[: pairs * blocks], refs[pairs * blocks :]
    keep_ref, away_ref, held, sems = refs
    size, cols = held.shape[2:]

    def copy(p, j, source, index):
        return pltpu.make_async_copy(
            source.at[index, :, start : start + cols], held.at[p, j], sems.at[p, j]
        )

    for j in range(blocks):
        for p in range(pairs):
            copy(p, j, weight_refs[p * blocks + j], indices[p * blocks + j]).start()
    half = keep_ref.shape[0]
    tile, count = tiles_of(half)

    def step(j, _):
        for p in range(pairs):
            copy(p, j, weight_refs[p * blocks], 0).wait()
        to = window(places_ref, j, size)
        for h, out_ref in enumerate((keep_ref, away_ref)):
            for m in range(count):
                at = slice(h * half + m * tile, h * half + (m + 1) * tile)
                out = functools.reduce(
                    jnp.add,
                    [
                        lax.dot_general(
                            act_refs[p][at, :],
                            held[p, j],
                            (((1,), (1,)), ((), ())),
                            preferred_element_type=F32,
                        )
                        for p in range(pairs)
                    ],
                )
                out_ref[m * tile : (m + 1) * tile, to] = out.astype(BF)
        return 0

    lax.fori_loop(0, blocks, step, 0)


def project_home(places, acts, weights, depth, start=0):
    total_rows, cols = acts[0].shape
    blocks, size = len(weights[0]), weights[0][0][0].shape[1]
    every = [w for blocks_of in weights for w in blocks_of]
    half = pl.BlockSpec((total_rows // 2, depth), lambda i, p: (0, 0))
    keep, away = pl.pallas_call(
        functools.partial(home_kernel, len(acts), [i for _, i in every], start),
        grid_spec=pltpu.PrefetchScalarGridSpec(
            num_scalar_prefetch=1,
            grid=(1,),
            in_specs=[whole(a) for a in acts]
            + [pl.BlockSpec(memory_space=pl.ANY)] * (len(acts) * blocks),
            out_specs=[half, half],
            scratch_shapes=[
                pltpu.VMEM((len(acts), blocks, size, cols), BF),
                pltpu.SemaphoreType.DMA((len(acts), blocks)),
            ],
        ),
        out_shape=[jax.ShapeDtypeStruct((total_rows // 2, depth), BF)] * 2,
        cost_estimate=cost(
            flops=2 * total_rows * depth * cols * len(acts),
            transcendentals=0,
            bytes_accessed=2 * (total_rows * depth + len(acts) * cols * (depth + total_rows)),
        ),
        name="project_home",
    )(places, *acts, *arrays(every))
    return keep, away


def weight_grad_kernel(n, lists, places_ref, *refs):
    row_refs, out_refs = [], refs[-(2 + n) :]
    at = 0
    for count in lists:
        row_refs.append(refs[at : at + count])
        at += count
    part_refs = refs[at : at + len(lists)]
    j = pl.program_id(0)
    low = 0
    for rows, part in zip(row_refs, part_refs):
        left = jnp.concatenate([r[...] for r in rows], axis=0)
        out = lax.dot_general(
            left, part[...], (((0,), (0,)), ((), ())), preferred_element_type=F32
        ).astype(BF)
        cols = slice(low, low + part.shape[1])
        low += part.shape[1]
        for g, ref in enumerate(out_refs):
            first = g * n if g < 2 else 2 * n + (g - 2) * 2
            last = first + (n if g < 2 else 2)

            @pl.when((j >= first) & (j < last))
            def _(ref=ref, out=out, cols=cols):
                ref[0, :, cols] = out


def weight_grad(order, pairs):
    n = lax.axis_size("ctx")
    blocks = 4 * n
    depth = pairs[0][0][0].shape[1]
    size = depth // blocks
    cols = sum(p.shape[1] for _, p in pairs)
    total_rows = pairs[0][1].shape[0]
    in_specs, operands = [], []
    for rows, _ in pairs:
        for r in rows:
            in_specs.append(pl.BlockSpec((r.shape[0], size), lambda j, o: (0, o[j])))
            operands.append(r)
    for _, part in pairs:
        in_specs.append(whole(part))
        operands.append(part)
    out_specs, out_shape = [], []
    for g in range(2 + n):
        first = g * n if g < 2 else 2 * n + (g - 2) * 2
        count = n if g < 2 else 2
        out_specs.append(
            pl.BlockSpec(
                (1, size, cols),
                lambda j, o, first=first, count=count: (
                    jnp.clip(j - first, 0, count - 1),
                    0,
                    0,
                ),
            )
        )
        out_shape.append(jax.ShapeDtypeStruct((count, size, cols), BF))
    return pl.pallas_call(
        functools.partial(weight_grad_kernel, n, [len(rows) for rows, _ in pairs]),
        grid_spec=pltpu.PrefetchScalarGridSpec(
            num_scalar_prefetch=1, grid=(blocks,), in_specs=in_specs, out_specs=out_specs
        ),
        out_shape=out_shape,
        cost_estimate=cost(
            flops=2 * total_rows * depth * cols,
            transcendentals=0,
            bytes_accessed=2 * (total_rows * (depth + cols) + depth * cols),
        ),
        name="weight_grad",
    )(order, *operands)


def allowed_keys(tokens, count, length, x):
    row = lax.broadcasted_iota(jnp.int32, (tokens, tokens), 0) + x * tokens
    col = lax.broadcasted_iota(jnp.int32, (tokens, tokens), 1)
    parts = []
    for s in range(count):
        place = col + (x - s) * tokens
        parts.append((place >= 0) & (place <= row) & (place < length))
    return jnp.concatenate(parts, axis=1)


def probabilities(query, keys, allowed, scale):
    scores = (
        lax.dot_general(query, keys, (((1,), (1,)), ((), ())), preferred_element_type=F32) * scale
    )
    masked = jnp.where(allowed, scores, NEGATIVE)
    top = jnp.max(masked, axis=1, keepdims=True)
    weights = jnp.where(allowed, jnp.exp(masked - top), 0.0)
    return weights / jnp.sum(weights, axis=1, keepdims=True)


def attend_kernel(scale, info_ref, q_ref, *refs):
    kv_refs, out_ref = refs[:-1], refs[-1]
    group = pl.program_id(0)
    tokens, width = q_ref.shape
    allowed = allowed_keys(tokens, len(kv_refs), info_ref[group], info_ref[pl.num_programs(0)])
    for h in range(width // HD):
        at = h * HD
        keys = jnp.concatenate([r[:, at : at + HD] for r in kv_refs], axis=0)
        values = jnp.concatenate([r[:, width + at : width + at + HD] for r in kv_refs], axis=0)
        prob = probabilities(q_ref[:, at : at + HD], keys, allowed, scale)
        out_ref[:, at : at + HD] = jnp.dot(
            prob.astype(BF), values, preferred_element_type=F32
        ).astype(BF)


def attend_call(info, query, kvs, tokens, scale):
    total, width = query.shape
    groups = total // tokens
    return pl.pallas_call(
        functools.partial(attend_kernel, scale),
        grid_spec=pltpu.PrefetchScalarGridSpec(
            num_scalar_prefetch=1,
            grid=(groups,),
            in_specs=[pl.BlockSpec((tokens, width), lambda i, info: (i, 0))]
            + [pl.BlockSpec((tokens, 2 * width), lambda i, info: (i, 0)) for _ in kvs],
            out_specs=pl.BlockSpec((tokens, width), lambda i, info: (i, 0)),
        ),
        out_shape=jax.ShapeDtypeStruct((total, width), BF),
        cost_estimate=cost(
            flops=4 * total * width * tokens * len(kvs),
            transcendentals=total * tokens * len(kvs) * width // HD,
            bytes_accessed=2 * total * width * (2 + 2 * len(kvs)),
        ),
        name="attend",
    )(info, query, *kvs)


def unrope(grad, cos, sin):
    return grad * cos - turn(grad * sin)


def attend_back_kernel(scale, count, info_ref, q_ref, da_ref, *refs):
    kv_refs = refs[:count]
    cos_ref, sin_ref = refs[count : count + 2]
    dq_ref = refs[count + 2]
    dkv_refs = refs[count + 3 :]
    group = pl.program_id(0)
    tokens, width = q_ref.shape
    allowed = allowed_keys(tokens, count, info_ref[group], info_ref[pl.num_programs(0)])
    for h in range(width // HD):
        at = h * HD
        keys = jnp.concatenate([r[:, at : at + HD] for r in kv_refs], axis=0)
        values = jnp.concatenate([r[:, width + at : width + at + HD] for r in kv_refs], axis=0)
        query, grad = q_ref[:, at : at + HD], da_ref[:, at : at + HD]
        prob = probabilities(query, keys, allowed, scale)
        dprob = lax.dot_general(
            grad, values, (((1,), (1,)), ((), ())), preferred_element_type=F32
        )
        row_dot = jnp.sum(prob * dprob, axis=1, keepdims=True)
        dscore = (prob * (dprob - row_dot)).astype(BF)
        dq = jnp.dot(dscore, keys, preferred_element_type=F32) * scale
        dq_ref[:, at : at + HD] = unrope(dq, cos_ref[:tokens], sin_ref[:tokens]).astype(BF)
        dk = (
            lax.dot_general(dscore, query, (((0,), (0,)), ((), ())), preferred_element_type=F32)
            * scale
        )
        dv = lax.dot_general(
            prob.astype(BF), grad, (((0,), (0,)), ((), ())), preferred_element_type=F32
        )
        for s in range(count):
            part = slice(s * tokens, (s + 1) * tokens)
            dkv_refs[s][:, at : at + HD] = unrope(dk[part], cos_ref[part], sin_ref[part]).astype(
                dkv_refs[s].dtype
            )
            dkv_refs[s][:, width + at : width + at + HD] = dv[part].astype(dkv_refs[s].dtype)


def attend_back_call(info, query, grad, kvs, cos, sin, tokens, scale):
    total, width = query.shape
    groups, count = total // tokens, len(kvs)
    one = pl.BlockSpec((tokens, width), lambda i, info: (i, 0))
    two = pl.BlockSpec((tokens, 2 * width), lambda i, info: (i, 0))
    table = pl.BlockSpec(cos.shape, lambda i, info: (0, 0))
    return pl.pallas_call(
        functools.partial(attend_back_kernel, scale, count),
        grid_spec=pltpu.PrefetchScalarGridSpec(
            num_scalar_prefetch=1,
            grid=(groups,),
            in_specs=[one, one] + [two] * count + [table, table],
            out_specs=[one] + [two] * count,
        ),
        out_shape=[jax.ShapeDtypeStruct((total, width), BF)]
        + [jax.ShapeDtypeStruct((total, 2 * width), F32 if s == 0 else BF) for s in range(count)],
        cost_estimate=cost(
            flops=10 * total * width * tokens * count,
            transcendentals=total * tokens * count * width // HD,
            bytes_accessed=2 * total * width * (3 + 5 * count),
        ),
        name="attend_back",
    )(info, query, grad, *kvs, cos, sin)


def rope_tables(positions):
    frequency = ROPE_BASE ** (-jnp.arange(0, HD, 2, dtype=F32) / HD)
    angles = positions[:, None] * frequency[None, :]
    return (
        jnp.concatenate([jnp.cos(angles), jnp.cos(angles)], axis=1),
        jnp.concatenate([jnp.sin(angles), jnp.sin(angles)], axis=1),
    )


def dot_t(a, b):
    return lax.dot_general(a, b, (((1,), (1,)), ((), ())), preferred_element_type=F32)


def norm_scale(values):
    return lax.rsqrt(jnp.mean(values * values, axis=1, keepdims=True) + EPSILON)


def norm_back(values, scale, gain, grads):
    weighted = grads * gain
    grad_values = scale * weighted - values * scale**3 * jnp.mean(
        weighted * values, axis=1, keepdims=True
    )
    return grad_values, jnp.sum(grads * values * scale, axis=0)


def body(
    tokens,
    teacher,
    lengths,
    routes,
    attn_gain,
    ffn_gain,
    router_weight,
    shared_gate,
    qkv_weight,
    qkv_bias,
    out_weight,
    shared_up,
    shared_down,
    expert_up,
    expert_down,
):
    tok_rows, model_width = tokens.shape[1:]
    nz, n = lax.axis_size("exp"), lax.axis_size("ctx")
    z, x, dp = lax.axis_index("exp"), lax.axis_index("ctx"), lax.axis_index("dp")
    c = dp % 2
    devices = lax.axis_size(("dp", "ctx", "exp"))
    seq_len = tok_rows * n
    experts = router_weight.shape[1]
    own_expert = 2 * z + c
    rows_w = qkv_weight.shape[0]
    width = qkv_weight.shape[2] // 2
    units, shared = expert_down.shape[2], shared_down.shape[1] // 2
    score_scale = HD ** (-0.5)
    first = c == 0

    def halves(v, axis):
        size = v.shape[axis] // 2
        low = lax.slice_in_dim(v, 0, size, axis=axis)
        high = lax.slice_in_dim(v, size, 2 * size, axis=axis)
        return jnp.where(first, low, high), jnp.where(first, high, low)

    token_mine = gather_exp(tokens[0])

    lanes = pl.cdiv(experts + 1, 16) * 16
    span = model_width // devices
    piece = jnp.concatenate(
        [router_weight.T, shared_gate[None], attn_gain[None], ffn_gain[None]], axis=0
    )
    held = pl.cdiv(experts + 3, 16) * 16
    piece = jnp.pad(piece, ((0, held - experts - 3), (0, tok_rows - span)))
    chosen = (
        (routes[0][None, :, :] == jnp.arange(lanes, dtype=jnp.int32)[:, None, None])
        .any(axis=2)
        .astype(BF)
    )
    grouped = gather_group(jnp.concatenate([piece, chosen], axis=0))
    vectors = gather_plane(grouped[:, :, : experts + 3, :span])
    chosen = grouped[:, :, held:]
    chosen = jnp.where(first, chosen, chosen[::-1])
    chosen_all = jnp.swapaxes(chosen, 2, 3).reshape(2 * nz * tok_rows, lanes)

    attn_halves = [
        jnp.concatenate([q[:, 0], q[:, 1], q[:, 2], o], axis=1)
        for q, o in zip(halves(qkv_weight, 2), halves(out_weight, 1))
    ]
    blank = jnp.zeros((rows_w, -(units + shared) % HD), BF)

    def pack(experts_of, shared_of):
        mine, other = [
            jnp.concatenate([e, s, blank], axis=1) for e, s in zip(experts_of, shared_of)
        ]
        return jnp.stack([mine, core_swap(other)])

    def up_pair(anchors, part):
        up_e, up_s = after((expert_up, shared_up), anchors)
        return pack(
            [v[:, 0] for v in halves(up_e[:, :, part * units : (part + 1) * units], 1)],
            halves(up_s[:, part], 1),
        )

    def down_pair(anchors):
        down_e, down_s = after((expert_down, shared_down), anchors)
        return pack([v[:, 0] for v in halves(down_e, 1)], halves(down_s, 1))

    attn_pair = jnp.stack([attn_halves[0], core_swap(attn_halves[1])])
    attn_near = weight_first(attn_pair)
    attn_far = weight_second(*attn_near)
    gate_pair = up_pair([attn_pair], 0)
    gate_near = weight_first(after((gate_pair,), attn_near)[0])
    token_mine, attn_near, attn_far, gate_pair, vectors = meet(
        token_mine, attn_near, attn_far, gate_pair, vectors
    )
    attn_weight = weight_blocks(attn_pair, *attn_near, *attn_far)
    vectors = vectors.transpose(4, 1, 2, 0, 3, 5).reshape(experts + 3, model_width)
    small = jnp.pad(vectors[: experts + 1], ((0, lanes - experts - 1), (0, 0)))
    attn_factor = vectors[experts + 1].astype(F32)[None]
    ffn_factor = vectors[experts + 2].astype(F32)[None]

    count_valid = jnp.sum(lengths).astype(F32)
    factor = lengths.shape[0] * seq_len / count_valid
    positions = x * tok_rows + jnp.arange(tok_rows, dtype=jnp.int32)
    own_length = lengths[dp * nz + z]
    valid_rows = (positions < own_length).astype(F32)[:, None]
    shard_dp = jnp.repeat(jnp.stack([dp, dp ^ 1]), nz)
    shard_z = jnp.tile(jnp.arange(nz, dtype=jnp.int32), 2)
    info = jnp.concatenate([lengths[shard_dp * nz + shard_z], x[None].astype(jnp.int32)])
    key_places = jnp.concatenate([positions - s * tok_rows for s in range(n)])
    cos_all, sin_all = rope_tables(key_places.astype(F32))
    cos, sin = cos_all[:tok_rows], sin_all[:tok_rows]

    def place(dy, dc, s):
        return (((dp // 2) ^ dy) * 2 + (c ^ dc)) * n + lax.rem(x + n - s, n)

    blocks = 4 * n
    places = jnp.stack(
        [place(dy, dc, s) for dy in range(2) for dc in range(2) for s in range(n)]
    ).astype(jnp.int32)
    order = jnp.stack(
        [place(dy, 0, s) for dy in range(2) for s in range(n)]
        + [place(dy, 1, s) for s in range(n) for dy in range(2)]
    ).astype(jnp.int32)
    facts = jnp.concatenate(
        [places, jnp.stack([own_expert, jnp.int32(units)]).astype(jnp.int32)]
    )

    inputs = tokens[0].astype(F32)
    attn_scale = norm_scale(inputs)
    bias = jnp.where(first, qkv_bias[:, :width], qkv_bias[:, width:])
    attn_rows, query, kv = qkv_call(
        places,
        both_cores(token_mine),
        attn_weight,
        attn_factor,
        bias.astype(F32).reshape(1, 3 * width),
        cos,
        sin,
        width,
    )
    kvs = [kv] + [
        lax.ppermute(kv, "ctx", [(i, i + s) for i in range(n - s)]) for s in range(1, n)
    ]
    upper_pair = up_pair([kv], 1)
    kvs, gate_near, upper_pair = meet(kvs, gate_near, upper_pair)
    gate_far = weight_second(*gate_near)
    upper_near = weight_first(upper_pair)
    attended = attend_call(info, query, kvs, tok_rows, score_scale)
    keep, away = project_home(places, [attended], [attn_weight], model_width, 3 * width)
    keep, away, gate_far = meet(keep, away, gate_far)
    gate_weight = weight_blocks(gate_pair, *gate_near, *gate_far)
    both, parts = home_start(keep, core_swap(away))
    lower_pair = down_pair([both])
    parts, upper_near, lower_pair = meet(parts, upper_near, lower_pair)
    upper_far = weight_second(*upper_near)
    lower_near = weight_first(lower_pair)
    hidden = inputs + total(parts)

    ffn_scale = norm_scale(hidden)
    normed_ffn = (hidden * ffn_scale * ffn_factor).astype(BF)
    ffn_mine, upper_far, lower_near = meet(gather_exp(normed_ffn), upper_far, lower_near)
    up_weight = weight_blocks(upper_pair, *upper_near, *upper_far)
    lower_far = weight_second(*lower_near)
    ffn_shards = both_cores(ffn_mine)
    act_scaled, silu, slope, plain, scales = up_call(
        facts, ffn_shards, gate_weight, up_weight, small, chosen_all, experts
    )
    down_weight = weight_blocks(lower_pair, *lower_near, *lower_far)
    keep, away = project_home(places, [act_scaled], [down_weight], model_width)
    _, parts = home_start(keep, core_swap(away))
    result = hidden + total(parts)
    grad_result = factor * valid_rows * (result - teacher[0])

    back_shards = gather_rows(grad_result.astype(BF))
    down_groups = weight_grad(order, [(back_shards, act_scaled)])
    down_moves = grad_first(down_groups)
    back_shards, down_groups = meet(back_shards, down_groups)
    grad_gate_pre, grad_up_pre, sums = down_back_call(
        facts, back_shards, down_weight, silu, slope, plain, scales
    )
    keep, away = project_home(
        places, [grad_gate_pre, grad_up_pre], [gate_weight, up_weight], model_width
    )
    got, down_moves = meet(core_swap(away), down_moves)
    both, parts = home_start(keep, got)
    own_col = (jnp.arange(experts, dtype=jnp.int32) == own_expert).astype(F32)[:, None]
    scalar_rows = jnp.concatenate(
        [own_col * sums[:, 0][None], sums[:, 1][None]], axis=0
    ).reshape(experts + 1, 2, nz, tok_rows)
    scalar_both = scalar_rows[:, 0] + core_swap(scalar_rows[:, 1])
    grad_gate_pre, grad_up_pre = after((grad_gate_pre, grad_up_pre), [both])
    wide_groups = weight_grad(order, [(ffn_shards, grad_gate_pre), (ffn_shards, grad_up_pre)])
    wide_moves = grad_first(wide_groups)
    (scalar_both,) = after((jnp.swapaxes(scalar_both, 0, 1),), [wide_groups])
    scalar_own = own_of(scalar_both, "exp", nz, z)
    down_kept, down_moves = grad_second(down_groups, *down_moves)
    parts, scalar_own, wide_groups, down_moves = meet(parts, scalar_own, wide_groups, down_moves)
    grad_normed = total(parts)

    own_logits = dot_t(normed_ffn, small)
    probs = jax.nn.softmax(own_logits[:, :experts], axis=1)
    sig = jax.nn.sigmoid(own_logits[:, experts])
    grad_probs = scalar_own[:experts].T
    grad_logits = probs * (grad_probs - jnp.sum(probs * grad_probs, axis=1, keepdims=True))
    grad_sig = scalar_own[experts] * sig * (1.0 - sig)
    grad_small = jnp.concatenate([grad_logits, grad_sig[:, None]], axis=1)
    normed_wide = normed_ffn.astype(F32)
    grad_small_full = lax.dot_general(
        grad_small, normed_wide, (((0,), (0,)), ((), ())), precision=HIGHEST
    )
    grad_normed = grad_normed + jnp.dot(
        grad_small, small[: experts + 1].astype(F32), precision=HIGHEST
    )
    grad_hidden_norm, grad_ffn_full = norm_back(hidden, ffn_scale, ffn_factor, grad_normed)
    grad_hidden = grad_result + grad_hidden_norm
    grad_hidden_low = grad_hidden.astype(BF)

    down_kept, down_moves = after((down_kept, down_moves), [grad_hidden_low])
    back_mine, grad_down = meet(gather_exp(grad_hidden_low), grad_last(down_kept, down_moves))
    grad_attended, attn_back = out_back_call(places, both_cores(back_mine), attn_weight, width)
    grad_query, grad_kv, *sent = attend_back_call(
        info, query, grad_attended, kvs, cos_all, sin_all, tok_rows, score_scale
    )
    sent = [
        lax.ppermute(v, "ctx", [(i + s, i) for i in range(n - s)])
        for s, v in enumerate(sent, start=1)
    ]
    wide_kept, onward = grad_addends(wide_groups, *after(wide_moves, [grad_query]))
    sent, onward = meet(sent, onward)
    wide_moves = grad_moves(onward)
    grad_kv = total([grad_kv, *sent])
    grad_projected = jnp.concatenate([grad_query, grad_kv.astype(BF)], axis=1)
    keep, away = project_home(places, [grad_projected], [attn_weight], model_width)
    both, parts = home_start(keep, core_swap(away))
    attn_groups = weight_grad(
        order,
        [
            ([attn_rows], after((grad_projected,), [both])[0]),
            ([attn_back], attended),
        ],
    )
    attn_moves = grad_first(attn_groups)
    (grad_down,) = after((grad_down,), [wide_moves[1]])
    bias_own = jnp.sum(grad_projected.astype(F32), axis=0).reshape(3, width)
    columns = 2 * nz
    column = lax.broadcasted_iota(jnp.int32, (3, columns * width), 1)
    bias_wide = jnp.where(column // width == own_expert, jnp.tile(bias_own, (1, columns)), 0.0)
    parts, attn_groups = meet(parts, attn_groups)
    grad_normed_attn = total(parts)
    grad_inputs_norm, grad_attn_full = norm_back(inputs, attn_scale, attn_factor, grad_normed_attn)
    grad_tokens = (grad_hidden + grad_inputs_norm)[None]
    vectors = jnp.concatenate(
        [bias_wide, grad_attn_full[None], grad_small_full, grad_ffn_full[None]], axis=0
    )
    vectors = scatter_everywhere(
        vectors.reshape(-1, 2, 2, n, nz, span).transpose(3, 1, 2, 4, 0, 5)
    )
    attn_kept, attn_moves = grad_second(attn_groups, *attn_moves)
    grad_wide = grad_last(wide_kept, wide_moves)
    grad_gate = [g[:, : act_scaled.shape[1]] for g in grad_wide]
    grad_up = [g[:, act_scaled.shape[1] :] for g in grad_wide]
    grad_attn = grad_last(attn_kept, attn_moves)

    def join(pair, axis):
        mine, theirs = pair
        return jnp.concatenate(
            [jnp.where(first, mine, theirs), jnp.where(first, theirs, mine)], axis=axis
        )

    grad_qkv = join([g[:, : 3 * width].reshape(rows_w, 3, width) for g in grad_attn], 2)
    grad_out = join([g[:, 3 * width :] for g in grad_attn], 1)
    grad_expert_up = join(
        [
            jnp.concatenate([g[:, :units], u[:, :units]], axis=1)[:, None]
            for g, u in zip(grad_gate, grad_up)
        ],
        1,
    )
    grad_shared_up = join(
        [
            jnp.concatenate([g[:, None, units : units + shared], u[:, None, units : units + shared]], axis=1)
            for g, u in zip(grad_gate, grad_up)
        ],
        2,
    )
    grad_expert_down = join([g[:, None, :units] for g in grad_down], 1)
    grad_shared_down = join([g[:, units : units + shared] for g in grad_down], 1)
    attn_own, ffn_own = vectors[:4], vectors[4:]
    return (
        result.astype(BF)[None],
        grad_tokens,
        attn_own[3],
        ffn_own[experts + 1],
        ffn_own[:experts].T,
        ffn_own[experts],
        grad_qkv,
        jnp.stack([attn_own[0], attn_own[2]]),
        attn_own[1],
        grad_out,
        grad_shared_up,
        grad_shared_down,
        grad_expert_up,
        grad_expert_down,
    )


def solution(mesh):
    every = ("dp", "ctx", "exp")
    return jax.shard_map(
        body,
        mesh=mesh,
        in_specs=(
            P(("dp", "exp"), "ctx", None),
            P(("dp", "exp"), "ctx", None),
            P(),
            P(("dp", "exp"), "ctx", None),
            P(every),
            P(every),
            P(every, None),
            P(every),
            P(("dp", "ctx"), None, "exp"),
            P(None, "exp"),
            P(("dp", "ctx"), "exp"),
            P(("dp", "ctx"), None, "exp"),
            P(("dp", "ctx"), "exp"),
            P(("dp", "ctx"), "exp", None),
            P(("dp", "ctx"), "exp", None),
        ),
        out_specs=(
            P(("dp", "exp"), "ctx", None),
            P(("dp", "exp"), "ctx", None),
            P(every),
            P(every),
            P(every, None),
            P(every),
            P(("dp", "ctx"), None, "exp"),
            P(None, every),
            P(every),
            P(("dp", "ctx"), "exp"),
            P(("dp", "ctx"), None, "exp"),
            P(("dp", "ctx"), "exp"),
            P(("dp", "ctx"), "exp", None),
            P(("dp", "ctx"), "exp", None),
        ),
        check_vma=False,
    )
```

```python
import functools

import jax
import jax.numpy as jnp
from jax import lax
from jax.experimental import pallas as pl
from jax.experimental.pallas import tpu as pltpu
from jax.sharding import PartitionSpec as P

HD = 128
EPSILON = 1e-06
ROPE_BASE = 1000000.0
NEGATIVE = -1e30
HIGHEST = lax.Precision.HIGHEST
BF = jnp.bfloat16
F32 = jnp.float32
TILE_M = 512
TILE_N = 256
PACE = 8


def core_swap(v):
    n = lax.axis_size("dp")
    return lax.ppermute(v, "dp", [(i, i ^ 1) for i in range(n)])


def y_swap(v):
    n = lax.axis_size("dp")
    return lax.ppermute(v, "dp", [(i, i ^ 2) for i in range(n)])


def shift(v, axis, s):
    n = lax.axis_size(axis)
    return lax.ppermute(v, axis, [(i, (i + s) % n) for i in range(n)])


def after(values, anchors):
    return lax.optimization_barrier((tuple(values), tuple(anchors)))[0]


def meet(*trees):
    return lax.optimization_barrier(trees)


def exchange(v):
    return lax.all_to_all(v, "exp", split_axis=0, concat_axis=0, tiled=True)


def gather_exp(v):
    nz = lax.axis_size("exp")
    wide = jnp.broadcast_to(v[None], (nz, *v.shape)).reshape(nz * v.shape[0], *v.shape[1:])
    return exchange(wide)


def gather_rows(v):
    return both_cores(gather_exp(v))


def both_cores(mine):
    return [mine, core_swap(mine)]


def home_start(keep, got):
    nz = lax.axis_size("exp")
    both = (keep.astype(F32) + got.astype(F32)).astype(keep.dtype)
    return both, list(exchange(both).reshape(nz, keep.shape[0] // nz, *keep.shape[1:]))


def total(parts):
    return functools.reduce(jnp.add, [p.astype(F32) for p in parts])


def sum_shifts(v, axis):
    return functools.reduce(
        jnp.add, [v] + [shift(v, axis, s) for s in range(1, lax.axis_size(axis))]
    )


def spread(v, size, index):
    place = lax.broadcasted_iota(jnp.int32, (size, *(1,) * v.ndim), 0)
    return jnp.where(place == index, v[None], jnp.zeros((), v.dtype))


def gather_group(v):
    v = sum_shifts(spread(v, lax.axis_size("exp"), lax.axis_index("exp")), "exp")
    v = spread(v, 2, lax.axis_index("dp") % 2)
    return v + core_swap(v)


def gather_plane(v):
    v = spread(v, 2, lax.axis_index("dp") // 2)
    v = v + y_swap(v)
    return sum_shifts(spread(v, lax.axis_size("ctx"), lax.axis_index("ctx")), "ctx")


def own_of(v, axis, size, index):
    return total(
        [
            shift(lax.dynamic_index_in_dim(v, lax.rem(index + s, size), 0, False), axis, s)
            if s
            else lax.dynamic_index_in_dim(v, index, 0, False)
            for s in range(size)
        ]
    )


def own_by_halves(v, axis):
    index, count = lax.axis_index(axis), lax.axis_size(axis)
    while v.shape[0] > 1:
        half = v.shape[0] // 2
        low = lax.rem(index // half, 2) == 0
        kept, sent = jnp.where(low, v[:half], v[half:]), jnp.where(low, v[half:], v[:half])
        v = kept + lax.ppermute(sent, axis, [(i, i ^ half) for i in range(count)])
    return v[0]


def scatter_everywhere(v):
    y, c = lax.axis_index("dp") // 2, lax.axis_index("dp") % 2
    v = own_of(v, "ctx", lax.axis_size("ctx"), lax.axis_index("ctx"))
    pick = lax.dynamic_index_in_dim
    v = pick(v, y, 0, False) + y_swap(pick(v, 1 - y, 0, False))
    v = pick(v, c, 0, False) + core_swap(pick(v, 1 - c, 0, False))
    return own_of(v, "exp", lax.axis_size("exp"), lax.axis_index("exp"))


def weight_ctx(pair):
    return [shift(pair, "ctx", s) for s in range(1, lax.axis_size("ctx"))]


def weight_first(pair):
    return weight_ctx(pair), y_swap(pair)


def weight_second(px, py):
    n = lax.axis_size("ctx")
    return [y_swap(v[0])[None] for v in px], [shift(py[1], "ctx", s)[None] for s in range(1, n)]


def weight_blocks(pair, px, py, axy, bxy):
    near = [pair, *px]
    return (
        [(v, 0) for v in near]
        + [(v, 1) for v in near]
        + [(py, 0)]
        + [(v, 0) for v in axy]
        + [(py, 1)]
        + [(v, 0) for v in bxy]
    )


def block_spec(block, cols, at):
    array, index = block
    return pl.BlockSpec((None, array.shape[1], cols), lambda i, p: (index, 0, at(i)))


def arrays(blocks):
    return [array for array, _ in blocks]


def grad_first_y(groups):
    return y_swap(groups[1])


def grad_first_ctx(groups, anchors=()):
    lines = list(groups[3:])
    if anchors:
        lines = after(lines, anchors)
    return [shift(v, "ctx", -s) for s, v in enumerate(lines, start=1)]


def grad_first(groups):
    return grad_first_y(groups), grad_first_ctx(groups)


def grad_addends(groups, far, sent):
    near, _, line, *_ = groups
    lines = [line, *sent]
    kept = ([near[0], far[0]], [v[0] for v in lines])
    onward = (
        [total([near[s], far[s]]).astype(BF) for s in range(1, near.shape[0])],
        total([v[1] for v in lines]).astype(BF),
    )
    return kept, onward


def grad_moves(onward):
    return [shift(v, "ctx", -s) for s, v in enumerate(onward[0], start=1)], [y_swap(onward[1])]


def grad_second(groups, far, sent):
    kept, onward = grad_addends(groups, far, sent)
    return kept, grad_moves(onward)


def grad_last(kept, sent):
    mine, theirs = total(kept[0] + sent[0]), total(kept[1] + sent[1])
    return mine, core_swap(theirs.astype(BF)).astype(F32)


def cost(flops, transcendentals, bytes_accessed):
    return pl.CostEstimate(
        flops=flops // PACE,
        transcendentals=transcendentals // PACE,
        bytes_accessed=bytes_accessed // PACE,
    )


def whole(v):
    return pl.BlockSpec(v.shape, lambda *_: (0,) * v.ndim)


def window(places_ref, j, size):
    return pl.ds(pl.multiple_of(places_ref[j] * size, size), size)


def reorder(places_ref, row_refs, scratch, blocks):
    start = 0
    size = scratch.shape[1] // blocks
    for ref in row_refs:
        rows = ref.shape[0]
        for j in range(blocks):
            scratch[start : start + rows, j * size : (j + 1) * size] = ref[
                :, window(places_ref, j, size)
            ]
        start += rows


def turn(v):
    lane = lax.broadcasted_iota(jnp.int32, v.shape, 1)
    rolled = pltpu.roll(v, HD // 2, 1)
    return jnp.where(lane < HD // 2, -rolled, rolled)


def tiles_of(total_rows):
    tile = min(TILE_M, total_rows)
    return tile, total_rows // tile


def qkv_kernel(shards, blocks, places_ref, *refs):
    token_refs, refs = refs[:shards], refs[shards:]
    weight_refs, refs = refs[:blocks], refs[blocks:]
    gain_ref, bias_ref, cos_ref, sin_ref, rows_ref, q_ref, kv_ref, scratch = refs
    width = q_ref.shape[1]
    tokens = cos_ref.shape[0]
    piece = min(32, tokens)
    low = 0
    for ref in token_refs:

        def norm(i, _, ref=ref, low=low):
            at = pl.multiple_of(i * piece, piece)
            wide = ref[pl.ds(at, piece), :].astype(F32)
            scale = lax.rsqrt(jnp.mean(wide * wide, axis=1, keepdims=True) + EPSILON)
            rows_ref[pl.ds(low + at, piece), :] = (wide * scale * gain_ref[...]).astype(BF)
            return 0

        lax.fori_loop(0, ref.shape[0] // piece, norm, 0)
        low += ref.shape[0]
    reorder(places_ref, [rows_ref], scratch, blocks)
    tile, count = tiles_of(rows_ref.shape[0])
    cos = jnp.concatenate([cos_ref[...]] * (tile // tokens), axis=0)
    sin = jnp.concatenate([sin_ref[...]] * (tile // tokens), axis=0)

    def step(m, _):
        at = pl.ds(pl.multiple_of(m * tile, tile), tile)
        rows = scratch[at, :]
        for part in range(3):
            cols = slice(part * width, (part + 1) * width)
            weight = jnp.concatenate([w[:, cols] for w in weight_refs], axis=0)
            out = jnp.dot(rows, weight, preferred_element_type=F32) + bias_ref[:, cols]
            if part == 2:
                kv_ref[at, width:] = out.astype(BF)
                continue
            for h in range(width // HD):
                head = out[:, h * HD : (h + 1) * HD]
                head = (head * cos + turn(head) * sin).astype(BF)
                if part == 0:
                    q_ref[at, h * HD : (h + 1) * HD] = head
                else:
                    kv_ref[at, h * HD : (h + 1) * HD] = head
        return 0

    lax.fori_loop(0, count, step, 0)


def qkv_call(places, shards, weights, gain, bias, cos, sin, width):
    tokens, depth = shards[0].shape
    total_rows = tokens * len(shards)
    return pl.pallas_call(
        functools.partial(qkv_kernel, len(shards), len(weights)),
        grid_spec=pltpu.PrefetchScalarGridSpec(
            num_scalar_prefetch=1,
            grid=(1,),
            in_specs=[whole(s) for s in shards]
            + [block_spec(w, 3 * width, lambda i: 0) for w in weights]
            + [whole(v) for v in (gain, bias, cos, sin)],
            out_specs=[
                pl.BlockSpec((total_rows, depth), lambda i, p: (0, 0)),
                pl.BlockSpec((total_rows, width), lambda i, p: (0, 0)),
                pl.BlockSpec((total_rows, 2 * width), lambda i, p: (0, 0)),
            ],
            scratch_shapes=[pltpu.VMEM((total_rows, depth), BF)],
        ),
        out_shape=[
            jax.ShapeDtypeStruct((total_rows, depth), BF),
            jax.ShapeDtypeStruct((total_rows, width), BF),
            jax.ShapeDtypeStruct((total_rows, 2 * width), BF),
        ],
        cost_estimate=cost(
            flops=2 * total_rows * depth * 3 * width,
            transcendentals=0,
            bytes_accessed=2 * (2 * total_rows * depth + depth * 3 * width),
        ),
        name="qkv_rope",
    )(places, *shards, *arrays(weights), gain, bias, cos, sin)


def up_kernel(shards, blocks, experts, info_ref, *refs):
    row_refs, refs = refs[:shards], refs[shards:]
    gate_refs, up_refs, refs = refs[:blocks], refs[blocks : 2 * blocks], refs[2 * blocks :]
    small_ref, chosen_ref, act_ref, silu_ref, slope_ref, plain_ref, scale_ref, scratch = refs
    step_n = pl.program_id(0)
    own = info_ref[blocks]
    units = info_ref[blocks + 1]
    tile, count = tiles_of(scratch.shape[0])

    @pl.when(step_n == 0)
    def _():
        tokens = row_refs[0].shape[0]
        for k, ref in enumerate(row_refs):
            logits = lax.dot_general(
                ref[...], small_ref[...], (((1,), (1,)), ((), ())), preferred_element_type=F32
            )
            lane = lax.broadcasted_iota(jnp.int32, logits.shape, 1)
            kept = jnp.where(lane < experts, logits, NEGATIVE)
            raised = jnp.exp(kept - jnp.max(kept, axis=1, keepdims=True))
            prob = raised / jnp.sum(raised, axis=1, keepdims=True)
            chosen = chosen_ref[k * tokens : (k + 1) * tokens, :].astype(F32)
            routed = jnp.sum(jnp.where(lane == own, chosen, 0.0), axis=1, keepdims=True)
            gate = jnp.sum(jnp.where(lane == own, prob, 0.0), axis=1, keepdims=True) * routed
            sig = jax.nn.sigmoid(
                jnp.sum(jnp.where(lane == experts, logits, 0.0), axis=1, keepdims=True)
            )
            place = lax.broadcasted_iota(jnp.int32, (tokens, HD), 1)
            scale_ref[k * tokens : (k + 1) * tokens, :] = jnp.where(
                place == 0, gate, jnp.where(place == 1, sig, routed)
            )
        reorder(info_ref, row_refs, scratch, blocks)

    for m in range(count):
        at = slice(m * tile, (m + 1) * tile)
        rows = scratch[at, :]
        gate = jnp.dot(
            rows, jnp.concatenate([w[...] for w in gate_refs], axis=0), preferred_element_type=F32
        )
        up = jnp.dot(
            rows, jnp.concatenate([w[...] for w in up_refs], axis=0), preferred_element_type=F32
        )
        sig = jax.nn.sigmoid(gate)
        act = gate * sig
        plain = act * up
        silu_ref[at, :] = act.astype(BF)
        slope_ref[at, :] = (up * (sig + act * (1.0 - sig))).astype(BF)
        plain_ref[at, :] = plain.astype(BF)
        for h in range(TILE_N // HD):
            cols = slice(h * HD, (h + 1) * HD)
            expert = step_n * (TILE_N // HD) + h < units // HD
            scale = jnp.where(expert, scale_ref[at, 0:1], scale_ref[at, 1:2])
            act_ref[at, cols] = (plain[:, cols] * scale).astype(BF)


def up_call(info, shards, gates, ups, small, chosen, experts):
    tokens, depth = shards[0].shape
    total_rows, cols = tokens * len(shards), gates[0][0].shape[2]
    out = pl.BlockSpec((total_rows, TILE_N), lambda i, p: (0, i))
    return pl.pallas_call(
        functools.partial(up_kernel, len(shards), len(gates), experts),
        grid_spec=pltpu.PrefetchScalarGridSpec(
            num_scalar_prefetch=1,
            grid=(pl.cdiv(cols, TILE_N),),
            in_specs=[whole(s) for s in shards]
            + [block_spec(w, TILE_N, lambda i: i) for w in gates + ups]
            + [whole(small), whole(chosen)],
            out_specs=[out] * 4 + [pl.BlockSpec((total_rows, HD), lambda i, p: (0, 0))],
            scratch_shapes=[pltpu.VMEM((total_rows, depth), BF)],
        ),
        out_shape=[jax.ShapeDtypeStruct((total_rows, cols), BF)] * 4
        + [jax.ShapeDtypeStruct((total_rows, HD), F32)],
        cost_estimate=cost(
            flops=4 * total_rows * depth * cols,
            transcendentals=total_rows * cols,
            bytes_accessed=2 * (total_rows * depth + 2 * depth * cols) + 8 * total_rows * cols,
        ),
        name="expert_up",
    )(info, *shards, *arrays(gates + ups), small, chosen)


def down_back_kernel(shards, blocks, cols, info_ref, *refs):
    row_refs, refs = refs[:shards], refs[shards:]
    weight_refs, refs = refs[:blocks], refs[blocks:]
    silu_ref, slope_ref, plain_ref, scale_ref, dgate_ref, dup_ref, sums_ref, scratch, sums = refs
    step_n = pl.program_id(0)
    units = info_ref[blocks + 1]
    tile, count = tiles_of(scratch.shape[0])

    @pl.when(step_n == 0)
    def _():
        reorder(info_ref, row_refs, scratch, blocks)
        sums[...] = jnp.zeros_like(sums)

    for m in range(count):
        at = slice(m * tile, (m + 1) * tile)
        back = jnp.dot(
            scratch[at, :],
            jnp.concatenate([w[...] for w in weight_refs], axis=0),
            preferred_element_type=F32,
        )
        for h in range(TILE_N // HD):
            lane = slice(h * HD, (h + 1) * HD)
            group = step_n * (TILE_N // HD) + h
            expert = group < units // HD
            part = back[:, lane]
            touched = jnp.where(group < cols // HD, part * plain_ref[at, lane].astype(F32), 0.0)
            kind = jnp.where(expert, 0, 1)
            sums[kind, at, :] += touched
            scaled = part * jnp.where(expert, scale_ref[at, 0:1], scale_ref[at, 1:2])
            dup_ref[at, lane] = (scaled * silu_ref[at, lane].astype(F32)).astype(BF)
            dgate_ref[at, lane] = (scaled * slope_ref[at, lane].astype(F32)).astype(BF)

    @pl.when(step_n == pl.num_programs(0) - 1)
    def _():
        for m in range(count):
            at = slice(m * tile, (m + 1) * tile)
            place = lax.broadcasted_iota(jnp.int32, (tile, HD), 1)
            expert_sum = jnp.sum(sums[0, at, :], axis=1, keepdims=True) * scale_ref[at, 2:3]
            shared_sum = jnp.sum(sums[1, at, :], axis=1, keepdims=True)
            sums_ref[at, :] = jnp.where(
                place == 0, expert_sum, jnp.where(place == 1, shared_sum, 0.0)
            )


def down_back_call(info, shards, weights, silu, slope, plain, scales):
    tokens, depth = shards[0].shape
    total_rows, cols = silu.shape
    out = pl.BlockSpec((total_rows, TILE_N), lambda i, p: (0, i))
    return pl.pallas_call(
        functools.partial(down_back_kernel, len(shards), len(weights), cols),
        grid_spec=pltpu.PrefetchScalarGridSpec(
            num_scalar_prefetch=1,
            grid=(pl.cdiv(cols, TILE_N),),
            in_specs=[whole(s) for s in shards]
            + [block_spec(w, TILE_N, lambda i: i) for w in weights]
            + [out, out, out, whole(scales)],
            out_specs=[out, out, whole(scales)],
            scratch_shapes=[
                pltpu.VMEM((total_rows, depth), BF),
                pltpu.VMEM((2, total_rows, HD), F32),
            ],
        ),
        out_shape=[
            jax.ShapeDtypeStruct((total_rows, cols), BF),
            jax.ShapeDtypeStruct((total_rows, cols), BF),
            jax.ShapeDtypeStruct((total_rows, HD), F32),
        ],
        cost_estimate=cost(
            flops=2 * total_rows * depth * cols,
            transcendentals=0,
            bytes_accessed=2 * (total_rows * depth + depth * cols) + 10 * total_rows * cols,
        ),
        name="down_back",
    )(info, *shards, *arrays(weights), silu, slope, plain, scales)


def out_back_kernel(shards, blocks, places_ref, *refs):
    row_refs, refs = refs[:shards], refs[shards:]
    weight_refs, (out_ref, rows_ref, scratch) = refs[:blocks], refs[blocks:]
    tokens = row_refs[0].shape[0]
    for k, ref in enumerate(row_refs):
        rows_ref[k * tokens : (k + 1) * tokens, :] = ref[...]
    reorder(places_ref, row_refs, scratch, blocks)
    tile, count = tiles_of(scratch.shape[0])

    def step(m, _):
        at = pl.ds(pl.multiple_of(m * tile, tile), tile)
        out_ref[at, :] = jnp.dot(
            scratch[at, :],
            jnp.concatenate([w[...] for w in weight_refs], axis=0),
            preferred_element_type=F32,
        ).astype(BF)
        return 0

    lax.fori_loop(0, count, step, 0)


def out_back_call(places, shards, weights, width):
    tokens, depth = shards[0].shape
    total_rows = tokens * len(shards)
    return pl.pallas_call(
        functools.partial(out_back_kernel, len(shards), len(weights)),
        grid_spec=pltpu.PrefetchScalarGridSpec(
            num_scalar_prefetch=1,
            grid=(1,),
            in_specs=[whole(s) for s in shards]
            + [block_spec(w, width, lambda i: 3) for w in weights],
            out_specs=[
                pl.BlockSpec((total_rows, width), lambda i, p: (0, 0)),
                pl.BlockSpec((total_rows, depth), lambda i, p: (0, 0)),
            ],
            scratch_shapes=[pltpu.VMEM((total_rows, depth), BF)],
        ),
        out_shape=[
            jax.ShapeDtypeStruct((total_rows, width), BF),
            jax.ShapeDtypeStruct((total_rows, depth), BF),
        ],
        cost_estimate=cost(
            flops=2 * total_rows * depth * width,
            transcendentals=0,
            bytes_accessed=2 * (2 * total_rows * depth + depth * width),
        ),
        name="out_back",
    )(places, *shards, *arrays(weights))


def home_kernel(pairs, indices, start, places_ref, *refs):
    blocks = len(indices) // pairs
    act_refs, refs = refs[:pairs], refs[pairs:]
    weight_refs, refs = refs[: pairs * blocks], refs[pairs * blocks :]
    keep_ref, away_ref, held, sems = refs
    size, cols = held.shape[2:]

    def copy(p, j, source, index):
        return pltpu.make_async_copy(
            source.at[index, :, start : start + cols], held.at[p, j], sems.at[p, j]
        )

    for j in range(blocks):
        for p in range(pairs):
            copy(p, j, weight_refs[p * blocks + j], indices[p * blocks + j]).start()
    half = keep_ref.shape[0]
    tile, count = tiles_of(half)

    def step(j, _):
        for p in range(pairs):
            copy(p, j, weight_refs[p * blocks], 0).wait()
        to = window(places_ref, j, size)
        for h, out_ref in enumerate((keep_ref, away_ref)):
            for m in range(count):
                at = slice(h * half + m * tile, h * half + (m + 1) * tile)
                out = functools.reduce(
                    jnp.add,
                    [
                        lax.dot_general(
                            act_refs[p][at, :],
                            held[p, j],
                            (((1,), (1,)), ((), ())),
                            preferred_element_type=F32,
                        )
                        for p in range(pairs)
                    ],
                )
                out_ref[m * tile : (m + 1) * tile, to] = out.astype(BF)
        return 0

    lax.fori_loop(0, blocks, step, 0)


def project_home(places, acts, weights, depth, start=0):
    total_rows, cols = acts[0].shape
    blocks, size = len(weights[0]), weights[0][0][0].shape[1]
    every = [w for blocks_of in weights for w in blocks_of]
    half = pl.BlockSpec((total_rows // 2, depth), lambda i, p: (0, 0))
    keep, away = pl.pallas_call(
        functools.partial(home_kernel, len(acts), [i for _, i in every], start),
        grid_spec=pltpu.PrefetchScalarGridSpec(
            num_scalar_prefetch=1,
            grid=(1,),
            in_specs=[whole(a) for a in acts]
            + [pl.BlockSpec(memory_space=pl.ANY)] * (len(acts) * blocks),
            out_specs=[half, half],
            scratch_shapes=[
                pltpu.VMEM((len(acts), blocks, size, cols), BF),
                pltpu.SemaphoreType.DMA((len(acts), blocks)),
            ],
        ),
        out_shape=[jax.ShapeDtypeStruct((total_rows // 2, depth), BF)] * 2,
        cost_estimate=cost(
            flops=2 * total_rows * depth * cols * len(acts),
            transcendentals=0,
            bytes_accessed=2 * (total_rows * depth + len(acts) * cols * (depth + total_rows)),
        ),
        name="project_home",
    )(places, *acts, *arrays(every))
    return keep, away


def weight_grad_kernel(n, lists, places_ref, *refs):
    row_refs, out_refs = [], refs[-(2 + n) :]
    at = 0
    for count in lists:
        row_refs.append(refs[at : at + count])
        at += count
    part_refs = refs[at : at + len(lists)]
    j = pl.program_id(0)
    low = 0
    for rows, part in zip(row_refs, part_refs):
        left = jnp.concatenate([r[...] for r in rows], axis=0)
        out = lax.dot_general(
            left, part[...], (((0,), (0,)), ((), ())), preferred_element_type=F32
        ).astype(BF)
        cols = slice(low, low + part.shape[1])
        low += part.shape[1]
        for g, ref in enumerate(out_refs):
            first = g * n if g < 2 else 2 * n + (g - 2) * 2
            last = first + (n if g < 2 else 2)

            @pl.when((j >= first) & (j < last))
            def _(ref=ref, out=out, cols=cols):
                ref[0, :, cols] = out


def weight_grad(order, pairs):
    n = lax.axis_size("ctx")
    blocks = 4 * n
    depth = pairs[0][0][0].shape[1]
    size = depth // blocks
    cols = sum(p.shape[1] for _, p in pairs)
    total_rows = pairs[0][1].shape[0]
    in_specs, operands = [], []
    for rows, _ in pairs:
        for r in rows:
            in_specs.append(pl.BlockSpec((r.shape[0], size), lambda j, o: (0, o[j])))
            operands.append(r)
    for _, part in pairs:
        in_specs.append(whole(part))
        operands.append(part)
    out_specs, out_shape = [], []
    for g in range(2 + n):
        first = g * n if g < 2 else 2 * n + (g - 2) * 2
        count = n if g < 2 else 2
        out_specs.append(
            pl.BlockSpec(
                (1, size, cols),
                lambda j, o, first=first, count=count: (
                    jnp.clip(j - first, 0, count - 1),
                    0,
                    0,
                ),
            )
        )
        out_shape.append(jax.ShapeDtypeStruct((count, size, cols), BF))
    return pl.pallas_call(
        functools.partial(weight_grad_kernel, n, [len(rows) for rows, _ in pairs]),
        grid_spec=pltpu.PrefetchScalarGridSpec(
            num_scalar_prefetch=1, grid=(blocks,), in_specs=in_specs, out_specs=out_specs
        ),
        out_shape=out_shape,
        cost_estimate=cost(
            flops=2 * total_rows * depth * cols,
            transcendentals=0,
            bytes_accessed=2 * (total_rows * (depth + cols) + depth * cols),
        ),
        name="weight_grad",
    )(order, *operands)


def allowed_keys(tokens, count, length, x):
    row = lax.broadcasted_iota(jnp.int32, (tokens, tokens), 0) + x * tokens
    col = lax.broadcasted_iota(jnp.int32, (tokens, tokens), 1)
    parts = []
    for s in range(count):
        place = col + (x - s) * tokens
        parts.append((place >= 0) & (place <= row) & (place < length))
    return jnp.concatenate(parts, axis=1)


def probabilities(query, keys, allowed, scale):
    scores = (
        lax.dot_general(query, keys, (((1,), (1,)), ((), ())), preferred_element_type=F32) * scale
    )
    masked = jnp.where(allowed, scores, NEGATIVE)
    top = jnp.max(masked, axis=1, keepdims=True)
    weights = jnp.where(allowed, jnp.exp(masked - top), 0.0)
    return weights / jnp.sum(weights, axis=1, keepdims=True)


def attend_kernel(scale, info_ref, q_ref, *refs):
    kv_refs, out_ref = refs[:-1], refs[-1]
    group = pl.program_id(0)
    tokens, width = q_ref.shape
    allowed = allowed_keys(tokens, len(kv_refs), info_ref[group], info_ref[pl.num_programs(0)])
    for h in range(width // HD):
        at = h * HD
        keys = jnp.concatenate([r[:, at : at + HD] for r in kv_refs], axis=0)
        values = jnp.concatenate([r[:, width + at : width + at + HD] for r in kv_refs], axis=0)
        prob = probabilities(q_ref[:, at : at + HD], keys, allowed, scale)
        out_ref[:, at : at + HD] = jnp.dot(
            prob.astype(BF), values, preferred_element_type=F32
        ).astype(BF)


def attend_call(info, query, kvs, tokens, scale):
    total, width = query.shape
    groups = total // tokens
    return pl.pallas_call(
        functools.partial(attend_kernel, scale),
        grid_spec=pltpu.PrefetchScalarGridSpec(
            num_scalar_prefetch=1,
            grid=(groups,),
            in_specs=[pl.BlockSpec((tokens, width), lambda i, info: (i, 0))]
            + [pl.BlockSpec((tokens, 2 * width), lambda i, info: (i, 0)) for _ in kvs],
            out_specs=pl.BlockSpec((tokens, width), lambda i, info: (i, 0)),
        ),
        out_shape=jax.ShapeDtypeStruct((total, width), BF),
        cost_estimate=cost(
            flops=4 * total * width * tokens * len(kvs),
            transcendentals=total * tokens * len(kvs) * width // HD,
            bytes_accessed=2 * total * width * (2 + 2 * len(kvs)),
        ),
        name="attend",
    )(info, query, *kvs)


def unrope(grad, cos, sin):
    return grad * cos - turn(grad * sin)


def attend_back_kernel(scale, count, info_ref, q_ref, da_ref, *refs):
    kv_refs = refs[:count]
    cos_ref, sin_ref = refs[count : count + 2]
    dq_ref = refs[count + 2]
    dkv_refs = refs[count + 3 :]
    group = pl.program_id(0)
    tokens, width = q_ref.shape
    allowed = allowed_keys(tokens, count, info_ref[group], info_ref[pl.num_programs(0)])
    for h in range(width // HD):
        at = h * HD
        keys = jnp.concatenate([r[:, at : at + HD] for r in kv_refs], axis=0)
        values = jnp.concatenate([r[:, width + at : width + at + HD] for r in kv_refs], axis=0)
        query, grad = q_ref[:, at : at + HD], da_ref[:, at : at + HD]
        prob = probabilities(query, keys, allowed, scale)
        dprob = lax.dot_general(
            grad, values, (((1,), (1,)), ((), ())), preferred_element_type=F32
        )
        row_dot = jnp.sum(prob * dprob, axis=1, keepdims=True)
        dscore = (prob * (dprob - row_dot)).astype(BF)
        dq = jnp.dot(dscore, keys, preferred_element_type=F32) * scale
        dq_ref[:, at : at + HD] = unrope(dq, cos_ref[:tokens], sin_ref[:tokens]).astype(BF)
        dk = (
            lax.dot_general(dscore, query, (((0,), (0,)), ((), ())), preferred_element_type=F32)
            * scale
        )
        dv = lax.dot_general(
            prob.astype(BF), grad, (((0,), (0,)), ((), ())), preferred_element_type=F32
        )
        for s in range(count):
            part = slice(s * tokens, (s + 1) * tokens)
            dkv_refs[s][:, at : at + HD] = unrope(dk[part], cos_ref[part], sin_ref[part]).astype(
                dkv_refs[s].dtype
            )
            dkv_refs[s][:, width + at : width + at + HD] = dv[part].astype(dkv_refs[s].dtype)


def attend_back_call(info, query, grad, kvs, cos, sin, tokens, scale):
    total, width = query.shape
    groups, count = total // tokens, len(kvs)
    one = pl.BlockSpec((tokens, width), lambda i, info: (i, 0))
    two = pl.BlockSpec((tokens, 2 * width), lambda i, info: (i, 0))
    table = pl.BlockSpec(cos.shape, lambda i, info: (0, 0))
    return pl.pallas_call(
        functools.partial(attend_back_kernel, scale, count),
        grid_spec=pltpu.PrefetchScalarGridSpec(
            num_scalar_prefetch=1,
            grid=(groups,),
            in_specs=[one, one] + [two] * count + [table, table],
            out_specs=[one] + [two] * count,
        ),
        out_shape=[jax.ShapeDtypeStruct((total, width), BF)]
        + [jax.ShapeDtypeStruct((total, 2 * width), F32 if s == 0 else BF) for s in range(count)],
        cost_estimate=cost(
            flops=10 * total * width * tokens * count,
            transcendentals=total * tokens * count * width // HD,
            bytes_accessed=2 * total * width * (3 + 5 * count),
        ),
        name="attend_back",
    )(info, query, grad, *kvs, cos, sin)


def rope_tables(positions):
    frequency = ROPE_BASE ** (-jnp.arange(0, HD, 2, dtype=F32) / HD)
    angles = positions[:, None] * frequency[None, :]
    return (
        jnp.concatenate([jnp.cos(angles), jnp.cos(angles)], axis=1),
        jnp.concatenate([jnp.sin(angles), jnp.sin(angles)], axis=1),
    )


def dot_t(a, b):
    return lax.dot_general(a, b, (((1,), (1,)), ((), ())), preferred_element_type=F32)


def norm_scale(values):
    return lax.rsqrt(jnp.mean(values * values, axis=1, keepdims=True) + EPSILON)


def norm_back(values, scale, gain, grads):
    weighted = grads * gain
    grad_values = scale * weighted - values * scale**3 * jnp.mean(
        weighted * values, axis=1, keepdims=True
    )
    return grad_values, jnp.sum(grads * values * scale, axis=0)


def body(
    tokens,
    teacher,
    lengths,
    routes,
    attn_gain,
    ffn_gain,
    router_weight,
    shared_gate,
    qkv_weight,
    qkv_bias,
    out_weight,
    shared_up,
    shared_down,
    expert_up,
    expert_down,
):
    tok_rows, model_width = tokens.shape[1:]
    nz, n = lax.axis_size("exp"), lax.axis_size("ctx")
    z, x, dp = lax.axis_index("exp"), lax.axis_index("ctx"), lax.axis_index("dp")
    c = dp % 2
    devices = lax.axis_size(("dp", "ctx", "exp"))
    seq_len = tok_rows * n
    experts = router_weight.shape[1]
    own_expert = 2 * z + c
    rows_w = qkv_weight.shape[0]
    width = qkv_weight.shape[2] // 2
    units, shared = expert_down.shape[2], shared_down.shape[1] // 2
    score_scale = HD ** (-0.5)
    first = c == 0

    def halves(v, axis):
        size = v.shape[axis] // 2
        low = lax.slice_in_dim(v, 0, size, axis=axis)
        high = lax.slice_in_dim(v, size, 2 * size, axis=axis)
        return jnp.where(first, low, high), jnp.where(first, high, low)

    token_mine = gather_exp(tokens[0])

    lanes = pl.cdiv(experts + 1, 16) * 16
    span = model_width // devices
    piece = jnp.concatenate(
        [router_weight.T, shared_gate[None], attn_gain[None], ffn_gain[None]], axis=0
    )
    held = pl.cdiv(experts + 3, 16) * 16
    piece = jnp.pad(piece, ((0, held - experts - 3), (0, tok_rows - span)))
    chosen = (
        (routes[0][None, :, :] == jnp.arange(lanes, dtype=jnp.int32)[:, None, None])
        .any(axis=2)
        .astype(BF)
    )
    grouped = gather_group(jnp.concatenate([piece, chosen], axis=0))
    vectors = gather_plane(grouped[:, :, : experts + 3, :span])
    chosen = grouped[:, :, held:]
    chosen = jnp.where(first, chosen, chosen[::-1])
    chosen_all = jnp.swapaxes(chosen, 2, 3).reshape(2 * nz * tok_rows, lanes)

    attn_halves = [
        jnp.concatenate([q[:, 0], q[:, 1], q[:, 2], o], axis=1)
        for q, o in zip(halves(qkv_weight, 2), halves(out_weight, 1))
    ]
    blank = jnp.zeros((rows_w, -(units + shared) % HD), BF)

    def pack(experts_of, shared_of):
        mine, other = [
            jnp.concatenate([e, s, blank], axis=1) for e, s in zip(experts_of, shared_of)
        ]
        return jnp.stack([mine, core_swap(other)])

    def up_pair(anchors, part):
        up_e, up_s = after((expert_up, shared_up), anchors)
        return pack(
            [v[:, 0] for v in halves(up_e[:, :, part * units : (part + 1) * units], 1)],
            halves(up_s[:, part], 1),
        )

    def down_pair(anchors):
        down_e, down_s = after((expert_down, shared_down), anchors)
        return pack([v[:, 0] for v in halves(down_e, 1)], halves(down_s, 1))

    attn_pair = jnp.stack([attn_halves[0], core_swap(attn_halves[1])])
    attn_near = weight_first(attn_pair)
    attn_far = weight_second(*attn_near)
    gate_pair = up_pair([attn_pair], 0)
    gate_near = weight_first(after((gate_pair,), attn_near)[0])
    token_mine, attn_near, attn_far, gate_pair, vectors = meet(
        token_mine, attn_near, attn_far, gate_pair, vectors
    )
    attn_weight = weight_blocks(attn_pair, *attn_near, *attn_far)
    vectors = vectors.transpose(4, 1, 2, 0, 3, 5).reshape(experts + 3, model_width)
    small = jnp.pad(vectors[: experts + 1], ((0, lanes - experts - 1), (0, 0)))
    attn_factor = vectors[experts + 1].astype(F32)[None]
    ffn_factor = vectors[experts + 2].astype(F32)[None]

    count_valid = jnp.sum(lengths).astype(F32)
    factor = lengths.shape[0] * seq_len / count_valid
    positions = x * tok_rows + jnp.arange(tok_rows, dtype=jnp.int32)
    own_length = lengths[dp * nz + z]
    valid_rows = (positions < own_length).astype(F32)[:, None]
    shard_dp = jnp.repeat(jnp.stack([dp, dp ^ 1]), nz)
    shard_z = jnp.tile(jnp.arange(nz, dtype=jnp.int32), 2)
    info = jnp.concatenate([lengths[shard_dp * nz + shard_z], x[None].astype(jnp.int32)])
    key_places = jnp.concatenate([positions - s * tok_rows for s in range(n)])
    cos_all, sin_all = rope_tables(key_places.astype(F32))
    cos, sin = cos_all[:tok_rows], sin_all[:tok_rows]

    def place(dy, dc, s):
        return (((dp // 2) ^ dy) * 2 + (c ^ dc)) * n + lax.rem(x + n - s, n)

    blocks = 4 * n
    places = jnp.stack(
        [place(dy, dc, s) for dy in range(2) for dc in range(2) for s in range(n)]
    ).astype(jnp.int32)
    order = jnp.stack(
        [place(dy, 0, s) for dy in range(2) for s in range(n)]
        + [place(dy, 1, s) for s in range(n) for dy in range(2)]
    ).astype(jnp.int32)
    facts = jnp.concatenate(
        [places, jnp.stack([own_expert, jnp.int32(units)]).astype(jnp.int32)]
    )

    inputs = tokens[0].astype(F32)
    attn_scale = norm_scale(inputs)
    bias = jnp.where(first, qkv_bias[:, :width], qkv_bias[:, width:])
    attn_rows, query, kv = qkv_call(
        places,
        both_cores(token_mine),
        attn_weight,
        attn_factor,
        bias.astype(F32).reshape(1, 3 * width),
        cos,
        sin,
        width,
    )
    kvs = [kv] + [
        lax.ppermute(kv, "ctx", [(i, i + s) for i in range(n - s)]) for s in range(1, n)
    ]
    upper_pair = up_pair([kv], 1)
    kvs, gate_near, upper_pair = meet(kvs, gate_near, upper_pair)
    gate_far = weight_second(*gate_near)
    upper_near = weight_first(upper_pair)
    attended = attend_call(info, query, kvs, tok_rows, score_scale)
    keep, away = project_home(places, [attended], [attn_weight], model_width, 3 * width)
    keep, away, gate_far = meet(keep, away, gate_far)
    gate_weight = weight_blocks(gate_pair, *gate_near, *gate_far)
    both, parts = home_start(keep, core_swap(away))
    lower_pair = down_pair([both])
    parts, upper_near, lower_pair = meet(parts, upper_near, lower_pair)
    upper_far = weight_second(*upper_near)
    lower_near = weight_first(lower_pair)
    hidden = inputs + total(parts)

    ffn_scale = norm_scale(hidden)
    normed_ffn = (hidden * ffn_scale * ffn_factor).astype(BF)
    ffn_mine, upper_far, lower_near = meet(gather_exp(normed_ffn), upper_far, lower_near)
    up_weight = weight_blocks(upper_pair, *upper_near, *upper_far)
    lower_far = weight_second(*lower_near)
    ffn_shards = both_cores(ffn_mine)
    act_scaled, silu, slope, plain, scales = up_call(
        facts, ffn_shards, gate_weight, up_weight, small, chosen_all, experts
    )
    down_weight = weight_blocks(lower_pair, *lower_near, *lower_far)
    keep, away = project_home(places, [act_scaled], [down_weight], model_width)
    _, parts = home_start(keep, core_swap(away))
    result = hidden + total(parts)
    grad_result = factor * valid_rows * (result - teacher[0])

    back_shards = gather_rows(grad_result.astype(BF))
    down_groups = weight_grad(order, [(back_shards, act_scaled)])
    down_moves = grad_first(down_groups)
    back_shards, down_groups = meet(back_shards, down_groups)
    grad_gate_pre, grad_up_pre, sums = down_back_call(
        facts, back_shards, down_weight, silu, slope, plain, scales
    )
    keep, away = project_home(
        places, [grad_gate_pre, grad_up_pre], [gate_weight, up_weight], model_width
    )
    got, down_moves = meet(core_swap(away), down_moves)
    both, parts = home_start(keep, got)
    own_col = (jnp.arange(experts, dtype=jnp.int32) == own_expert).astype(F32)[:, None]
    scalar_rows = jnp.concatenate(
        [own_col * sums[:, 0][None], sums[:, 1][None]], axis=0
    ).reshape(experts + 1, 2, nz, tok_rows)
    scalar_both = scalar_rows[:, 0] + core_swap(scalar_rows[:, 1])
    grad_gate_pre, grad_up_pre = after((grad_gate_pre, grad_up_pre), [both])
    wide_groups = weight_grad(order, [(ffn_shards, grad_gate_pre), (ffn_shards, grad_up_pre)])
    wide_moves = grad_first(wide_groups)
    scalar_own = own_by_halves(jnp.swapaxes(scalar_both, 0, 1), "exp")
    down_kept, down_moves = grad_second(down_groups, *down_moves)
    parts, scalar_own, wide_groups, down_moves = meet(parts, scalar_own, wide_groups, down_moves)
    grad_normed = total(parts)

    own_logits = dot_t(normed_ffn, small)
    probs = jax.nn.softmax(own_logits[:, :experts], axis=1)
    sig = jax.nn.sigmoid(own_logits[:, experts])
    grad_probs = scalar_own[:experts].T
    grad_logits = probs * (grad_probs - jnp.sum(probs * grad_probs, axis=1, keepdims=True))
    grad_sig = scalar_own[experts] * sig * (1.0 - sig)
    grad_small = jnp.concatenate([grad_logits, grad_sig[:, None]], axis=1)
    normed_wide = normed_ffn.astype(F32)
    grad_small_full = lax.dot_general(
        grad_small, normed_wide, (((0,), (0,)), ((), ())), precision=HIGHEST
    )
    grad_normed = grad_normed + jnp.dot(
        grad_small, small[: experts + 1].astype(F32), precision=HIGHEST
    )
    grad_hidden_norm, grad_ffn_full = norm_back(hidden, ffn_scale, ffn_factor, grad_normed)
    grad_hidden = grad_result + grad_hidden_norm
    grad_hidden_low = grad_hidden.astype(BF)

    down_kept, down_moves = after((down_kept, down_moves), [grad_hidden_low])
    back_mine, grad_down = meet(gather_exp(grad_hidden_low), grad_last(down_kept, down_moves))
    grad_attended, attn_back = out_back_call(places, both_cores(back_mine), attn_weight, width)
    grad_query, grad_kv, *sent = attend_back_call(
        info, query, grad_attended, kvs, cos_all, sin_all, tok_rows, score_scale
    )
    sent = [
        lax.ppermute(v, "ctx", [(i + s, i) for i in range(n - s)])
        for s, v in enumerate(sent, start=1)
    ]
    wide_kept, onward = grad_addends(wide_groups, *after(wide_moves, [grad_query]))
    sent, onward = meet(sent, onward)
    wide_moves = grad_moves(onward)
    grad_kv = total([grad_kv, *sent])
    grad_projected = jnp.concatenate([grad_query, grad_kv.astype(BF)], axis=1)
    keep, away = project_home(places, [grad_projected], [attn_weight], model_width)
    both, parts = home_start(keep, core_swap(away))
    attn_groups = weight_grad(
        order,
        [
            ([attn_rows], after((grad_projected,), [both])[0]),
            ([attn_back], attended),
        ],
    )
    attn_moves = grad_first(attn_groups)
    (grad_down,) = after((grad_down,), [wide_moves[1]])
    bias_own = jnp.sum(grad_projected.astype(F32), axis=0).reshape(3, width)
    columns = 2 * nz
    column = lax.broadcasted_iota(jnp.int32, (3, columns * width), 1)
    bias_wide = jnp.where(column // width == own_expert, jnp.tile(bias_own, (1, columns)), 0.0)
    parts, attn_groups = meet(parts, attn_groups)
    grad_normed_attn = total(parts)
    grad_inputs_norm, grad_attn_full = norm_back(inputs, attn_scale, attn_factor, grad_normed_attn)
    grad_tokens = (grad_hidden + grad_inputs_norm)[None]
    vectors = jnp.concatenate(
        [bias_wide, grad_attn_full[None], grad_small_full, grad_ffn_full[None]], axis=0
    )
    vectors = scatter_everywhere(
        vectors.reshape(-1, 2, 2, n, nz, span).transpose(3, 1, 2, 4, 0, 5)
    )
    attn_kept, attn_moves = grad_second(attn_groups, *attn_moves)
    grad_wide = grad_last(wide_kept, wide_moves)
    grad_gate = [g[:, : act_scaled.shape[1]] for g in grad_wide]
    grad_up = [g[:, act_scaled.shape[1] :] for g in grad_wide]
    grad_attn = grad_last(attn_kept, attn_moves)

    def join(pair, axis):
        mine, theirs = pair
        return jnp.concatenate(
            [jnp.where(first, mine, theirs), jnp.where(first, theirs, mine)], axis=axis
        )

    grad_qkv = join([g[:, : 3 * width].reshape(rows_w, 3, width) for g in grad_attn], 2)
    grad_out = join([g[:, 3 * width :] for g in grad_attn], 1)
    grad_expert_up = join(
        [
            jnp.concatenate([g[:, :units], u[:, :units]], axis=1)[:, None]
            for g, u in zip(grad_gate, grad_up)
        ],
        1,
    )
    grad_shared_up = join(
        [
            jnp.concatenate([g[:, None, units : units + shared], u[:, None, units : units + shared]], axis=1)
            for g, u in zip(grad_gate, grad_up)
        ],
        2,
    )
    grad_expert_down = join([g[:, None, :units] for g in grad_down], 1)
    grad_shared_down = join([g[:, units : units + shared] for g in grad_down], 1)
    attn_own, ffn_own = vectors[:4], vectors[4:]
    return (
        result.astype(BF)[None],
        grad_tokens,
        attn_own[3],
        ffn_own[experts + 1],
        ffn_own[:experts].T,
        ffn_own[experts],
        grad_qkv,
        jnp.stack([attn_own[0], attn_own[2]]),
        attn_own[1],
        grad_out,
        grad_shared_up,
        grad_shared_down,
        grad_expert_up,
        grad_expert_down,
    )


def solution(mesh):
    every = ("dp", "ctx", "exp")
    return jax.shard_map(
        body,
        mesh=mesh,
        in_specs=(
            P(("dp", "exp"), "ctx", None),
            P(("dp", "exp"), "ctx", None),
            P(),
            P(("dp", "exp"), "ctx", None),
            P(every),
            P(every),
            P(every, None),
            P(every),
            P(("dp", "ctx"), None, "exp"),
            P(None, "exp"),
            P(("dp", "ctx"), "exp"),
            P(("dp", "ctx"), None, "exp"),
            P(("dp", "ctx"), "exp"),
            P(("dp", "ctx"), "exp", None),
            P(("dp", "ctx"), "exp", None),
        ),
        out_specs=(
            P(("dp", "exp"), "ctx", None),
            P(("dp", "exp"), "ctx", None),
            P(every),
            P(every),
            P(every, None),
            P(every),
            P(("dp", "ctx"), None, "exp"),
            P(None, every),
            P(every),
            P(("dp", "ctx"), "exp"),
            P(("dp", "ctx"), None, "exp"),
            P(("dp", "ctx"), "exp"),
            P(("dp", "ctx"), "exp", None),
            P(("dp", "ctx"), "exp", None),
        ),
        check_vma=False,
    )
```
